32 devices in a mesh: freq: 16 (over z, y, x), plane: 2 (over core).
Axes of the slice: x: 2, y: 2, z: 4, core: 2. Of those that a mesh axis runs over, the one named last changes fastest.
Arguments:
- state_in: float32 [2, 32, 5, 256, 128], P(None, 'freq', None, 'plane'), may hold values from -6 to 6
- forcing_in: float32 [2, 32, 5, 256, 128], P(None, 'freq', None, 'plane'), may hold values from -6 to 6
- base_flow: float32 [16, 5, 256, 128], P('freq', None, 'plane'), may hold values from -1 to 1
- station_index: int32 [2], replicated, may hold values from 0 to 15
- lobe_count: int32 [1], replicated, may hold values from 3 to 127
Outputs:
- state_out: float32 [2, 32, 5, 256, 128], P(None, 'freq', None, 'plane')
- forcing_out: float32 [2, 32, 5, 256, 128], P(None, 'freq', None, 'plane')
The draws below stay inside these ranges and needn't reach their ends.
All inputs are finite; a program needn't handle non-finite values.
Results may differ from the reference program's by a relative error of at most 0.0003.
Values sent between devices are 32-bit elements; how exact they have to be, the bound alone decides.
A program may use at most 128 MiB of HBM per device.

```python
import math
import jax
import jax.numpy as jnp
from jax import lax

VARS = 5
R = 128
A = 256
SWEEPS = 4
STEPS = 2
F = 32
NT = 48
STATIONS = 16


def block_levels(stream_key, dims, split, smallest, largest):
    gain, own = 1.0, jax.random.fold_in(stream_key, 6)
    for dim, parts in split:
        heights = jnp.exp(jax.random.uniform(jax.random.fold_in(own, dim), (parts,), jnp.float32, smallest / len(split), largest / len(split)))
        gain = gain * jnp.repeat(heights, dims[dim] // parts).reshape([-1 if axis == dim else 1 for axis in range(len(dims))])
    return gain


def noise(own_key, dims, scale, bound, shards=(), held_as=jnp.bfloat16):
    array = jax.random.normal(own_key, dims, jnp.float32) * scale
    if len(shards) > 0:
        array = block_levels(own_key, dims, shards, -0.22, 0.18) * array
    return jnp.clip(array, min=-bound, max=bound).astype(held_as)


def setup_inputs(seed: int = 0) -> dict:
    streams_of = jax.random.split(jax.random.key(seed), 6)
    state_in = noise(streams_of[0], (2, F, VARS, A, R), 1.0, 6.0, ((1, 16), (3, 2)), jnp.float32)
    forcing_in = noise(streams_of[1], (2, F, VARS, A, R), 1.0, 6.0, ((1, 16), (3, 2)), jnp.float32)
    base_flow = jnp.clip(jax.random.uniform(streams_of[2], (STATIONS, VARS, A, R), jnp.float32, -1.0, 1.0) * block_levels(streams_of[2], (STATIONS, VARS, A, R), ((0, 16), (2, 2)), -0.4, 0.0), -1.0, 1.0)
    station_index = jax.random.randint(streams_of[3], (STEPS,), 0, STATIONS).astype(jnp.int32)
    lobe_count = jax.random.randint(streams_of[4], (1,), 3, 128).astype(jnp.int32)
    return {"state_in": state_in, "forcing_in": forcing_in, "base_flow": base_flow, "station_index": station_index, "lobe_count": lobe_count}


SIDE_WEIGHT = 1.25
MARCH_WEIGHT = 4.0
DIAG_SHIFT = 4.0
ADVECT_SCALE = 0.5
BASE_SCALE = 0.5
HIGHEST_MODE = lax.Precision.HIGHEST

def radial_tables(radius_count):
    indices = jnp.arange(radius_count)
    angles = math.pi * indices.astype(jnp.float32) / (radius_count - 1)
    cheb_nodes = jnp.cos(angles)
    weights = jnp.where((indices == 0) | (indices == radius_count - 1), 2.0, 1.0).astype(jnp.float32)
    parity = (1 - 2 * ((indices[:, None] + indices[None, :]) % 2)).astype(jnp.float32)
    offdiag = indices[:, None] != indices[None, :]
    spacing = jnp.where(offdiag, cheb_nodes[:, None] - cheb_nodes[None, :], 1.0)
    entries = jnp.where(offdiag, weights[:, None] / weights[None, :] * parity / spacing, 0.0)
    entries = entries - jnp.diag(lax.optimization_barrier(jnp.sum(entries, axis=1)))
    slopes = jnp.sin(angles)[:, None] * entries / (radius_count - 1)
    stiffness = jnp.dot(slopes.T, slopes, precision=HIGHEST_MODE)
    system = stiffness + DIAG_SHIFT * jnp.eye(radius_count, dtype=jnp.float32)
    factor = jnp.linalg.cholesky(system)
    factor_inv = lax.linalg.triangular_solve(factor, jnp.eye(radius_count, dtype=jnp.float32), left_side=True, lower=True)
    return (slopes, jnp.dot(factor_inv.T, factor_inv, precision=HIGHEST_MODE))

def transform_tables(freqs, ntime):
    mode_ids = jnp.arange(freqs)
    time_ids = jnp.arange(ntime)
    phases = mode_ids[:, None] * time_ids[None, :] % ntime
    angles = 2.0 * math.pi * phases.astype(jnp.float32) / ntime
    cosines = jnp.cos(angles)
    sine_tab = jnp.sin(angles)
    stacked = jnp.concatenate([cosines, -sine_tab], axis=0)
    return (stacked.T / math.sqrt(freqs), stacked / math.sqrt(ntime))

def chevron(lobe_count, azimuths, start_az, total_az):
    position = (start_az + jnp.arange(azimuths)).astype(jnp.int32)
    phases = lobe_count[0] * position % total_az
    return 1.0 + 0.5 * jnp.cos(2.0 * math.pi * phases.astype(jnp.float32) / total_az)

def relax_sweep(inner, neighbours, right_side, coefficient, omegas, inverse_p):
    real_part = inner[0]
    imag_part = inner[1]
    rate_col = omegas[:, None, None, None]
    scaled = coefficient[None]
    mixing = jnp.stack([scaled * real_part - rate_col * imag_part, scaled * imag_part + rate_col * real_part])
    summed = right_side - mixing + SIDE_WEIGHT * neighbours
    radius_count = summed.shape[-1]
    return jnp.dot(summed.reshape(-1, radius_count), inverse_p.T, precision=HIGHEST_MODE).reshape(summed.shape)

def advect(velocity, radial_time, around_time):
    carried = velocity[:, 1:2] * radial_time + velocity[:, 2:3] * around_time
    spread = velocity[:, 0] * (radial_time[:, 1] + around_time[:, 2])
    carried = jnp.concatenate([carried[:, 0:1] + spread[:, None], carried[:, 1:]], axis=1)
    return -ADVECT_SCALE * carried

def forcing_of(march_state, slopes, inverse, forward):
    radial = jnp.dot(march_state.reshape(-1, R), slopes.T, precision=HIGHEST_MODE).reshape(march_state.shape)
    beside_all = 0.5 * (jnp.roll(march_state, -1, 3) - jnp.roll(march_state, 1, 3))
    fields = jnp.stack([march_state, radial, beside_all])
    az_block = 32 if A % 32 == 0 else A
    pieces = []
    for first_az in range(0, A, az_block):
        block_data = fields[:, :, :, :, first_az:first_az + az_block, :].reshape(3, 2 * F, -1)
        in_time = jnp.einsum('tc,kcx->ktx', inverse, block_data, precision=HIGHEST_MODE).reshape(3, NT, VARS, -1)
        source = advect(in_time[0], in_time[1], in_time[2])
        spectral = jnp.dot(forward, source.reshape(NT, -1), precision=HIGHEST_MODE)
        pieces.append(spectral.reshape(2, F, VARS, az_block, R))
    return jnp.concatenate(pieces, axis=3)

def reference(state_in, forcing_in, base_flow, station_index, lobe_count):
    slopes, inverse_p = radial_tables(R)
    inverse, forward = transform_tables(F, NT)
    omegas = 0.5 * jnp.arange(F).astype(jnp.float32) / F
    shape_az = chevron(lobe_count, A, 0, A)
    march_state = state_in
    forcing = forcing_in
    for station in range(STEPS):
        plane_flow = lax.dynamic_index_in_dim(base_flow, station_index[station], 0, keepdims=False)
        coefficient = BASE_SCALE * plane_flow * shape_az[None, :, None]
        right_side = MARCH_WEIGHT * march_state + forcing
        iterate = march_state
        for sweep_no in range(SWEEPS):
            iterate = relax_sweep(iterate, jnp.roll(iterate, -1, 3) + jnp.roll(iterate, 1, 3), right_side, coefficient, omegas, inverse_p)
        march_state = iterate
        forcing = forcing_of(march_state, slopes, inverse, forward)
    return (march_state, forcing)
```

```python
import functools
import math

import jax
import jax.numpy as jnp
import numpy as np
from jax import lax
from jax.experimental import pallas as pl
from jax.experimental.pallas import tpu as pltpu
from jax.sharding import PartitionSpec as P

SWEEPS = 4
STEPS = 2


SIDE_WEIGHT = 1.25
MARCH_WEIGHT = 4.0
DIAG_SHIFT = 4.0
ADVECT_SCALE = 0.5
BASE_SCALE = 0.5


def radial_tables(radius_count):
    indices = np.arange(radius_count)
    angles = math.pi * indices / (radius_count - 1)
    nodes = np.cos(angles)
    weights = np.where((indices == 0) | (indices == radius_count - 1), 2.0, 1.0)
    parity = 1.0 - 2.0 * ((indices[:, None] + indices[None, :]) % 2)
    offdiag = indices[:, None] != indices[None, :]
    spacing = np.where(offdiag, nodes[:, None] - nodes[None, :], 1.0)
    entries = np.where(offdiag, weights[:, None] / weights[None, :] * parity / spacing, 0.0)
    entries = entries - np.diag(entries.sum(axis=1))
    slopes = np.sin(angles)[:, None] * entries / (radius_count - 1)
    system = slopes.T @ slopes + DIAG_SHIFT * np.eye(radius_count)
    return slopes.astype(np.float32), np.linalg.inv(system).astype(np.float32)


def transform_tables(mode_ids, freqs, ntime):
    time_ids = np.arange(ntime)
    angles = 2.0 * math.pi * (mode_ids[:, None] * time_ids[None, :] % ntime) / ntime
    stacked = np.stack([np.cos(angles), -np.sin(angles)])
    return (
        (stacked / math.sqrt(freqs)).astype(np.float32),
        (stacked / math.sqrt(ntime)).astype(np.float32),
    )


def chevron(lobe_count, azimuths, start_az, total_az):
    position = start_az + jnp.arange(azimuths)
    phases = lobe_count[0] * position % total_az
    return 1.0 + 0.5 * jnp.cos(2.0 * math.pi * phases.astype(jnp.float32) / total_az)


def halves(x):
    high = x.astype(jnp.bfloat16)
    return high, (x - high.astype(jnp.float32)).astype(jnp.bfloat16)


def right_table(table):
    high, low = np_halves(table)
    return jnp.asarray(np.tile(np.concatenate([high, low], axis=1), (2, 1)))


def left_table(table):
    high, low = np_halves(table)
    return jnp.asarray(np.concatenate([high, high, low, low], axis=1))


def np_halves(table):
    high = table.astype(jnp.bfloat16)
    return high, (table - high.astype(np.float32)).astype(jnp.bfloat16)


def times_right(x, table):
    width = table.shape[1] // 2
    y = jnp.dot(jnp.concatenate(halves(x), axis=1), table, preferred_element_type=jnp.float32)
    return y[:, :width] + y[:, width:]


def times_left(table, x):
    high, low = halves(x)
    return jnp.dot(
        table,
        jnp.concatenate([high, low, high, low], axis=0),
        preferred_element_type=jnp.float32,
    )


def ring_of(f, p, nf, planes):
    at = f
    if nf % 4 == 0:
        high = nf // 4
        z, y, x = f // 4, (f // 2) % 2, f % 2
        column = 2 * y + (x + y) % 2
        at = column * high + z + (column % 2) * (high - 1 - 2 * z)
    return at * planes + p


def device_of(g, nf, planes):
    at = g // planes
    f = at
    if nf % 4 == 0:
        high = nf // 4
        column, z = at // high, at % high
        z = z + (column % 2) * (high - 1 - 2 * z)
        y = column // 2
        f = 4 * z + 2 * y + (column + y) % 2
    return f, g % planes


def march(
    dims,
    station_ref,
    shape_ref,
    rate_ref,
    state_ref,
    s_base,
    forcing_ref,
    far_omega,
    far_qt,
    far_st,
    far_inv,
    far_fwd,
    g_state,
    g_forcing,
    r_state,
    r_base,
    s_state,
    s_w,
    r_w,
    plane_w,
    x_one,
    b_one,
    edge_out,
    edge_in,
    x_ref,
    b_ref,
    f_ref,
    w_ref,
    o_state,
    o_forcing,
    send_sem,
    recv_sem,
    own_sem,
    halo_send,
    halo_recv,
    edge_send,
    edge_recv,
    load_sem,
    omega_ref,
    qt_ref,
    st_ref,
    inv_ref,
    fwd_ref,
    table_sem,
):
    nf, planes, own_az, variables, per_dev, radii, stored, rows, base_rows, w_rows = dims
    freqs = nf * per_dev
    span = nf * own_az
    runs = 2 * per_dev * variables
    ntime = inv_ref.shape[0]
    half = variables * freqs
    me = lax.axis_index("freq")
    plane = lax.axis_index("plane")
    ring = nf * planes
    here = ring_of(me, plane, nf, planes)
    part, block = here // nf, here % nf

    def named(device):
        return {"freq": device[0], "plane": device[1]}

    right_id = named(device_of((here + 1) % ring, nf, planes))
    left_id = named(device_of((here + ring - 1) % ring, nf, planes))
    barrier = pltpu.get_barrier_semaphore()

    @pl.loop(1, ring)
    def _(d):
        other = (me * planes + plane + d) % ring
        pl.semaphore_signal(
            barrier,
            inc=1,
            device_id={"freq": other // planes, "plane": other % planes},
            device_id_type=MESH,
        )

    beyond = {"freq": me, "plane": (plane + 1) % planes}
    behind = {"freq": me, "plane": (plane + planes - 1) % planes}
    load_state = pltpu.make_async_copy(state_ref, x_one.at[0, :, pl.ds(8, span), :], load_sem.at[0])
    load_forcing = pltpu.make_async_copy(forcing_ref, b_one, load_sem.at[1])
    load_state.start()
    load_forcing.start()
    tables = [
        pltpu.make_async_copy(far, near, table_sem.at[i])
        for i, (far, near) in enumerate(
            (
                (far_omega, omega_ref),
                (far_qt, qt_ref),
                (far_st, st_ref),
                (far_inv, inv_ref),
                (far_fwd, fwd_ref),
            )
        )
    ]
    for table in tables:
        table.start()
    pl.semaphore_wait(barrier, ring - 1)

    def owner(i):
        return device_of(plane * nf + i, nf, planes)

    def holder(i):
        return i, part

    def is_me(device):
        return (device[0] == me) & (device[1] == plane)

    def exchange(k, source, landing, target, origin, pick, mine, size, first):
        def rows_of(ref, i):
            return ref.at[pl.ds(pl.multiple_of(i * size, 8), size), :]

        def copy(i):
            return pltpu.make_async_remote_copy(
                src_ref=rows_of(source, pick(i)),
                dst_ref=rows_of(landing, mine),
                send_sem=send_sem.at[k, i],
                recv_sem=recv_sem.at[k, mine],
                device_id=named(target(i)),
                device_id_type=MESH,
            )

        def arrival(i):
            return pltpu.make_async_remote_copy(
                src_ref=rows_of(landing, i),
                dst_ref=rows_of(landing, i),
                send_sem=send_sem.at[k, i],
                recv_sem=recv_sem.at[k, i],
                device_id=named(origin(i)),
                device_id_type=MESH,
            )

        def own(i):
            return pltpu.make_async_copy(
                rows_of(source, pick(i)), rows_of(landing, mine), own_sem.at[k]
            )

        @pl.loop(0, nf)
        def _(d):
            i = (d + me) % nf
            stays = is_me(target(i))

            @pl.when(stays)
            def _():
                if first:
                    own(i).start()
                else:
                    own(i).wait()

            @pl.when(jnp.logical_not(stays))
            def _():
                if first:
                    copy(i).start()
                else:
                    copy(i).wait_send()

            if not first:

                @pl.when(jnp.logical_not(is_me(origin(i))))
                def _():
                    arrival(i).wait_recv()

    def same(i):
        return i

    base_args = (1, s_base, r_base, owner, holder, same, me, base_rows)
    state_args = (0, s_state, r_state, owner, holder, same, me, rows)
    w_args = (2, s_w, r_w, holder, owner, lambda i: 0, block, w_rows)
    out_state_args = (3, o_state, g_state, holder, owner, same, block, rows)
    out_forcing_args = (4, o_forcing, g_forcing, holder, owner, same, block, rows)
    exchange(*base_args, True)

    def halo_copies(e):
        slot = e % 2
        return (
            pltpu.make_async_remote_copy(
                src_ref=x_ref.at[slot, own_az],
                dst_ref=x_ref.at[slot, 0],
                send_sem=halo_send.at[0, e],
                recv_sem=halo_recv.at[0, e],
                device_id=right_id,
                device_id_type=MESH,
            ),
            pltpu.make_async_remote_copy(
                src_ref=x_ref.at[slot, 1],
                dst_ref=x_ref.at[slot, own_az + 1],
                send_sem=halo_send.at[1, e],
                recv_sem=halo_recv.at[1, e],
                device_id=left_id,
                device_id_type=MESH,
            ),
        )

    def place(a, c, v, kk):
        return ((c * variables + v) * per_dev + kk) * nf

    def packed_row(a, c, v, kk):
        return ((c * per_dev + kk) * variables + v) * own_az + a

    def each_run(visit):
        @pl.loop(0, own_az)
        def _(a):
            for c in range(2):
                for v in range(variables):
                    for kk in range(per_dev):
                        visit(a, place(a, c, v, kk), packed_row(a, c, v, kk))

    def in_row(a, c, v, kk):
        return ((c * per_dev + kk) * variables + v) * own_az + a

    def edge_copies(e):
        return [
            pltpu.make_async_remote_copy(
                src_ref=edge_out.at[e, side],
                dst_ref=edge_in.at[e, side],
                send_sem=edge_send.at[side, e],
                recv_sem=edge_recv.at[side, e],
                device_id=target,
                device_id_type=MESH,
            )
            for side, target in ((0, beyond), (1, behind))
        ]

    def send_edges(slot, e):
        for m in range(runs):
            edge_out[e, 0, pl.ds(m, 1), :] = x_one[slot, m, pl.ds(7 + span, 1), :]
            edge_out[e, 1, pl.ds(m, 1), :] = x_one[slot, m, pl.ds(8, 1), :]
        for copy in edge_copies(e):
            copy.start()

    for table in tables:
        table.wait()
    load_state.wait()
    send_edges(0, 0)
    load_forcing.wait()

    @pl.loop(0, runs)
    def _(m):
        b_one[m] = MARCH_WEIGHT * x_one[0, m, pl.ds(8, span), :] + b_one[m]

    exchange(*base_args, False)
    for station in range(STEPS):
        wanted = station_ref[station]

        @pl.loop(0, own_az)
        def _(a):
            for v in range(variables):
                scaled = (BASE_SCALE * shape_ref[a]) * r_base[
                    pl.ds(
                        (wanted // stored) * base_rows
                        + ((wanted % stored) * variables + v) * own_az
                        + a,
                        1,
                    ),
                    :,
                ]
                if station == 0:
                    s_w[pl.ds(v * own_az + a, 1), :] = scaled
                else:
                    w_ref[(station - 1) * own_az + a, pl.ds(v, 1), :] = scaled

        if station == 0:
            exchange(*w_args, True)
    exchange(*w_args, False)

    @pl.loop(0, nf)
    def _(j):
        for v in range(variables):
            plane_w[v, pl.ds(j * own_az, own_az), :] = r_w[pl.ds(j * w_rows + v * own_az, own_az), :]

    @pl.loop(0, SWEEPS)
    def _(e):
        src, dst = e % 2, (e + 1) % 2
        for copy in edge_copies(e):
            copy.wait()
        for m in range(runs):
            x_one[src, m, pl.ds(7, 1), :] = edge_in[e, 0, pl.ds(m, 1), :]
            x_one[src, m, pl.ds(8 + span, 1), :] = edge_in[e, 1, pl.ds(m, 1), :]
        for kk in range(per_dev):
            rate = rate_ref[kk]

            @pl.loop(0, variables)
            def _(v):
                w = plane_w[v]
                at = [(c * per_dev + kk) * variables + v for c in range(2)]
                real, imag = [x_one[src, m, pl.ds(8, span), :] for m in at]
                mixing = (w * real - rate * imag, w * imag + rate * real)
                summed = [
                    SIDE_WEIGHT
                    * (x_one[src, m, pl.ds(7, span), :] + x_one[src, m, pl.ds(9, span), :])
                    + b_one[m]
                    - mixed
                    for m, mixed in zip(at, mixing)
                ]
                q = times_right(jnp.concatenate(summed, axis=0), qt_ref[...])
                x_one[dst, at[0], pl.ds(8, span), :] = q[:span]
                x_one[dst, at[1], pl.ds(8, span), :] = q[span:]

        @pl.when(e < SWEEPS - 1)
        def _():
            send_edges(dst, e + 1)

    settled = SWEEPS % 2

    @pl.loop(0, nf)
    def _(j):
        for m in range(runs):
            s_state[pl.ds(j * rows + m * own_az, own_az), :] = x_one[
                settled, m, pl.ds(8 + j * own_az, own_az), :
            ]

    exchange(*state_args, True)
    exchange(*state_args, False)

    def unpack_state(a, start, row):
        x_ref[0, a + 1, pl.ds(start, nf), :] = r_state[pl.ds(row, nf, stride=rows), :]

    each_run(unpack_state)
    for copy in halo_copies(0):
        copy.start()
    omega = omega_ref[...][None]
    flat = (2 * half, radii)
    cube = (variables, freqs, radii)

    def sweep_slab(src, dst, a, station):
        x = x_ref[src, a + 1]
        beside = SIDE_WEIGHT * (x_ref[src, a] + x_ref[src, a + 2]) + b_ref[a]
        real, imag = x[:half].reshape(cube), x[half:].reshape(cube)
        w = w_ref[(station - 1) * own_az + a][:variables][:, None, :]
        mixing = jnp.concatenate([w * real - omega * imag, w * imag + omega * real], axis=0)
        summed = beside - mixing.reshape(flat)
        x_ref[dst, a + 1] = times_right(summed, qt_ref[...])

    def advect_slab(slot, a, final):
        x = x_ref[slot, a + 1]
        beside = 0.5 * (x_ref[slot, a + 2] - x_ref[slot, a])

        def lanes(y):
            return [
                jnp.concatenate(
                    [
                        y[v * freqs : (v + 1) * freqs],
                        y[half + v * freqs : half + (v + 1) * freqs],
                    ],
                    axis=0,
                )
                for v in range(variables)
            ]

        both = jnp.concatenate(lanes(x) + lanes(beside), axis=1)
        in_time = times_left(inv_ref[...], both)
        u = [in_time[:, v * radii : (v + 1) * radii] for v in range(variables)]
        ua = [
            in_time[:, (variables + v) * radii : (variables + v + 1) * radii]
            for v in range(variables)
        ]
        radial = times_right(jnp.concatenate(u, axis=0), st_ref[...])
        ur = [radial[v * ntime : (v + 1) * ntime] for v in range(variables)]
        n = [u[1] * ur[v] + u[2] * ua[v] for v in range(variables)]
        n[0] = n[0] + u[0] * (ur[1] + ua[2])
        source = -ADVECT_SCALE * jnp.concatenate(n, axis=1)
        spectral = times_left(fwd_ref[...], source)
        forcing = jnp.concatenate(
            [
                spectral[c * freqs : (c + 1) * freqs, v * radii : (v + 1) * radii]
                for c in range(2)
                for v in range(variables)
            ],
            axis=0,
        )
        if final:
            f_ref[a] = forcing
        else:
            b_ref[a] = MARCH_WEIGHT * x + forcing

    def advect_all(slot, e, final):
        @pl.loop(1, own_az - 1)
        def _(a):
            advect_slab(slot, a, final)

        for copy in halo_copies(e):
            copy.wait()
        advect_slab(slot, 0, final)
        if own_az > 1:
            advect_slab(slot, own_az - 1, final)

    advect_all(0, 0, False)
    for station in range(1, STEPS):

        @pl.loop(0, SWEEPS)
        def _(sweep):
            e = (station - 1) * SWEEPS + sweep
            src, dst = e % 2, (e + 1) % 2

            @pl.when(sweep > 0)
            def _():
                for copy in halo_copies(e):
                    copy.wait()

            sweep_slab(src, dst, 0, station)
            if own_az > 1:
                sweep_slab(src, dst, own_az - 1, station)
            for copy in halo_copies(e + 1):
                copy.start()

            @pl.loop(1, own_az - 1)
            def _(a):
                sweep_slab(src, dst, a, station)

        last = station * SWEEPS
        slot = last % 2
        final = station == STEPS - 1
        if final:

            def pack_state(a, start, row):
                o_state[pl.ds(row, nf, stride=rows), :] = x_ref[slot, a + 1, pl.ds(start, nf), :]

            each_run(pack_state)
            exchange(*out_state_args, True)

        advect_all(slot, last, final)

    def pack_forcing(a, start, row):
        o_forcing[pl.ds(row, nf, stride=rows), :] = f_ref[a, pl.ds(start, nf), :]

    each_run(pack_forcing)
    exchange(*out_forcing_args, True)
    exchange(*out_state_args, False)
    exchange(*out_forcing_args, False)


def per_device(state_in, forcing_in, base_flow, station_index, lobe_count):
    _, per_dev, variables, span_az, radii = state_in.shape
    nf = lax.axis_size("freq")
    planes = lax.axis_size("plane")
    freqs = per_dev * nf
    ntime = 3 * freqs // 2
    own_az = span_az // nf
    stored = base_flow.shape[0]
    slopes, inverse_p = radial_tables(radii)
    mode_ids = (np.arange(nf)[None, :] * per_dev + np.arange(per_dev)[:, None]).reshape(-1)
    inverse, forward = transform_tables(mode_ids, freqs, ntime)
    omegas = np.broadcast_to((0.5 * mode_ids / freqs).astype(np.float32)[:, None], (freqs, radii))
    plane = lax.axis_index("plane")
    here = ring_of(lax.axis_index("freq"), plane, nf, planes)
    shape_az = chevron(lobe_count, own_az, here * own_az, span_az * planes)

    def padded_rows(count):
        return -(-count // 8) * 8

    def chunks(x, size):
        x = x.reshape(-1, nf, own_az, radii).transpose(1, 0, 2, 3).reshape(nf, -1, radii)
        x = jnp.pad(x, ((0, 0), (0, size - x.shape[1]), (0, 0)))
        return x.reshape(nf * size, radii)

    count = 2 * per_dev * variables * own_az
    rows = padded_rows(count)
    base_rows = padded_rows(stored * variables * own_az)
    w_rows = padded_rows(variables * own_az)
    dims = (nf, planes, own_az, variables, per_dev, radii, stored, rows, base_rows, w_rows)
    half = variables * freqs
    exchanges = (STEPS - 1) * SWEEPS + 1
    runs = 2 * per_dev * variables
    edge_rows = padded_rows(runs)
    first_mode = lax.axis_index("freq") * per_dev
    rates = 0.5 * (first_mode + jnp.arange(per_dev)).astype(jnp.float32) / freqs
    smem = pl.BlockSpec(memory_space=pltpu.SMEM)
    anywhere = pl.BlockSpec(memory_space=pl.ANY)
    packed = (nf * rows, radii)
    f32 = jnp.float32
    outs = pl.pallas_call(
        functools.partial(march, dims),
        out_shape=[jax.ShapeDtypeStruct(packed, f32)] * 2,
        in_specs=[smem, smem, smem, anywhere, anywhere, anywhere] + [anywhere] * 5,
        out_specs=[anywhere, anywhere],
        scratch_shapes=[
            pltpu.VMEM(packed, f32),
            pltpu.VMEM((nf * base_rows, radii), f32),
            pltpu.VMEM(packed, f32),
            pltpu.VMEM((w_rows, radii), f32),
            pltpu.VMEM((nf * w_rows, radii), f32),
            pltpu.VMEM((variables, span_az, radii), f32),
            pltpu.VMEM((2, runs, span_az + 16, radii), f32),
            pltpu.VMEM((runs, span_az, radii), f32),
            pltpu.VMEM((SWEEPS, 2, edge_rows, radii), f32),
            pltpu.VMEM((SWEEPS, 2, edge_rows, radii), f32),
            pltpu.VMEM((2, own_az + 2, 2 * half, radii), f32),
            pltpu.VMEM((own_az, 2 * half, radii), f32),
            pltpu.VMEM((own_az, 2 * half, radii), f32),
            pltpu.VMEM(((STEPS - 1) * own_az, padded_rows(variables), radii), f32),
            pltpu.VMEM(packed, f32),
            pltpu.VMEM(packed, f32),
            pltpu.SemaphoreType.DMA((5, nf)),
            pltpu.SemaphoreType.DMA((5, nf)),
            pltpu.SemaphoreType.DMA((5,)),
            pltpu.SemaphoreType.DMA((2, exchanges)),
            pltpu.SemaphoreType.DMA((2, exchanges)),
            pltpu.SemaphoreType.DMA((2, SWEEPS)),
            pltpu.SemaphoreType.DMA((2, SWEEPS)),
            pltpu.SemaphoreType.DMA((2,)),
            pltpu.VMEM((freqs, radii), f32),
            pltpu.VMEM((2 * radii, 2 * radii), jnp.bfloat16),
            pltpu.VMEM((2 * radii, 2 * radii), jnp.bfloat16),
            pltpu.VMEM((ntime, 8 * freqs), jnp.bfloat16),
            pltpu.VMEM((2 * freqs, 4 * ntime), jnp.bfloat16),
            pltpu.SemaphoreType.DMA((5,)),
        ],
        compiler_params=pltpu.CompilerParams(
            collective_id=0, has_side_effects=True, vmem_limit_bytes=63_000 * 1024
        ),
    )(
        station_index,
        shape_az,
        rates,
        state_in.reshape(runs, span_az, radii),
        chunks(base_flow, base_rows),
        forcing_in.reshape(runs, span_az, radii),
        jnp.asarray(omegas),
        right_table(inverse_p.T),
        right_table(slopes.T),
        left_table(inverse.transpose(2, 0, 1).reshape(ntime, 2 * freqs)),
        left_table(forward.reshape(2 * freqs, ntime)),
    )

    return tuple(finish(y, nf, per_dev, variables, own_az, radii, rows, count) for y in outs)


def finish(y, nf, per_dev, variables, own_az, radii, rows, count):
    y = y.reshape(nf, rows, radii)[:, :count].reshape(nf, -1, own_az, radii)
    return y.transpose(1, 0, 2, 3).reshape(2, per_dev, variables, nf * own_az, radii)


def relay(
    dims,
    station_ref,
    lobe_ref,
    state_ref,
    base_ref,
    forcing_ref,
    far_qt,
    far_st,
    far_inv,
    far_fwd,
    g_state,
    g_forcing,
    r_state,
    r_base,
    s_w,
    plane_w,
    x_one,
    b_one,
    edge_out,
    edge_in,
    x_ref,
    b_ref,
    f_ref,
    w_ref,
    o_march,
    o_forcing,
    send_sem,
    recv_sem,
    own_sem,
    halo_send,
    halo_recv,
    edge_send,
    edge_recv,
    load_sem,
    omega_ref,
    qt_ref,
    st_ref,
    inv_ref,
    fwd_ref,
    table_sem,
):
    nf, planes, own_az, variables, per_dev, radii, stored = dims
    freqs = nf * per_dev
    span = nf * own_az
    runs = 2 * per_dev * variables
    ntime = inv_ref.shape[0]
    half = variables * freqs
    me = lax.axis_index("freq")
    plane = lax.axis_index("plane")
    ring = nf * planes
    here = ring_of(me, plane, nf, planes)
    part, block = here // nf, here % nf

    def named(device):
        return {"freq": device[0], "plane": device[1]}

    right_id = named(device_of((here + 1) % ring, nf, planes))
    left_id = named(device_of((here + ring - 1) % ring, nf, planes))
    barrier = pltpu.get_barrier_semaphore()

    @pl.loop(1, ring)
    def _(d):
        other = (me * planes + plane + d) % ring
        pl.semaphore_signal(
            barrier,
            inc=1,
            device_id={"freq": other // planes, "plane": other % planes},
            device_id_type=MESH,
        )

    beyond = {"freq": me, "plane": (plane + 1) % planes}
    behind = {"freq": me, "plane": (plane + planes - 1) % planes}
    load_state = pltpu.make_async_copy(state_ref, x_one.at[0, :, pl.ds(8, span), :], load_sem.at[0])
    load_forcing = pltpu.make_async_copy(forcing_ref, b_one, load_sem.at[1])
    load_state.start()
    load_forcing.start()
    tables = [
        pltpu.make_async_copy(far, near, table_sem.at[i])
        for i, (far, near) in enumerate(
            ((far_qt, qt_ref), (far_st, st_ref), (far_inv, inv_ref), (far_fwd, fwd_ref))
        )
    ]
    for table in tables:
        table.start()
    pl.semaphore_wait(barrier, ring - 1)

    def owner(i):
        return device_of(plane * nf + i, nf, planes)

    def holder(i):
        return i, part

    def is_me(device):
        return (device[0] == me) & (device[1] == plane)

    def azimuths(i):
        return pl.ds(pl.multiple_of(i * own_az, 8), own_az)

    def exchange(k, piece, landing, target, origin, mine):
        def copy(i):
            return pltpu.make_async_remote_copy(
                src_ref=piece(i),
                dst_ref=landing(mine),
                send_sem=send_sem.at[k, i],
                recv_sem=recv_sem.at[k, mine],
                device_id=named(target(i)),
                device_id_type=MESH,
            )

        def arrival(i):
            return pltpu.make_async_remote_copy(
                src_ref=landing(i),
                dst_ref=landing(i),
                send_sem=send_sem.at[k, i],
                recv_sem=recv_sem.at[k, i],
                device_id=named(origin(i)),
                device_id_type=MESH,
            )

        def own(i):
            return pltpu.make_async_copy(piece(i), landing(mine), own_sem.at[k])

        def start():
            @pl.loop(0, nf)
            def _(d):
                i = (d + me) % nf
                stays = is_me(target(i))

                @pl.when(stays)
                def _():
                    own(i).start()

                @pl.when(jnp.logical_not(stays))
                def _():
                    copy(i).start()

        def wait():
            @pl.loop(0, nf)
            def _(d):
                i = (d + me) % nf
                stays = is_me(target(i))

                @pl.when(stays)
                def _():
                    own(i).wait()

                @pl.when(jnp.logical_not(stays))
                def _():
                    copy(i).wait_send()

                @pl.when(jnp.logical_not(is_me(origin(i))))
                def _():
                    arrival(i).wait_recv()

        return start, wait

    base_start, base_wait = exchange(
        0,
        lambda i: base_ref.at[:, azimuths(i), :],
        lambda j: r_base.at[j],
        owner,
        holder,
        me,
    )
    w_moves = [
        exchange(
            1 + s,
            lambda i, s=s: s_w.at[s],
            lambda j, s=s: plane_w.at[s, :, azimuths(j), :],
            holder,
            owner,
            block,
        )
        for s in range(STEPS)
    ]
    settled = SWEEPS % 2
    state_start, state_wait = exchange(
        1 + STEPS,
        lambda i: x_one.at[settled, :, pl.ds(pl.multiple_of(8 + i * own_az, 8), own_az), :],
        lambda j: r_state.at[j],
        owner,
        holder,
        me,
    )
    march_start, march_wait = exchange(
        2 + STEPS,
        lambda i: o_march.at[i],
        lambda j: b_one.at[:, azimuths(j), :],
        holder,
        owner,
        block,
    )
    forcing_start, forcing_wait = exchange(
        3 + STEPS,
        lambda i: o_forcing.at[i],
        lambda j: g_forcing.at[:, azimuths(j), :],
        holder,
        owner,
        block,
    )
    base_start()

    def halo_copies(e):
        slot = e % 2
        return (
            pltpu.make_async_remote_copy(
                src_ref=x_ref.at[slot, own_az],
                dst_ref=x_ref.at[slot, 0],
                send_sem=halo_send.at[0, e],
                recv_sem=halo_recv.at[0, e],
                device_id=right_id,
                device_id_type=MESH,
            ),
            pltpu.make_async_remote_copy(
                src_ref=x_ref.at[slot, 1],
                dst_ref=x_ref.at[slot, own_az + 1],
                send_sem=halo_send.at[1, e],
                recv_sem=halo_recv.at[1, e],
                device_id=left_id,
                device_id_type=MESH,
            ),
        )

    def each_run(visit):
        @pl.loop(0, own_az)
        def _(a):
            for c in range(2):
                for v in range(variables):
                    for kk in range(per_dev):
                        start = ((c * variables + v) * per_dev + kk) * nf
                        visit(a, start, (c * per_dev + kk) * variables + v)

    def edge_copies(e):
        return [
            pltpu.make_async_remote_copy(
                src_ref=edge_out.at[e, side],
                dst_ref=edge_in.at[e, side],
                send_sem=edge_send.at[side, e],
                recv_sem=edge_recv.at[side, e],
                device_id=target,
                device_id_type=MESH,
            )
            for side, target in ((0, beyond), (1, behind))
        ]

    def send_edges(slot, e):
        for m in range(runs):
            edge_out[e, 0, pl.ds(m, 1), :] = x_one[slot, m, pl.ds(7 + span, 1), :]
            edge_out[e, 1, pl.ds(m, 1), :] = x_one[slot, m, pl.ds(8, 1), :]
        for copy in edge_copies(e):
            copy.start()

    for kk in range(per_dev):
        modes = lax.broadcasted_iota(jnp.int32, (nf, radii), 0) * per_dev + kk
        omega_ref[pl.ds(kk * nf, nf), :] = 0.5 * modes.astype(jnp.float32) / freqs
    load_state.wait()
    send_edges(0, 0)
    load_forcing.wait()

    @pl.loop(0, runs)
    def _(m):
        b_one[m] = MARCH_WEIGHT * x_one[0, m, pl.ds(8, span), :] + b_one[m]

    for table in tables:
        table.wait()
    position = here * own_az + lax.broadcasted_iota(jnp.int32, (own_az, radii), 0)
    phases = (lobe_ref[0] * position) % (span * planes)
    shape = 1.0 + 0.5 * jnp.cos(2.0 * math.pi * phases.astype(jnp.float32) / (span * planes))
    base_wait()
    for station in range(STEPS):
        wanted = station_ref[station]
        for v in range(variables):
            scaled = (BASE_SCALE * shape) * r_base[
                wanted // stored, (wanted % stored) * variables + v
            ]
            s_w[station, v] = scaled
            if station > 0:
                for a in range(own_az):
                    w_ref[(station - 1) * own_az + a, pl.ds(v, 1), :] = scaled[a : a + 1]
        w_moves[station][0]()

    def freq_sweeps(station):
        @pl.loop(0, SWEEPS)
        def _(sweep):
            e = station * SWEEPS + sweep
            src, dst = e % 2, (e + 1) % 2
            for copy in edge_copies(e):
                copy.wait()
            for m in range(runs):
                x_one[src, m, pl.ds(7, 1), :] = edge_in[e, 0, pl.ds(m, 1), :]
                x_one[src, m, pl.ds(8 + span, 1), :] = edge_in[e, 1, pl.ds(m, 1), :]
            for kk in range(per_dev):
                rate = (me * per_dev + kk).astype(jnp.float32) * (0.5 / freqs)

                @pl.loop(0, variables)
                def _(v):
                    w = plane_w[station, v]
                    at = [(c * per_dev + kk) * variables + v for c in range(2)]
                    real, imag = [x_one[src, m, pl.ds(8, span), :] for m in at]
                    mixing = (w * real - rate * imag, w * imag + rate * real)
                    summed = [
                        SIDE_WEIGHT
                        * (x_one[src, m, pl.ds(7, span), :] + x_one[src, m, pl.ds(9, span), :])
                        + b_one[m]
                        - mixed
                        for m, mixed in zip(at, mixing)
                    ]
                    q = times_right(jnp.concatenate(summed, axis=0), qt_ref[...])
                    x_one[dst, at[0], pl.ds(8, span), :] = q[:span]
                    x_one[dst, at[1], pl.ds(8, span), :] = q[span:]

            @pl.when(e < STEPS * SWEEPS - 1)
            def _():
                send_edges(dst, e + 1)

    w_moves[0][1]()
    freq_sweeps(0)
    state_start()
    state_wait()

    def unpack_state(a, start, m):
        x_ref[0, a + 1, pl.ds(start, nf), :] = r_state[:, m, a, :]

    each_run(unpack_state)
    for copy in halo_copies(0):
        copy.start()
    omega = omega_ref[...][None]
    flat = (2 * half, radii)
    cube = (variables, freqs, radii)

    def sweep_slab(src, dst, a, station):
        x = x_ref[src, a + 1]
        beside = SIDE_WEIGHT * (x_ref[src, a] + x_ref[src, a + 2]) + b_ref[a]
        real, imag = x[:half].reshape(cube), x[half:].reshape(cube)
        w = w_ref[(station - 1) * own_az + a][:variables][:, None, :]
        mixing = jnp.concatenate([w * real - omega * imag, w * imag + omega * real], axis=0)
        summed = beside - mixing.reshape(flat)
        x_ref[dst, a + 1] = times_right(summed, qt_ref[...])

    def advect_slab(slot, a, final):
        x = x_ref[slot, a + 1]
        beside = 0.5 * (x_ref[slot, a + 2] - x_ref[slot, a])

        def lanes(y):
            return [
                jnp.concatenate(
                    [
                        y[v * freqs : (v + 1) * freqs],
                        y[half + v * freqs : half + (v + 1) * freqs],
                    ],
                    axis=0,
                )
                for v in range(variables)
            ]

        both = jnp.concatenate(lanes(x) + lanes(beside), axis=1)
        in_time = times_left(inv_ref[...], both)
        u = [in_time[:, v * radii : (v + 1) * radii] for v in range(variables)]
        ua = [
            in_time[:, (variables + v) * radii : (variables + v + 1) * radii]
            for v in range(variables)
        ]
        radial = times_right(jnp.concatenate(u, axis=0), st_ref[...])
        ur = [radial[v * ntime : (v + 1) * ntime] for v in range(variables)]
        n = [u[1] * ur[v] + u[2] * ua[v] for v in range(variables)]
        n[0] = n[0] + u[0] * (ur[1] + ua[2])
        source = -ADVECT_SCALE * jnp.concatenate(n, axis=1)
        spectral = times_left(fwd_ref[...], source)
        forcing = jnp.concatenate(
            [
                spectral[c * freqs : (c + 1) * freqs, v * radii : (v + 1) * radii]
                for c in range(2)
                for v in range(variables)
            ],
            axis=0,
        )
        if final:
            f_ref[a] = forcing
        else:
            b_ref[a] = MARCH_WEIGHT * x + forcing

    def advect_all(slot, e, final):
        @pl.loop(1, own_az - 1)
        def _(a):
            advect_slab(slot, a, final)

        for copy in halo_copies(e):
            copy.wait()
        advect_slab(slot, 0, final)
        advect_slab(slot, own_az - 1, final)

    def pack_march(a, start, m):
        o_march[:, m, a, :] = b_ref[a, pl.ds(start, nf), :]

    def pack_forcing(a, start, m):
        o_forcing[:, m, a, :] = f_ref[a, pl.ds(start, nf), :]

    advect_all(0, 0, False)
    each_run(pack_march)
    march_start()

    @pl.loop(0, SWEEPS)
    def _(e):
        src, dst = e % 2, (e + 1) % 2

        @pl.when(e > 0)
        def _():
            for copy in halo_copies(e):
                copy.wait()

        sweep_slab(src, dst, 0, 1)
        sweep_slab(src, dst, own_az - 1, 1)
        for copy in halo_copies(e + 1):
            copy.start()

        @pl.loop(1, own_az - 1)
        def _(a):
            sweep_slab(src, dst, a, 1)

    advect_all(SWEEPS % 2, SWEEPS, True)
    each_run(pack_forcing)
    march_wait()
    forcing_start()
    w_moves[1][1]()
    freq_sweeps(1)
    out_state = pltpu.make_async_copy(
        x_one.at[(2 * SWEEPS) % 2, :, pl.ds(8, span), :], g_state, load_sem.at[0]
    )
    out_state.start()
    out_state.wait()
    forcing_wait()


def per_device_tiled(state_in, forcing_in, base_flow, station_index, lobe_count):
    _, per_dev, variables, span_az, radii = state_in.shape
    nf = lax.axis_size("freq")
    planes = lax.axis_size("plane")
    freqs = per_dev * nf
    ntime = 3 * freqs // 2
    own_az = span_az // nf
    stored = base_flow.shape[0]
    slopes, inverse_p = radial_tables(radii)
    mode_ids = (np.arange(nf)[None, :] * per_dev + np.arange(per_dev)[:, None]).reshape(-1)
    inverse, forward = transform_tables(mode_ids, freqs, ntime)
    dims = (nf, planes, own_az, variables, per_dev, radii, stored)
    half = variables * freqs
    runs = 2 * per_dev * variables
    edge_rows = -(-runs // 8) * 8
    rounds = STEPS * SWEEPS
    smem = pl.BlockSpec(memory_space=pltpu.SMEM)
    anywhere = pl.BlockSpec(memory_space=pl.ANY)
    f32 = jnp.float32
    pieces = (nf, runs, own_az, radii)
    outs = pl.pallas_call(
        functools.partial(relay, dims),
        out_shape=[jax.ShapeDtypeStruct((runs, span_az, radii), f32)] * 2,
        in_specs=[smem, smem] + [anywhere] * 7,
        out_specs=[anywhere, anywhere],
        scratch_shapes=[
            pltpu.VMEM(pieces, f32),
            pltpu.VMEM((nf, stored * variables, own_az, radii), f32),
            pltpu.VMEM((STEPS, variables, own_az, radii), f32),
            pltpu.VMEM((STEPS, variables, span_az, radii), f32),
            pltpu.VMEM((2, runs, span_az + 16, radii), f32),
            pltpu.VMEM((runs, span_az, radii), f32),
            pltpu.VMEM((rounds, 2, edge_rows, radii), f32),
            pltpu.VMEM((rounds, 2, edge_rows, radii), f32),
            pltpu.VMEM((2, own_az + 2, 2 * half, radii), f32),
            pltpu.VMEM((own_az, 2 * half, radii), f32),
            pltpu.VMEM((own_az, 2 * half, radii), f32),
            pltpu.VMEM(((STEPS - 1) * own_az, -(-variables // 8) * 8, radii), f32),
            pltpu.VMEM(pieces, f32),
            pltpu.VMEM(pieces, f32),
            pltpu.SemaphoreType.DMA((4 + STEPS, nf)),
            pltpu.SemaphoreType.DMA((4 + STEPS, nf)),
            pltpu.SemaphoreType.DMA((4 + STEPS,)),
            pltpu.SemaphoreType.DMA((2, SWEEPS + 1)),
            pltpu.SemaphoreType.DMA((2, SWEEPS + 1)),
            pltpu.SemaphoreType.DMA((2, rounds)),
            pltpu.SemaphoreType.DMA((2, rounds)),
            pltpu.SemaphoreType.DMA((2,)),
            pltpu.VMEM((freqs, radii), f32),
            pltpu.VMEM((2 * radii, 2 * radii), jnp.bfloat16),
            pltpu.VMEM((2 * radii, 2 * radii), jnp.bfloat16),
            pltpu.VMEM((ntime, 8 * freqs), jnp.bfloat16),
            pltpu.VMEM((2 * freqs, 4 * ntime), jnp.bfloat16),
            pltpu.SemaphoreType.DMA((4,)),
        ],
        compiler_params=pltpu.CompilerParams(
            collective_id=0, has_side_effects=True, vmem_limit_bytes=63_000 * 1024
        ),
    )(
        station_index,
        lobe_count,
        state_in.reshape(runs, span_az, radii),
        base_flow.reshape(stored * variables, span_az, radii),
        forcing_in.reshape(runs, span_az, radii),
        right_table(inverse_p.T),
        right_table(slopes.T),
        left_table(inverse.transpose(2, 0, 1).reshape(ntime, 2 * freqs)),
        left_table(forward.reshape(2 * freqs, ntime)),
    )
    return tuple(y.reshape(state_in.shape) for y in outs)


def per_device_any(*args):
    tiles = args[0].shape[3] % (8 * lax.axis_size("freq")) == 0
    return (per_device_tiled if tiles else per_device)(*args)


MESH = pl.DeviceIdType.MESH


def solution(mesh):
    return jax.shard_map(
        per_device_any,
        mesh=mesh,
        in_specs=(
            P(None, "freq", None, "plane", None),
            P(None, "freq", None, "plane", None),
            P("freq", None, "plane", None),
            P(),
            P(),
        ),
        out_specs=(P(None, "freq", None, "plane", None), P(None, "freq", None, "plane", None)),
        check_vma=False,
    )
```

```python
import functools
import math

import jax
import jax.numpy as jnp
import numpy as np
from jax import lax
from jax.experimental import pallas as pl
from jax.experimental.pallas import tpu as pltpu
from jax.sharding import PartitionSpec as P

SWEEPS = 4
STEPS = 2


SIDE_WEIGHT = 1.25
MARCH_WEIGHT = 4.0
DIAG_SHIFT = 4.0
ADVECT_SCALE = 0.5
BASE_SCALE = 0.5


def radial_tables(radius_count):
    indices = np.arange(radius_count)
    angles = math.pi * indices / (radius_count - 1)
    nodes = np.cos(angles)
    weights = np.where((indices == 0) | (indices == radius_count - 1), 2.0, 1.0)
    parity = 1.0 - 2.0 * ((indices[:, None] + indices[None, :]) % 2)
    offdiag = indices[:, None] != indices[None, :]
    spacing = np.where(offdiag, nodes[:, None] - nodes[None, :], 1.0)
    entries = np.where(offdiag, weights[:, None] / weights[None, :] * parity / spacing, 0.0)
    entries = entries - np.diag(entries.sum(axis=1))
    slopes = np.sin(angles)[:, None] * entries / (radius_count - 1)
    system = slopes.T @ slopes + DIAG_SHIFT * np.eye(radius_count)
    return slopes.astype(np.float32), np.linalg.inv(system).astype(np.float32)


def transform_tables(mode_ids, freqs, ntime):
    time_ids = np.arange(ntime)
    angles = 2.0 * math.pi * (mode_ids[:, None] * time_ids[None, :] % ntime) / ntime
    stacked = np.stack([np.cos(angles), -np.sin(angles)])
    return (
        (stacked / math.sqrt(freqs)).astype(np.float32),
        (stacked / math.sqrt(ntime)).astype(np.float32),
    )


def chevron(lobe_count, azimuths, start_az, total_az):
    position = start_az + jnp.arange(azimuths)
    phases = lobe_count[0] * position % total_az
    return 1.0 + 0.5 * jnp.cos(2.0 * math.pi * phases.astype(jnp.float32) / total_az)


def halves(x):
    high = x.astype(jnp.bfloat16)
    return high, (x - high.astype(jnp.float32)).astype(jnp.bfloat16)


def right_table(table):
    high, low = np_halves(table)
    return jnp.asarray(np.tile(np.concatenate([high, low], axis=1), (2, 1)))


def left_table(table):
    high, low = np_halves(table)
    return jnp.asarray(np.concatenate([high, high, low, low], axis=1))


def np_halves(table):
    high = table.astype(jnp.bfloat16)
    return high, (table - high.astype(np.float32)).astype(jnp.bfloat16)


def times_right(x, table):
    width = table.shape[1] // 2
    y = jnp.dot(jnp.concatenate(halves(x), axis=1), table, preferred_element_type=jnp.float32)
    return y[:, :width] + y[:, width:]


def times_left(table, x):
    high, low = halves(x)
    return jnp.dot(
        table,
        jnp.concatenate([high, low, high, low], axis=0),
        preferred_element_type=jnp.float32,
    )


def ring_of(f, p, nf, planes):
    at = f
    if nf % 4 == 0:
        high = nf // 4
        z, y, x = f // 4, (f // 2) % 2, f % 2
        column = 2 * y + (x + y) % 2
        at = column * high + z + (column % 2) * (high - 1 - 2 * z)
    return at * planes + p


def device_of(g, nf, planes):
    at = g // planes
    f = at
    if nf % 4 == 0:
        high = nf // 4
        column, z = at // high, at % high
        z = z + (column % 2) * (high - 1 - 2 * z)
        y = column // 2
        f = 4 * z + 2 * y + (column + y) % 2
    return f, g % planes


def march(
    dims,
    station_ref,
    shape_ref,
    rate_ref,
    state_ref,
    s_base,
    forcing_ref,
    far_omega,
    far_qt,
    far_st,
    far_inv,
    far_fwd,
    g_state,
    g_forcing,
    r_state,
    r_base,
    s_state,
    s_w,
    r_w,
    plane_w,
    x_one,
    b_one,
    edge_out,
    edge_in,
    x_ref,
    b_ref,
    f_ref,
    w_ref,
    o_state,
    o_forcing,
    send_sem,
    recv_sem,
    own_sem,
    halo_send,
    halo_recv,
    edge_send,
    edge_recv,
    load_sem,
    omega_ref,
    qt_ref,
    st_ref,
    inv_ref,
    fwd_ref,
    table_sem,
):
    nf, planes, own_az, variables, per_dev, radii, stored, rows, base_rows, w_rows = dims
    freqs = nf * per_dev
    span = nf * own_az
    runs = 2 * per_dev * variables
    ntime = inv_ref.shape[0]
    half = variables * freqs
    me = lax.axis_index("freq")
    plane = lax.axis_index("plane")
    ring = nf * planes
    here = ring_of(me, plane, nf, planes)
    part, block = here // nf, here % nf

    def named(device):
        return {"freq": device[0], "plane": device[1]}

    right_id = named(device_of((here + 1) % ring, nf, planes))
    left_id = named(device_of((here + ring - 1) % ring, nf, planes))
    barrier = pltpu.get_barrier_semaphore()

    @pl.loop(1, ring)
    def _(d):
        other = (me * planes + plane + d) % ring
        pl.semaphore_signal(
            barrier,
            inc=1,
            device_id={"freq": other // planes, "plane": other % planes},
            device_id_type=MESH,
        )

    beyond = {"freq": me, "plane": (plane + 1) % planes}
    behind = {"freq": me, "plane": (plane + planes - 1) % planes}
    load_state = pltpu.make_async_copy(state_ref, x_one.at[0, :, pl.ds(8, span), :], load_sem.at[0])
    load_forcing = pltpu.make_async_copy(forcing_ref, b_one, load_sem.at[1])
    load_state.start()
    load_forcing.start()
    tables = [
        pltpu.make_async_copy(far, near, table_sem.at[i])
        for i, (far, near) in enumerate(
            (
                (far_omega, omega_ref),
                (far_qt, qt_ref),
                (far_st, st_ref),
                (far_inv, inv_ref),
                (far_fwd, fwd_ref),
            )
        )
    ]
    for table in tables:
        table.start()
    pl.semaphore_wait(barrier, ring - 1)

    def owner(i):
        return device_of(plane * nf + i, nf, planes)

    def holder(i):
        return i, part

    def is_me(device):
        return (device[0] == me) & (device[1] == plane)

    def exchange(k, source, landing, target, origin, pick, mine, size, first):
        def rows_of(ref, i):
            return ref.at[pl.ds(pl.multiple_of(i * size, 8), size), :]

        def copy(i):
            return pltpu.make_async_remote_copy(
                src_ref=rows_of(source, pick(i)),
                dst_ref=rows_of(landing, mine),
                send_sem=send_sem.at[k, i],
                recv_sem=recv_sem.at[k, mine],
                device_id=named(target(i)),
                device_id_type=MESH,
            )

        def arrival(i):
            return pltpu.make_async_remote_copy(
                src_ref=rows_of(landing, i),
                dst_ref=rows_of(landing, i),
                send_sem=send_sem.at[k, i],
                recv_sem=recv_sem.at[k, i],
                device_id=named(origin(i)),
                device_id_type=MESH,
            )

        def own(i):
            return pltpu.make_async_copy(
                rows_of(source, pick(i)), rows_of(landing, mine), own_sem.at[k]
            )

        @pl.loop(0, nf)
        def _(d):
            i = (d + me) % nf
            stays = is_me(target(i))

            @pl.when(stays)
            def _():
                if first:
                    own(i).start()
                else:
                    own(i).wait()

            @pl.when(jnp.logical_not(stays))
            def _():
                if first:
                    copy(i).start()
                else:
                    copy(i).wait_send()

            if not first:

                @pl.when(jnp.logical_not(is_me(origin(i))))
                def _():
                    arrival(i).wait_recv()

    def same(i):
        return i

    base_args = (1, s_base, r_base, owner, holder, same, me, base_rows)
    state_args = (0, s_state, r_state, owner, holder, same, me, rows)
    w_args = (2, s_w, r_w, holder, owner, lambda i: 0, block, w_rows)
    out_state_args = (3, o_state, g_state, holder, owner, same, block, rows)
    out_forcing_args = (4, o_forcing, g_forcing, holder, owner, same, block, rows)
    exchange(*base_args, True)

    def halo_copies(e):
        slot = e % 2
        return (
            pltpu.make_async_remote_copy(
                src_ref=x_ref.at[slot, own_az],
                dst_ref=x_ref.at[slot, 0],
                send_sem=halo_send.at[0, e],
                recv_sem=halo_recv.at[0, e],
                device_id=right_id,
                device_id_type=MESH,
            ),
            pltpu.make_async_remote_copy(
                src_ref=x_ref.at[slot, 1],
                dst_ref=x_ref.at[slot, own_az + 1],
                send_sem=halo_send.at[1, e],
                recv_sem=halo_recv.at[1, e],
                device_id=left_id,
                device_id_type=MESH,
            ),
        )

    def place(a, c, v, kk):
        return ((c * variables + v) * per_dev + kk) * nf

    def packed_row(a, c, v, kk):
        return ((c * per_dev + kk) * variables + v) * own_az + a

    def each_run(visit):
        @pl.loop(0, own_az)
        def _(a):
            for c in range(2):
                for v in range(variables):
                    for kk in range(per_dev):
                        visit(a, place(a, c, v, kk), packed_row(a, c, v, kk))

    def in_row(a, c, v, kk):
        return ((c * per_dev + kk) * variables + v) * own_az + a

    def edge_copies(e):
        return [
            pltpu.make_async_remote_copy(
                src_ref=edge_out.at[e, side],
                dst_ref=edge_in.at[e, side],
                send_sem=edge_send.at[side, e],
                recv_sem=edge_recv.at[side, e],
                device_id=target,
                device_id_type=MESH,
            )
            for side, target in ((0, beyond), (1, behind))
        ]

    def send_edges(slot, e):
        for m in range(runs):
            edge_out[e, 0, pl.ds(m, 1), :] = x_one[slot, m, pl.ds(7 + span, 1), :]
            edge_out[e, 1, pl.ds(m, 1), :] = x_one[slot, m, pl.ds(8, 1), :]
        for copy in edge_copies(e):
            copy.start()

    for table in tables:
        table.wait()
    load_state.wait()
    send_edges(0, 0)
    load_forcing.wait()

    @pl.loop(0, runs)
    def _(m):
        b_one[m] = MARCH_WEIGHT * x_one[0, m, pl.ds(8, span), :] + b_one[m]

    exchange(*base_args, False)
    for station in range(STEPS):
        wanted = station_ref[station]

        @pl.loop(0, own_az)
        def _(a):
            for v in range(variables):
                scaled = (BASE_SCALE * shape_ref[a]) * r_base[
                    pl.ds(
                        (wanted // stored) * base_rows
                        + ((wanted % stored) * variables + v) * own_az
                        + a,
                        1,
                    ),
                    :,
                ]
                if station == 0:
                    s_w[pl.ds(v * own_az + a, 1), :] = scaled
                else:
                    w_ref[(station - 1) * own_az + a, pl.ds(v, 1), :] = scaled

        if station == 0:
            exchange(*w_args, True)
    exchange(*w_args, False)

    @pl.loop(0, nf)
    def _(j):
        for v in range(variables):
            plane_w[v, pl.ds(j * own_az, own_az), :] = r_w[pl.ds(j * w_rows + v * own_az, own_az), :]

    @pl.loop(0, SWEEPS)
    def _(e):
        src, dst = e % 2, (e + 1) % 2
        for copy in edge_copies(e):
            copy.wait()
        for m in range(runs):
            x_one[src, m, pl.ds(7, 1), :] = edge_in[e, 0, pl.ds(m, 1), :]
            x_one[src, m, pl.ds(8 + span, 1), :] = edge_in[e, 1, pl.ds(m, 1), :]
        for kk in range(per_dev):
            rate = rate_ref[kk]

            @pl.loop(0, variables)
            def _(v):
                w = plane_w[v]
                at = [(c * per_dev + kk) * variables + v for c in range(2)]
                real, imag = [x_one[src, m, pl.ds(8, span), :] for m in at]
                mixing = (w * real - rate * imag, w * imag + rate * real)
                summed = [
                    SIDE_WEIGHT
                    * (x_one[src, m, pl.ds(7, span), :] + x_one[src, m, pl.ds(9, span), :])
                    + b_one[m]
                    - mixed
                    for m, mixed in zip(at, mixing)
                ]
                q = times_right(jnp.concatenate(summed, axis=0), qt_ref[...])
                x_one[dst, at[0], pl.ds(8, span), :] = q[:span]
                x_one[dst, at[1], pl.ds(8, span), :] = q[span:]

        @pl.when(e < SWEEPS - 1)
        def _():
            send_edges(dst, e + 1)

    settled = SWEEPS % 2

    @pl.loop(0, nf)
    def _(j):
        for m in range(runs):
            s_state[pl.ds(j * rows + m * own_az, own_az), :] = x_one[
                settled, m, pl.ds(8 + j * own_az, own_az), :
            ]

    exchange(*state_args, True)
    exchange(*state_args, False)

    def unpack_state(a, start, row):
        x_ref[0, a + 1, pl.ds(start, nf), :] = r_state[pl.ds(row, nf, stride=rows), :]

    each_run(unpack_state)
    for copy in halo_copies(0):
        copy.start()
    omega = omega_ref[...][None]
    flat = (2 * half, radii)
    cube = (variables, freqs, radii)

    def sweep_slab(src, dst, a, station):
        x = x_ref[src, a + 1]
        beside = SIDE_WEIGHT * (x_ref[src, a] + x_ref[src, a + 2]) + b_ref[a]
        real, imag = x[:half].reshape(cube), x[half:].reshape(cube)
        w = w_ref[(station - 1) * own_az + a][:variables][:, None, :]
        mixing = jnp.concatenate([w * real - omega * imag, w * imag + omega * real], axis=0)
        summed = beside - mixing.reshape(flat)
        x_ref[dst, a + 1] = times_right(summed, qt_ref[...])

    def advect_slab(slot, a, final):
        x = x_ref[slot, a + 1]
        beside = 0.5 * (x_ref[slot, a + 2] - x_ref[slot, a])

        def lanes(y):
            return [
                jnp.concatenate(
                    [
                        y[v * freqs : (v + 1) * freqs],
                        y[half + v * freqs : half + (v + 1) * freqs],
                    ],
                    axis=0,
                )
                for v in range(variables)
            ]

        both = jnp.concatenate(lanes(x) + lanes(beside), axis=1)
        in_time = times_left(inv_ref[...], both)
        u = [in_time[:, v * radii : (v + 1) * radii] for v in range(variables)]
        ua = [
            in_time[:, (variables + v) * radii : (variables + v + 1) * radii]
            for v in range(variables)
        ]
        radial = times_right(jnp.concatenate(u, axis=0), st_ref[...])
        ur = [radial[v * ntime : (v + 1) * ntime] for v in range(variables)]
        n = [u[1] * ur[v] + u[2] * ua[v] for v in range(variables)]
        n[0] = n[0] + u[0] * (ur[1] + ua[2])
        source = -ADVECT_SCALE * jnp.concatenate(n, axis=1)
        spectral = times_left(fwd_ref[...], source)
        forcing = jnp.concatenate(
            [
                spectral[c * freqs : (c + 1) * freqs, v * radii : (v + 1) * radii]
                for c in range(2)
                for v in range(variables)
            ],
            axis=0,
        )
        if final:
            f_ref[a] = forcing
        else:
            b_ref[a] = MARCH_WEIGHT * x + forcing

    def advect_all(slot, e, final):
        @pl.loop(1, own_az - 1)
        def _(a):
            advect_slab(slot, a, final)

        for copy in halo_copies(e):
            copy.wait()
        advect_slab(slot, 0, final)
        if own_az > 1:
            advect_slab(slot, own_az - 1, final)

    advect_all(0, 0, False)
    for station in range(1, STEPS):

        @pl.loop(0, SWEEPS)
        def _(sweep):
            e = (station - 1) * SWEEPS + sweep
            src, dst = e % 2, (e + 1) % 2

            @pl.when(sweep > 0)
            def _():
                for copy in halo_copies(e):
                    copy.wait()

            sweep_slab(src, dst, 0, station)
            if own_az > 1:
                sweep_slab(src, dst, own_az - 1, station)
            for copy in halo_copies(e + 1):
                copy.start()

            @pl.loop(1, own_az - 1)
            def _(a):
                sweep_slab(src, dst, a, station)

        last = station * SWEEPS
        slot = last % 2
        final = station == STEPS - 1
        if final:

            def pack_state(a, start, row):
                o_state[pl.ds(row, nf, stride=rows), :] = x_ref[slot, a + 1, pl.ds(start, nf), :]

            each_run(pack_state)
            exchange(*out_state_args, True)

        advect_all(slot, last, final)

    def pack_forcing(a, start, row):
        o_forcing[pl.ds(row, nf, stride=rows), :] = f_ref[a, pl.ds(start, nf), :]

    each_run(pack_forcing)
    exchange(*out_forcing_args, True)
    exchange(*out_state_args, False)
    exchange(*out_forcing_args, False)


def per_device(state_in, forcing_in, base_flow, station_index, lobe_count):
    _, per_dev, variables, span_az, radii = state_in.shape
    nf = lax.axis_size("freq")
    planes = lax.axis_size("plane")
    freqs = per_dev * nf
    ntime = 3 * freqs // 2
    own_az = span_az // nf
    stored = base_flow.shape[0]
    slopes, inverse_p = radial_tables(radii)
    mode_ids = (np.arange(nf)[None, :] * per_dev + np.arange(per_dev)[:, None]).reshape(-1)
    inverse, forward = transform_tables(mode_ids, freqs, ntime)
    omegas = np.broadcast_to((0.5 * mode_ids / freqs).astype(np.float32)[:, None], (freqs, radii))
    plane = lax.axis_index("plane")
    here = ring_of(lax.axis_index("freq"), plane, nf, planes)
    shape_az = chevron(lobe_count, own_az, here * own_az, span_az * planes)

    def padded_rows(count):
        return -(-count // 8) * 8

    def chunks(x, size):
        x = x.reshape(-1, nf, own_az, radii).transpose(1, 0, 2, 3).reshape(nf, -1, radii)
        x = jnp.pad(x, ((0, 0), (0, size - x.shape[1]), (0, 0)))
        return x.reshape(nf * size, radii)

    count = 2 * per_dev * variables * own_az
    rows = padded_rows(count)
    base_rows = padded_rows(stored * variables * own_az)
    w_rows = padded_rows(variables * own_az)
    dims = (nf, planes, own_az, variables, per_dev, radii, stored, rows, base_rows, w_rows)
    half = variables * freqs
    exchanges = (STEPS - 1) * SWEEPS + 1
    runs = 2 * per_dev * variables
    edge_rows = padded_rows(runs)
    first_mode = lax.axis_index("freq") * per_dev
    rates = 0.5 * (first_mode + jnp.arange(per_dev)).astype(jnp.float32) / freqs
    smem = pl.BlockSpec(memory_space=pltpu.SMEM)
    anywhere = pl.BlockSpec(memory_space=pl.ANY)
    packed = (nf * rows, radii)
    f32 = jnp.float32
    outs = pl.pallas_call(
        functools.partial(march, dims),
        out_shape=[jax.ShapeDtypeStruct(packed, f32)] * 2,
        in_specs=[smem, smem, smem, anywhere, anywhere, anywhere] + [anywhere] * 5,
        out_specs=[anywhere, anywhere],
        scratch_shapes=[
            pltpu.VMEM(packed, f32),
            pltpu.VMEM((nf * base_rows, radii), f32),
            pltpu.VMEM(packed, f32),
            pltpu.VMEM((w_rows, radii), f32),
            pltpu.VMEM((nf * w_rows, radii), f32),
            pltpu.VMEM((variables, span_az, radii), f32),
            pltpu.VMEM((2, runs, span_az + 16, radii), f32),
            pltpu.VMEM((runs, span_az, radii), f32),
            pltpu.VMEM((SWEEPS, 2, edge_rows, radii), f32),
            pltpu.VMEM((SWEEPS, 2, edge_rows, radii), f32),
            pltpu.VMEM((2, own_az + 2, 2 * half, radii), f32),
            pltpu.VMEM((own_az, 2 * half, radii), f32),
            pltpu.VMEM((own_az, 2 * half, radii), f32),
            pltpu.VMEM(((STEPS - 1) * own_az, padded_rows(variables), radii), f32),
            pltpu.VMEM(packed, f32),
            pltpu.VMEM(packed, f32),
            pltpu.SemaphoreType.DMA((5, nf)),
            pltpu.SemaphoreType.DMA((5, nf)),
            pltpu.SemaphoreType.DMA((5,)),
            pltpu.SemaphoreType.DMA((2, exchanges)),
            pltpu.SemaphoreType.DMA((2, exchanges)),
            pltpu.SemaphoreType.DMA((2, SWEEPS)),
            pltpu.SemaphoreType.DMA((2, SWEEPS)),
            pltpu.SemaphoreType.DMA((2,)),
            pltpu.VMEM((freqs, radii), f32),
            pltpu.VMEM((2 * radii, 2 * radii), jnp.bfloat16),
            pltpu.VMEM((2 * radii, 2 * radii), jnp.bfloat16),
            pltpu.VMEM((ntime, 8 * freqs), jnp.bfloat16),
            pltpu.VMEM((2 * freqs, 4 * ntime), jnp.bfloat16),
            pltpu.SemaphoreType.DMA((5,)),
        ],
        compiler_params=pltpu.CompilerParams(
            collective_id=0, has_side_effects=True, vmem_limit_bytes=63_000 * 1024
        ),
    )(
        station_index,
        shape_az,
        rates,
        state_in.reshape(runs, span_az, radii),
        chunks(base_flow, base_rows),
        forcing_in.reshape(runs, span_az, radii),
        jnp.asarray(omegas),
        right_table(inverse_p.T),
        right_table(slopes.T),
        left_table(inverse.transpose(2, 0, 1).reshape(ntime, 2 * freqs)),
        left_table(forward.reshape(2 * freqs, ntime)),
    )

    return tuple(finish(y, nf, per_dev, variables, own_az, radii, rows, count) for y in outs)


def finish(y, nf, per_dev, variables, own_az, radii, rows, count):
    y = y.reshape(nf, rows, radii)[:, :count].reshape(nf, -1, own_az, radii)
    return y.transpose(1, 0, 2, 3).reshape(2, per_dev, variables, nf * own_az, radii)


def relay(
    dims,
    station_ref,
    lobe_ref,
    state_ref,
    base_ref,
    forcing_ref,
    far_qt,
    far_st,
    far_inv,
    far_fwd,
    g_state,
    g_forcing,
    r_state,
    r_base,
    s_w,
    plane_w,
    x_one,
    b_one,
    edge_out,
    edge_in,
    x_ref,
    b_ref,
    w_ref,
    o_state,
    o_forcing,
    send_sem,
    recv_sem,
    own_sem,
    halo_send,
    halo_recv,
    edge_send,
    edge_recv,
    load_sem,
    omega_ref,
    qt_ref,
    st_ref,
    inv_ref,
    fwd_ref,
    table_sem,
):
    nf, planes, own_az, variables, per_dev, radii, stored = dims
    freqs = nf * per_dev
    span = nf * own_az
    parts = 2 * per_dev
    ntime = inv_ref.shape[0]
    pair = 2 * freqs
    me = lax.axis_index("freq")
    plane = lax.axis_index("plane")
    ring = nf * planes
    here = ring_of(me, plane, nf, planes)
    part, block = here // nf, here % nf

    def named(device):
        return {"freq": device[0], "plane": device[1]}

    right_id = named(device_of((here + 1) % ring, nf, planes))
    left_id = named(device_of((here + ring - 1) % ring, nf, planes))
    barrier = pltpu.get_barrier_semaphore()

    @pl.loop(1, ring)
    def _(d):
        other = (me * planes + plane + d) % ring
        pl.semaphore_signal(
            barrier,
            inc=1,
            device_id={"freq": other // planes, "plane": other % planes},
            device_id_type=MESH,
        )

    beyond = {"freq": me, "plane": (plane + 1) % planes}
    behind = {"freq": me, "plane": (plane + planes - 1) % planes}
    load_state = pltpu.make_async_copy(
        state_ref, x_one.at[0, :, :, pl.ds(8, span), :], load_sem.at[0]
    )
    load_forcing = pltpu.make_async_copy(forcing_ref, b_one, load_sem.at[1])
    load_state.start()
    load_forcing.start()
    tables = [
        pltpu.make_async_copy(far, near, table_sem.at[i])
        for i, (far, near) in enumerate(
            ((far_qt, qt_ref), (far_st, st_ref), (far_inv, inv_ref), (far_fwd, fwd_ref))
        )
    ]
    for table in tables:
        table.start()
    pl.semaphore_wait(barrier, ring - 1)

    def owner(i):
        return device_of(plane * nf + i, nf, planes)

    def holder(i):
        return i, part

    def is_me(device):
        return (device[0] == me) & (device[1] == plane)

    def azimuths(i):
        return pl.ds(pl.multiple_of(i * own_az, 8), own_az)

    def exchange(k, piece, landing, target, origin, mine):
        def copy(i):
            return pltpu.make_async_remote_copy(
                src_ref=piece(i),
                dst_ref=landing(mine),
                send_sem=send_sem.at[k, i],
                recv_sem=recv_sem.at[k, mine],
                device_id=named(target(i)),
                device_id_type=MESH,
            )

        def arrival(i):
            return pltpu.make_async_remote_copy(
                src_ref=landing(i),
                dst_ref=landing(i),
                send_sem=send_sem.at[k, i],
                recv_sem=recv_sem.at[k, i],
                device_id=named(origin(i)),
                device_id_type=MESH,
            )

        def own(i):
            return pltpu.make_async_copy(piece(i), landing(mine), own_sem.at[k])

        def start():
            @pl.loop(0, nf)
            def _(d):
                i = (d + me) % nf
                stays = is_me(target(i))

                @pl.when(stays)
                def _():
                    own(i).start()

                @pl.when(jnp.logical_not(stays))
                def _():
                    copy(i).start()

        def wait():
            @pl.loop(0, nf)
            def _(d):
                i = (d + me) % nf
                stays = is_me(target(i))

                @pl.when(stays)
                def _():
                    own(i).wait()

                @pl.when(jnp.logical_not(stays))
                def _():
                    copy(i).wait_send()

                @pl.when(jnp.logical_not(is_me(origin(i))))
                def _():
                    arrival(i).wait_recv()

        return start, wait

    base_start, base_wait = exchange(
        0,
        lambda i: base_ref.at[:, :, azimuths(i), :],
        lambda j: r_base.at[j],
        owner,
        holder,
        me,
    )
    groups = [(v, min(v + GROUP, variables)) for v in range(0, variables, GROUP)]

    def w_moves(g):
        first, stop = groups[g]
        return exchange(
            1 + g,
            lambda i: s_w.at[pl.ds(first, stop - first)],
            lambda j: plane_w.at[pl.ds(first, stop - first), azimuths(j), :],
            holder,
            owner,
            block,
        )

    settled = SWEEPS % 2

    def state_moves(v):
        return exchange(
            1 + variables + v,
            lambda i: x_one.at[
                settled, :, v, pl.ds(pl.multiple_of(8 + i * own_az, 8), own_az), :
            ],
            lambda j: r_state.at[j, v],
            owner,
            holder,
            me,
        )

    def out_moves(v):
        return exchange(
            1 + 2 * variables + v,
            lambda i: o_state.at[i, v],
            lambda j: g_state.at[:, v, azimuths(j), :],
            holder,
            owner,
            block,
        )

    forcing_start, forcing_wait = exchange(
        1 + 3 * variables,
        lambda i: o_forcing.at[i],
        lambda j: g_forcing.at[:, :, azimuths(j), :],
        holder,
        owner,
        block,
    )
    base_start()

    def halo_copies(e, v):
        slot = e % 2
        rows = pl.ds(pl.multiple_of(v * pair, 8), pair)
        return [
            pltpu.make_async_remote_copy(
                src_ref=x_ref.at[slot, source, rows, :],
                dst_ref=x_ref.at[slot, target, rows, :],
                send_sem=halo_send.at[side, e, v],
                recv_sem=halo_recv.at[side, e, v],
                device_id=device,
                device_id_type=MESH,
            )
            for side, source, target, device in (
                (0, own_az, 0, right_id),
                (1, 1, own_az + 1, left_id),
            )
        ]

    def edge_copies(e, v):
        return [
            pltpu.make_async_remote_copy(
                src_ref=edge_out.at[e, v, side],
                dst_ref=edge_in.at[e, v, side],
                send_sem=edge_send.at[side, e, v],
                recv_sem=edge_recv.at[side, e, v],
                device_id=target,
                device_id_type=MESH,
            )
            for side, target in ((0, beyond), (1, behind))
        ]

    def send_edges(slot, e, v):
        for ck in range(parts):
            edge_out[e, v, 0, pl.ds(ck, 1), :] = x_one[slot, ck, v, pl.ds(7 + span, 1), :]
            edge_out[e, v, 1, pl.ds(ck, 1), :] = x_one[slot, ck, v, pl.ds(8, 1), :]
        for copy in edge_copies(e, v):
            copy.start()

    for kk in range(per_dev):
        modes = lax.broadcasted_iota(jnp.int32, (nf, radii), 0) * per_dev + kk
        omega_ref[pl.ds(kk * nf, nf), :] = 0.5 * modes.astype(jnp.float32) / freqs
    load_state.wait()

    @pl.loop(0, variables)
    def _(v):
        send_edges(0, 0, v)

    load_forcing.wait()

    @pl.loop(0, variables)
    def _(v):
        for ck in range(parts):
            b_one[ck, v] = MARCH_WEIGHT * x_one[0, ck, v, pl.ds(8, span), :] + b_one[ck, v]

    for table in tables:
        table.wait()
    position = here * own_az + lax.broadcasted_iota(jnp.int32, (own_az, radii), 0)
    phases = (lobe_ref[0] * position) % (span * planes)
    shape = 1.0 + 0.5 * jnp.cos(2.0 * math.pi * phases.astype(jnp.float32) / (span * planes))
    base_wait()

    def coefficient(station, v):
        wanted = station_ref[station]
        return (BASE_SCALE * shape) * r_base[wanted // stored, wanted % stored, v]

    for g, (first, stop) in enumerate(groups):
        for v in range(first, stop):
            s_w[v] = coefficient(0, v)
        w_moves(g)[0]()
    for v in range(variables):
        w_ref[v] = coefficient(1, v)

    for g, (first, stop) in enumerate(groups):
        w_moves(g)[1]()

        @pl.loop(0, SWEEPS * (stop - first))
        def _(turn):
            e, v = turn // (stop - first), first + turn % (stop - first)
            src, dst = e % 2, (e + 1) % 2
            for copy in edge_copies(e, v):
                copy.wait()
            for ck in range(parts):
                x_one[src, ck, v, pl.ds(7, 1), :] = edge_in[e, v, 0, pl.ds(ck, 1), :]
                x_one[src, ck, v, pl.ds(8 + span, 1), :] = edge_in[e, v, 1, pl.ds(ck, 1), :]
            w = plane_w[v]
            for kk in range(per_dev):
                rate = (me * per_dev + kk).astype(jnp.float32) * (0.5 / freqs)
                at = [c * per_dev + kk for c in range(2)]
                real, imag = [x_one[src, ck, v, pl.ds(8, span), :] for ck in at]
                mixing = (w * real - rate * imag, w * imag + rate * real)
                summed = [
                    SIDE_WEIGHT
                    * (x_one[src, ck, v, pl.ds(7, span), :] + x_one[src, ck, v, pl.ds(9, span), :])
                    + b_one[ck, v]
                    - mixed
                    for ck, mixed in zip(at, mixing)
                ]
                q = times_right(jnp.concatenate(summed, axis=0), qt_ref[...])
                x_one[dst, at[0], v, pl.ds(8, span), :] = q[:span]
                x_one[dst, at[1], v, pl.ds(8, span), :] = q[span:]

            @pl.when(e < SWEEPS - 1)
            def _():
                send_edges(dst, e + 1, v)

            @pl.when(e == SWEEPS - 1)
            def _():
                state_moves(v)[0]()

    def each_run(v, visit):
        for c in range(2):
            for kk in range(per_dev):
                start = pl.multiple_of(v * pair + (c * per_dev + kk) * nf, 8)
                visit(start, c * per_dev + kk)

    @pl.loop(0, variables)
    def _(v):
        state_moves(v)[1]()

        @pl.loop(0, own_az)
        def _(a):
            def unpack(start, ck):
                x_ref[0, a + 1, pl.ds(start, nf), :] = r_state[:, v, ck, a, :]

            each_run(v, unpack)

        for copy in halo_copies(0, v):
            copy.start()

    omega = omega_ref[...]

    def sweep_slabs(e, v):
        src, dst = e % 2, (e + 1) % 2
        rows = pl.ds(pl.multiple_of(v * pair, 8), pair)
        w = w_ref[v]
        summed = []
        for a in range(own_az):
            x = x_ref[src, a + 1, rows, :]
            beside = SIDE_WEIGHT * (x_ref[src, a, rows, :] + x_ref[src, a + 2, rows, :])
            real, imag = x[:freqs], x[freqs:]
            here_w = w[a : a + 1]
            mixing = [here_w * real - omega * imag, here_w * imag + omega * real]
            summed.append(beside + b_ref[a, rows, :] - jnp.concatenate(mixing, axis=0))
        q = times_right(jnp.concatenate(summed, axis=0), qt_ref[...])
        for a in range(own_az):
            x_ref[dst, a + 1, rows, :] = q[a * pair : (a + 1) * pair]

    def advect_slab(slot, a, final):
        x = x_ref[slot, a + 1]
        beside = 0.5 * (x_ref[slot, a + 2] - x_ref[slot, a])

        def lanes(y):
            return [y[v * pair : (v + 1) * pair] for v in range(variables)]

        both = jnp.concatenate(lanes(x) + lanes(beside), axis=1)
        in_time = times_left(inv_ref[...], both)
        u = [in_time[:, v * radii : (v + 1) * radii] for v in range(variables)]
        ua = [
            in_time[:, (variables + v) * radii : (variables + v + 1) * radii]
            for v in range(variables)
        ]
        radial = times_right(jnp.concatenate(u, axis=0), st_ref[...])
        ur = [radial[v * ntime : (v + 1) * ntime] for v in range(variables)]
        n = [u[1] * ur[v] + u[2] * ua[v] for v in range(variables)]
        n[0] = n[0] + u[0] * (ur[1] + ua[2])
        source = -ADVECT_SCALE * jnp.concatenate(n, axis=1)
        spectral = times_left(fwd_ref[...], source)
        for v in range(variables):
            forcing = spectral[:, v * radii : (v + 1) * radii]
            if final:
                for ck in range(parts):
                    o_forcing[:, ck, v, a, :] = forcing[ck * nf : (ck + 1) * nf]
            else:
                b_ref[a, pl.ds(v * pair, pair), :] = (
                    MARCH_WEIGHT * x[v * pair : (v + 1) * pair] + forcing
                )

    def advect_all(e, final):
        slot = e % 2

        @pl.loop(1, own_az - 1)
        def _(a):
            advect_slab(slot, a, final)

        @pl.loop(0, variables)
        def _(v):
            for copy in halo_copies(e, v):
                copy.wait()

        @pl.loop(0, 2)
        def _(side):
            advect_slab(slot, side * (own_az - 1), final)

    advect_all(0, False)

    @pl.loop(0, SWEEPS * variables)
    def _(turn):
        e, v = turn // variables, turn % variables

        @pl.when(e > 0)
        def _():
            for copy in halo_copies(e, v):
                copy.wait()

        sweep_slabs(e, v)
        for copy in halo_copies(e + 1, v):
            copy.start()

        @pl.when(e == SWEEPS - 1)
        def _():
            @pl.loop(0, own_az)
            def _(a):
                def pack(start, ck):
                    o_state[:, v, ck, a, :] = x_ref[settled, a + 1, pl.ds(start, nf), :]

                each_run(v, pack)

            out_moves(v)[0]()

    advect_all(SWEEPS, True)
    forcing_start()

    @pl.loop(0, variables)
    def _(v):
        out_moves(v)[1]()

    forcing_wait()


GROUP = 3


def per_device_tiled(state_in, forcing_in, base_flow, station_index, lobe_count):
    _, per_dev, variables, span_az, radii = state_in.shape
    nf = lax.axis_size("freq")
    planes = lax.axis_size("plane")
    freqs = per_dev * nf
    ntime = 3 * freqs // 2
    own_az = span_az // nf
    stored = base_flow.shape[0]
    slopes, inverse_p = radial_tables(radii)
    mode_ids = (np.arange(nf)[None, :] * per_dev + np.arange(per_dev)[:, None]).reshape(-1)
    inverse, forward = transform_tables(mode_ids, freqs, ntime)
    dims = (nf, planes, own_az, variables, per_dev, radii, stored)
    parts = 2 * per_dev
    edge_rows = -(-parts // 8) * 8
    smem = pl.BlockSpec(memory_space=pltpu.SMEM)
    anywhere = pl.BlockSpec(memory_space=pl.ANY)
    f32 = jnp.float32
    whole = (parts, variables, span_az, radii)
    slab = variables * 2 * freqs
    moves = 2 + 3 * variables
    outs = pl.pallas_call(
        functools.partial(relay, dims),
        out_shape=[jax.ShapeDtypeStruct(whole, f32)] * 2,
        in_specs=[smem, smem] + [anywhere] * 7,
        out_specs=[anywhere, anywhere],
        scratch_shapes=[
            pltpu.VMEM((nf, variables, parts, own_az, radii), f32),
            pltpu.VMEM((nf, stored, variables, own_az, radii), f32),
            pltpu.VMEM((variables, own_az, radii), f32),
            pltpu.VMEM((variables, span_az, radii), f32),
            pltpu.VMEM((2, parts, variables, span_az + 16, radii), f32),
            pltpu.VMEM(whole, f32),
            pltpu.VMEM((SWEEPS, variables, 2, edge_rows, radii), f32),
            pltpu.VMEM((SWEEPS, variables, 2, edge_rows, radii), f32),
            pltpu.VMEM((2, own_az + 2, slab, radii), f32),
            pltpu.VMEM((own_az, slab, radii), f32),
            pltpu.VMEM((variables, own_az, radii), f32),
            pltpu.VMEM((nf, variables, parts, own_az, radii), f32),
            pltpu.VMEM((nf, parts, variables, own_az, radii), f32),
            pltpu.SemaphoreType.DMA((moves, nf)),
            pltpu.SemaphoreType.DMA((moves, nf)),
            pltpu.SemaphoreType.DMA((moves,)),
            pltpu.SemaphoreType.DMA((2, SWEEPS + 1, variables)),
            pltpu.SemaphoreType.DMA((2, SWEEPS + 1, variables)),
            pltpu.SemaphoreType.DMA((2, SWEEPS, variables)),
            pltpu.SemaphoreType.DMA((2, SWEEPS, variables)),
            pltpu.SemaphoreType.DMA((2,)),
            pltpu.VMEM((freqs, radii), f32),
            pltpu.VMEM((2 * radii, 2 * radii), jnp.bfloat16),
            pltpu.VMEM((2 * radii, 2 * radii), jnp.bfloat16),
            pltpu.VMEM((ntime, 8 * freqs), jnp.bfloat16),
            pltpu.VMEM((2 * freqs, 4 * ntime), jnp.bfloat16),
            pltpu.SemaphoreType.DMA((4,)),
        ],
        compiler_params=pltpu.CompilerParams(
            collective_id=0, has_side_effects=True, vmem_limit_bytes=63_000 * 1024
        ),
    )(
        station_index,
        lobe_count,
        state_in.reshape(whole),
        base_flow,
        forcing_in.reshape(whole),
        right_table(inverse_p.T),
        right_table(slopes.T),
        left_table(inverse.transpose(2, 0, 1).reshape(ntime, 2 * freqs)),
        left_table(forward.reshape(2 * freqs, ntime)),
    )
    return tuple(y.reshape(state_in.shape) for y in outs)


def per_device_any(*args):
    tiles = args[0].shape[3] % (8 * lax.axis_size("freq")) == 0
    return (per_device_tiled if tiles else per_device)(*args)


MESH = pl.DeviceIdType.MESH


def solution(mesh):
    return jax.shard_map(
        per_device_any,
        mesh=mesh,
        in_specs=(
            P(None, "freq", None, "plane", None),
            P(None, "freq", None, "plane", None),
            P("freq", None, "plane", None),
            P(),
            P(),
        ),
        out_specs=(P(None, "freq", None, "plane", None), P(None, "freq", None, "plane", None)),
        check_vma=False,
    )
```

```python
import functools
import math

import jax
import jax.numpy as jnp
import numpy as np
from jax import lax
from jax.experimental import pallas as pl
from jax.experimental.pallas import tpu as pltpu
from jax.sharding import PartitionSpec as P

SWEEPS = 4
STEPS = 2


SIDE_WEIGHT = 1.25
MARCH_WEIGHT = 4.0
DIAG_SHIFT = 4.0
ADVECT_SCALE = 0.5
BASE_SCALE = 0.5


def radial_tables(radius_count):
    indices = np.arange(radius_count)
    angles = math.pi * indices / (radius_count - 1)
    nodes = np.cos(angles)
    weights = np.where((indices == 0) | (indices == radius_count - 1), 2.0, 1.0)
    parity = 1.0 - 2.0 * ((indices[:, None] + indices[None, :]) % 2)
    offdiag = indices[:, None] != indices[None, :]
    spacing = np.where(offdiag, nodes[:, None] - nodes[None, :], 1.0)
    entries = np.where(offdiag, weights[:, None] / weights[None, :] * parity / spacing, 0.0)
    entries = entries - np.diag(entries.sum(axis=1))
    slopes = np.sin(angles)[:, None] * entries / (radius_count - 1)
    system = slopes.T @ slopes + DIAG_SHIFT * np.eye(radius_count)
    return slopes.astype(np.float32), np.linalg.inv(system).astype(np.float32)


def transform_tables(mode_ids, freqs, ntime):
    time_ids = np.arange(ntime)
    angles = 2.0 * math.pi * (mode_ids[:, None] * time_ids[None, :] % ntime) / ntime
    stacked = np.stack([np.cos(angles), -np.sin(angles)])
    return (
        (stacked / math.sqrt(freqs)).astype(np.float32),
        (stacked / math.sqrt(ntime)).astype(np.float32),
    )


def chevron(lobe_count, azimuths, start_az, total_az):
    position = start_az + jnp.arange(azimuths)
    phases = lobe_count[0] * position % total_az
    return 1.0 + 0.5 * jnp.cos(2.0 * math.pi * phases.astype(jnp.float32) / total_az)


def halves(x):
    high = x.astype(jnp.bfloat16)
    return high, (x - high.astype(jnp.float32)).astype(jnp.bfloat16)


def right_table(table):
    high, low = np_halves(table)
    return jnp.asarray(np.tile(np.concatenate([high, low], axis=1), (2, 1)))


def left_table(table):
    high, low = np_halves(table)
    return jnp.asarray(np.concatenate([high, high, low, low], axis=1))


def np_halves(table):
    high = table.astype(jnp.bfloat16)
    return high, (table - high.astype(np.float32)).astype(jnp.bfloat16)


def times_right(x, table):
    width = table.shape[1] // 2
    y = jnp.dot(jnp.concatenate(halves(x), axis=1), table, preferred_element_type=jnp.float32)
    return y[:, :width] + y[:, width:]


def times_left(table, x):
    high, low = halves(x)
    return jnp.dot(
        table,
        jnp.concatenate([high, low, high, low], axis=0),
        preferred_element_type=jnp.float32,
    )


def ring_of(f, p, nf, planes):
    at = f
    if nf % 4 == 0:
        high = nf // 4
        z, y, x = f // 4, (f // 2) % 2, f % 2
        column = 2 * y + (x + y) % 2
        at = column * high + z + (column % 2) * (high - 1 - 2 * z)
    return at * planes + p


def device_of(g, nf, planes):
    at = g // planes
    f = at
    if nf % 4 == 0:
        high = nf // 4
        column, z = at // high, at % high
        z = z + (column % 2) * (high - 1 - 2 * z)
        y = column // 2
        f = 4 * z + 2 * y + (column + y) % 2
    return f, g % planes


def march(
    dims,
    station_ref,
    shape_ref,
    rate_ref,
    state_ref,
    s_base,
    forcing_ref,
    far_omega,
    far_qt,
    far_st,
    far_inv,
    far_fwd,
    g_state,
    g_forcing,
    r_state,
    r_base,
    s_state,
    s_w,
    r_w,
    plane_w,
    x_one,
    b_one,
    edge_out,
    edge_in,
    x_ref,
    b_ref,
    f_ref,
    w_ref,
    o_state,
    o_forcing,
    send_sem,
    recv_sem,
    own_sem,
    halo_send,
    halo_recv,
    edge_send,
    edge_recv,
    load_sem,
    omega_ref,
    qt_ref,
    st_ref,
    inv_ref,
    fwd_ref,
    table_sem,
):
    nf, planes, own_az, variables, per_dev, radii, stored, rows, base_rows, w_rows = dims
    freqs = nf * per_dev
    span = nf * own_az
    runs = 2 * per_dev * variables
    ntime = inv_ref.shape[0]
    half = variables * freqs
    me = lax.axis_index("freq")
    plane = lax.axis_index("plane")
    ring = nf * planes
    here = ring_of(me, plane, nf, planes)
    part, block = here // nf, here % nf

    def named(device):
        return {"freq": device[0], "plane": device[1]}

    right_id = named(device_of((here + 1) % ring, nf, planes))
    left_id = named(device_of((here + ring - 1) % ring, nf, planes))
    barrier = pltpu.get_barrier_semaphore()

    @pl.loop(1, ring)
    def _(d):
        other = (me * planes + plane + d) % ring
        pl.semaphore_signal(
            barrier,
            inc=1,
            device_id={"freq": other // planes, "plane": other % planes},
            device_id_type=MESH,
        )

    beyond = {"freq": me, "plane": (plane + 1) % planes}
    behind = {"freq": me, "plane": (plane + planes - 1) % planes}
    load_state = pltpu.make_async_copy(state_ref, x_one.at[0, :, pl.ds(8, span), :], load_sem.at[0])
    load_forcing = pltpu.make_async_copy(forcing_ref, b_one, load_sem.at[1])
    load_state.start()
    load_forcing.start()
    tables = [
        pltpu.make_async_copy(far, near, table_sem.at[i])
        for i, (far, near) in enumerate(
            (
                (far_omega, omega_ref),
                (far_qt, qt_ref),
                (far_st, st_ref),
                (far_inv, inv_ref),
                (far_fwd, fwd_ref),
            )
        )
    ]
    for table in tables:
        table.start()
    pl.semaphore_wait(barrier, ring - 1)

    def owner(i):
        return device_of(plane * nf + i, nf, planes)

    def holder(i):
        return i, part

    def is_me(device):
        return (device[0] == me) & (device[1] == plane)

    def exchange(k, source, landing, target, origin, pick, mine, size, first):
        def rows_of(ref, i):
            return ref.at[pl.ds(pl.multiple_of(i * size, 8), size), :]

        def copy(i):
            return pltpu.make_async_remote_copy(
                src_ref=rows_of(source, pick(i)),
                dst_ref=rows_of(landing, mine),
                send_sem=send_sem.at[k, i],
                recv_sem=recv_sem.at[k, mine],
                device_id=named(target(i)),
                device_id_type=MESH,
            )

        def arrival(i):
            return pltpu.make_async_remote_copy(
                src_ref=rows_of(landing, i),
                dst_ref=rows_of(landing, i),
                send_sem=send_sem.at[k, i],
                recv_sem=recv_sem.at[k, i],
                device_id=named(origin(i)),
                device_id_type=MESH,
            )

        def own(i):
            return pltpu.make_async_copy(
                rows_of(source, pick(i)), rows_of(landing, mine), own_sem.at[k]
            )

        @pl.loop(0, nf)
        def _(d):
            i = (d + me) % nf
            stays = is_me(target(i))

            @pl.when(stays)
            def _():
                if first:
                    own(i).start()
                else:
                    own(i).wait()

            @pl.when(jnp.logical_not(stays))
            def _():
                if first:
                    copy(i).start()
                else:
                    copy(i).wait_send()

            if not first:

                @pl.when(jnp.logical_not(is_me(origin(i))))
                def _():
                    arrival(i).wait_recv()

    def same(i):
        return i

    base_args = (1, s_base, r_base, owner, holder, same, me, base_rows)
    state_args = (0, s_state, r_state, owner, holder, same, me, rows)
    w_args = (2, s_w, r_w, holder, owner, lambda i: 0, block, w_rows)
    out_state_args = (3, o_state, g_state, holder, owner, same, block, rows)
    out_forcing_args = (4, o_forcing, g_forcing, holder, owner, same, block, rows)
    exchange(*base_args, True)

    def halo_copies(e):
        slot = e % 2
        return (
            pltpu.make_async_remote_copy(
                src_ref=x_ref.at[slot, own_az],
                dst_ref=x_ref.at[slot, 0],
                send_sem=halo_send.at[0, e],
                recv_sem=halo_recv.at[0, e],
                device_id=right_id,
                device_id_type=MESH,
            ),
            pltpu.make_async_remote_copy(
                src_ref=x_ref.at[slot, 1],
                dst_ref=x_ref.at[slot, own_az + 1],
                send_sem=halo_send.at[1, e],
                recv_sem=halo_recv.at[1, e],
                device_id=left_id,
                device_id_type=MESH,
            ),
        )

    def place(a, c, v, kk):
        return ((c * variables + v) * per_dev + kk) * nf

    def packed_row(a, c, v, kk):
        return ((c * per_dev + kk) * variables + v) * own_az + a

    def each_run(visit):
        @pl.loop(0, own_az)
        def _(a):
            for c in range(2):
                for v in range(variables):
                    for kk in range(per_dev):
                        visit(a, place(a, c, v, kk), packed_row(a, c, v, kk))

    def in_row(a, c, v, kk):
        return ((c * per_dev + kk) * variables + v) * own_az + a

    def edge_copies(e):
        return [
            pltpu.make_async_remote_copy(
                src_ref=edge_out.at[e, side],
                dst_ref=edge_in.at[e, side],
                send_sem=edge_send.at[side, e],
                recv_sem=edge_recv.at[side, e],
                device_id=target,
                device_id_type=MESH,
            )
            for side, target in ((0, beyond), (1, behind))
        ]

    def send_edges(slot, e):
        for m in range(runs):
            edge_out[e, 0, pl.ds(m, 1), :] = x_one[slot, m, pl.ds(7 + span, 1), :]
            edge_out[e, 1, pl.ds(m, 1), :] = x_one[slot, m, pl.ds(8, 1), :]
        for copy in edge_copies(e):
            copy.start()

    for table in tables:
        table.wait()
    load_state.wait()
    send_edges(0, 0)
    load_forcing.wait()

    @pl.loop(0, runs)
    def _(m):
        b_one[m] = MARCH_WEIGHT * x_one[0, m, pl.ds(8, span), :] + b_one[m]

    exchange(*base_args, False)
    for station in range(STEPS):
        wanted = station_ref[station]

        @pl.loop(0, own_az)
        def _(a):
            for v in range(variables):
                scaled = (BASE_SCALE * shape_ref[a]) * r_base[
                    pl.ds(
                        (wanted // stored) * base_rows
                        + ((wanted % stored) * variables + v) * own_az
                        + a,
                        1,
                    ),
                    :,
                ]
                if station == 0:
                    s_w[pl.ds(v * own_az + a, 1), :] = scaled
                else:
                    w_ref[(station - 1) * own_az + a, pl.ds(v, 1), :] = scaled

        if station == 0:
            exchange(*w_args, True)
    exchange(*w_args, False)

    @pl.loop(0, nf)
    def _(j):
        for v in range(variables):
            plane_w[v, pl.ds(j * own_az, own_az), :] = r_w[pl.ds(j * w_rows + v * own_az, own_az), :]

    @pl.loop(0, SWEEPS)
    def _(e):
        src, dst = e % 2, (e + 1) % 2
        for copy in edge_copies(e):
            copy.wait()
        for m in range(runs):
            x_one[src, m, pl.ds(7, 1), :] = edge_in[e, 0, pl.ds(m, 1), :]
            x_one[src, m, pl.ds(8 + span, 1), :] = edge_in[e, 1, pl.ds(m, 1), :]
        for kk in range(per_dev):
            rate = rate_ref[kk]

            @pl.loop(0, variables)
            def _(v):
                w = plane_w[v]
                at = [(c * per_dev + kk) * variables + v for c in range(2)]
                real, imag = [x_one[src, m, pl.ds(8, span), :] for m in at]
                mixing = (w * real - rate * imag, w * imag + rate * real)
                summed = [
                    SIDE_WEIGHT
                    * (x_one[src, m, pl.ds(7, span), :] + x_one[src, m, pl.ds(9, span), :])
                    + b_one[m]
                    - mixed
                    for m, mixed in zip(at, mixing)
                ]
                q = times_right(jnp.concatenate(summed, axis=0), qt_ref[...])
                x_one[dst, at[0], pl.ds(8, span), :] = q[:span]
                x_one[dst, at[1], pl.ds(8, span), :] = q[span:]

        @pl.when(e < SWEEPS - 1)
        def _():
            send_edges(dst, e + 1)

    settled = SWEEPS % 2

    @pl.loop(0, nf)
    def _(j):
        for m in range(runs):
            s_state[pl.ds(j * rows + m * own_az, own_az), :] = x_one[
                settled, m, pl.ds(8 + j * own_az, own_az), :
            ]

    exchange(*state_args, True)
    exchange(*state_args, False)

    def unpack_state(a, start, row):
        x_ref[0, a + 1, pl.ds(start, nf), :] = r_state[pl.ds(row, nf, stride=rows), :]

    each_run(unpack_state)
    for copy in halo_copies(0):
        copy.start()
    omega = omega_ref[...][None]
    flat = (2 * half, radii)
    cube = (variables, freqs, radii)

    def sweep_slab(src, dst, a, station):
        x = x_ref[src, a + 1]
        beside = SIDE_WEIGHT * (x_ref[src, a] + x_ref[src, a + 2]) + b_ref[a]
        real, imag = x[:half].reshape(cube), x[half:].reshape(cube)
        w = w_ref[(station - 1) * own_az + a][:variables][:, None, :]
        mixing = jnp.concatenate([w * real - omega * imag, w * imag + omega * real], axis=0)
        summed = beside - mixing.reshape(flat)
        x_ref[dst, a + 1] = times_right(summed, qt_ref[...])

    def advect_slab(slot, a, final):
        x = x_ref[slot, a + 1]
        beside = 0.5 * (x_ref[slot, a + 2] - x_ref[slot, a])

        def lanes(y):
            return [
                jnp.concatenate(
                    [
                        y[v * freqs : (v + 1) * freqs],
                        y[half + v * freqs : half + (v + 1) * freqs],
                    ],
                    axis=0,
                )
                for v in range(variables)
            ]

        both = jnp.concatenate(lanes(x) + lanes(beside), axis=1)
        in_time = times_left(inv_ref[...], both)
        u = [in_time[:, v * radii : (v + 1) * radii] for v in range(variables)]
        ua = [
            in_time[:, (variables + v) * radii : (variables + v + 1) * radii]
            for v in range(variables)
        ]
        radial = times_right(jnp.concatenate(u, axis=0), st_ref[...])
        ur = [radial[v * ntime : (v + 1) * ntime] for v in range(variables)]
        n = [u[1] * ur[v] + u[2] * ua[v] for v in range(variables)]
        n[0] = n[0] + u[0] * (ur[1] + ua[2])
        source = -ADVECT_SCALE * jnp.concatenate(n, axis=1)
        spectral = times_left(fwd_ref[...], source)
        forcing = jnp.concatenate(
            [
                spectral[c * freqs : (c + 1) * freqs, v * radii : (v + 1) * radii]
                for c in range(2)
                for v in range(variables)
            ],
            axis=0,
        )
        if final:
            f_ref[a] = forcing
        else:
            b_ref[a] = MARCH_WEIGHT * x + forcing

    def advect_all(slot, e, final):
        @pl.loop(1, own_az - 1)
        def _(a):
            advect_slab(slot, a, final)

        for copy in halo_copies(e):
            copy.wait()
        advect_slab(slot, 0, final)
        if own_az > 1:
            advect_slab(slot, own_az - 1, final)

    advect_all(0, 0, False)
    for station in range(1, STEPS):

        @pl.loop(0, SWEEPS)
        def _(sweep):
            e = (station - 1) * SWEEPS + sweep
            src, dst = e % 2, (e + 1) % 2

            @pl.when(sweep > 0)
            def _():
                for copy in halo_copies(e):
                    copy.wait()

            sweep_slab(src, dst, 0, station)
            if own_az > 1:
                sweep_slab(src, dst, own_az - 1, station)
            for copy in halo_copies(e + 1):
                copy.start()

            @pl.loop(1, own_az - 1)
            def _(a):
                sweep_slab(src, dst, a, station)

        last = station * SWEEPS
        slot = last % 2
        final = station == STEPS - 1
        if final:

            def pack_state(a, start, row):
                o_state[pl.ds(row, nf, stride=rows), :] = x_ref[slot, a + 1, pl.ds(start, nf), :]

            each_run(pack_state)
            exchange(*out_state_args, True)

        advect_all(slot, last, final)

    def pack_forcing(a, start, row):
        o_forcing[pl.ds(row, nf, stride=rows), :] = f_ref[a, pl.ds(start, nf), :]

    each_run(pack_forcing)
    exchange(*out_forcing_args, True)
    exchange(*out_state_args, False)
    exchange(*out_forcing_args, False)


def per_device(state_in, forcing_in, base_flow, station_index, lobe_count):
    _, per_dev, variables, span_az, radii = state_in.shape
    nf = lax.axis_size("freq")
    planes = lax.axis_size("plane")
    freqs = per_dev * nf
    ntime = 3 * freqs // 2
    own_az = span_az // nf
    stored = base_flow.shape[0]
    slopes, inverse_p = radial_tables(radii)
    mode_ids = (np.arange(nf)[None, :] * per_dev + np.arange(per_dev)[:, None]).reshape(-1)
    inverse, forward = transform_tables(mode_ids, freqs, ntime)
    omegas = np.broadcast_to((0.5 * mode_ids / freqs).astype(np.float32)[:, None], (freqs, radii))
    plane = lax.axis_index("plane")
    here = ring_of(lax.axis_index("freq"), plane, nf, planes)
    shape_az = chevron(lobe_count, own_az, here * own_az, span_az * planes)

    def padded_rows(count):
        return -(-count // 8) * 8

    def chunks(x, size):
        x = x.reshape(-1, nf, own_az, radii).transpose(1, 0, 2, 3).reshape(nf, -1, radii)
        x = jnp.pad(x, ((0, 0), (0, size - x.shape[1]), (0, 0)))
        return x.reshape(nf * size, radii)

    count = 2 * per_dev * variables * own_az
    rows = padded_rows(count)
    base_rows = padded_rows(stored * variables * own_az)
    w_rows = padded_rows(variables * own_az)
    dims = (nf, planes, own_az, variables, per_dev, radii, stored, rows, base_rows, w_rows)
    half = variables * freqs
    exchanges = (STEPS - 1) * SWEEPS + 1
    runs = 2 * per_dev * variables
    edge_rows = padded_rows(runs)
    first_mode = lax.axis_index("freq") * per_dev
    rates = 0.5 * (first_mode + jnp.arange(per_dev)).astype(jnp.float32) / freqs
    smem = pl.BlockSpec(memory_space=pltpu.SMEM)
    anywhere = pl.BlockSpec(memory_space=pl.ANY)
    packed = (nf * rows, radii)
    f32 = jnp.float32
    outs = pl.pallas_call(
        functools.partial(march, dims),
        out_shape=[jax.ShapeDtypeStruct(packed, f32)] * 2,
        in_specs=[smem, smem, smem, anywhere, anywhere, anywhere] + [anywhere] * 5,
        out_specs=[anywhere, anywhere],
        scratch_shapes=[
            pltpu.VMEM(packed, f32),
            pltpu.VMEM((nf * base_rows, radii), f32),
            pltpu.VMEM(packed, f32),
            pltpu.VMEM((w_rows, radii), f32),
            pltpu.VMEM((nf * w_rows, radii), f32),
            pltpu.VMEM((variables, span_az, radii), f32),
            pltpu.VMEM((2, runs, span_az + 16, radii), f32),
            pltpu.VMEM((runs, span_az, radii), f32),
            pltpu.VMEM((SWEEPS, 2, edge_rows, radii), f32),
            pltpu.VMEM((SWEEPS, 2, edge_rows, radii), f32),
            pltpu.VMEM((2, own_az + 2, 2 * half, radii), f32),
            pltpu.VMEM((own_az, 2 * half, radii), f32),
            pltpu.VMEM((own_az, 2 * half, radii), f32),
            pltpu.VMEM(((STEPS - 1) * own_az, padded_rows(variables), radii), f32),
            pltpu.VMEM(packed, f32),
            pltpu.VMEM(packed, f32),
            pltpu.SemaphoreType.DMA((5, nf)),
            pltpu.SemaphoreType.DMA((5, nf)),
            pltpu.SemaphoreType.DMA((5,)),
            pltpu.SemaphoreType.DMA((2, exchanges)),
            pltpu.SemaphoreType.DMA((2, exchanges)),
            pltpu.SemaphoreType.DMA((2, SWEEPS)),
            pltpu.SemaphoreType.DMA((2, SWEEPS)),
            pltpu.SemaphoreType.DMA((2,)),
            pltpu.VMEM((freqs, radii), f32),
            pltpu.VMEM((2 * radii, 2 * radii), jnp.bfloat16),
            pltpu.VMEM((2 * radii, 2 * radii), jnp.bfloat16),
            pltpu.VMEM((ntime, 8 * freqs), jnp.bfloat16),
            pltpu.VMEM((2 * freqs, 4 * ntime), jnp.bfloat16),
            pltpu.SemaphoreType.DMA((5,)),
        ],
        compiler_params=pltpu.CompilerParams(
            collective_id=0, has_side_effects=True, vmem_limit_bytes=63_000 * 1024
        ),
    )(
        station_index,
        shape_az,
        rates,
        state_in.reshape(runs, span_az, radii),
        chunks(base_flow, base_rows),
        forcing_in.reshape(runs, span_az, radii),
        jnp.asarray(omegas),
        right_table(inverse_p.T),
        right_table(slopes.T),
        left_table(inverse.transpose(2, 0, 1).reshape(ntime, 2 * freqs)),
        left_table(forward.reshape(2 * freqs, ntime)),
    )

    return tuple(finish(y, nf, per_dev, variables, own_az, radii, rows, count) for y in outs)


def finish(y, nf, per_dev, variables, own_az, radii, rows, count):
    y = y.reshape(nf, rows, radii)[:, :count].reshape(nf, -1, own_az, radii)
    return y.transpose(1, 0, 2, 3).reshape(2, per_dev, variables, nf * own_az, radii)


def stacked_table(table):
    high, low = np_halves(table)
    return jnp.asarray(np.tile(np.concatenate([high, low], axis=0), (1, 2)))


def times_stacked(table, x):
    height = table.shape[0] // 2
    y = jnp.dot(table, jnp.concatenate(halves(x), axis=0), preferred_element_type=jnp.float32)
    return y[:height] + y[height:]


def relay(
    dims,
    lobe_ref,
    far_station,
    state_ref,
    base_ref,
    forcing_ref,
    far_qt,
    far_st,
    far_inv,
    far_fwd,
    g_state,
    g_forcing,
    r_state,
    r_base,
    s_w,
    plane_w,
    x_one,
    b_one,
    edge_out,
    edge_in,
    x_ref,
    b_ref,
    w_ref,
    o_state,
    o_march,
    o_forcing,
    send_sem,
    recv_sem,
    own_sem,
    halo_send,
    halo_recv,
    edge_send,
    edge_recv,
    load_sem,
    omega_ref,
    qt_ref,
    st_ref,
    inv_ref,
    fwd_ref,
    table_sem,
    station_ref,
):
    nf, planes, own_az, variables, per_dev, radii, stored = dims
    freqs = nf * per_dev
    span = nf * own_az
    parts = 2 * per_dev
    ntime = inv_ref.shape[0] // 2
    pair = 2 * freqs
    me = lax.axis_index("freq")
    plane = lax.axis_index("plane")
    ring = nf * planes
    here = ring_of(me, plane, nf, planes)
    part, block = here // nf, here % nf

    def named(device):
        return {"freq": device[0], "plane": device[1]}

    def is_me(device):
        return (device[0] == me) & (device[1] == plane)

    right_id = named(device_of((here + 1) % ring, nf, planes))
    left_id = named(device_of((here + ring - 1) % ring, nf, planes))
    barrier = pltpu.get_barrier_semaphore()

    def greet(device):
        pl.semaphore_signal(barrier, inc=1, device_id=device, device_id_type=MESH)

    @pl.loop(0, nf)
    def _(d):
        i = (me + nf // 2 + d) % nf

        @pl.when(jnp.logical_not(is_me((i, part))))
        def _():
            greet(named((i, part)))

    beyond = {"freq": me, "plane": (plane + 1) % planes}
    behind = {"freq": me, "plane": (plane + planes - 1) % planes}
    for device in (beyond, right_id, left_id):
        greet(device)
    load_state = pltpu.make_async_copy(
        state_ref, x_one.at[0, :, :, pl.ds(8, span), :], load_sem.at[0]
    )
    load_forcing = pltpu.make_async_copy(forcing_ref, b_one, load_sem.at[1])
    load_state.start()
    load_forcing.start()
    tables = [
        pltpu.make_async_copy(far, near, table_sem.at[i])
        for i, (far, near) in enumerate(
            (
                (far_station, station_ref),
                (far_qt, qt_ref),
                (far_st, st_ref),
                (far_inv, inv_ref),
                (far_fwd, fwd_ref),
            )
        )
    ]
    for table in tables:
        table.start()
    pl.semaphore_wait(barrier, nf + 3 - (part == plane).astype(jnp.int32))

    def owner(i):
        return device_of(plane * nf + i, nf, planes)

    def holder(i):
        return i, part

    def azimuths(i):
        return pl.ds(pl.multiple_of(i * own_az, 8), own_az)

    def mixed(d):
        return d

    def exchange(k, piece, landing, target, origin, mine):
        def copy(i):
            return pltpu.make_async_remote_copy(
                src_ref=piece(i),
                dst_ref=landing(mine),
                send_sem=send_sem.at[k, i],
                recv_sem=recv_sem.at[k, mine],
                device_id=named(target(i)),
                device_id_type=MESH,
            )

        def arrival(i):
            return pltpu.make_async_remote_copy(
                src_ref=landing(i),
                dst_ref=landing(i),
                send_sem=send_sem.at[k, i],
                recv_sem=recv_sem.at[k, i],
                device_id=named(origin(i)),
                device_id_type=MESH,
            )

        def own(i):
            return pltpu.make_async_copy(piece(i), landing(mine), own_sem.at[k])

        def start(first=0, stop=nf):
            @pl.loop(first, stop)
            def _(d):
                i = (mixed(d) + me) % nf
                stays = is_me(target(i))

                @pl.when(stays)
                def _():
                    own(i).start()

                @pl.when(jnp.logical_not(stays))
                def _():
                    copy(i).start()

        def wait():
            @pl.loop(0, nf)
            def _(d):
                i = (d + me) % nf
                stays = is_me(target(i))

                @pl.when(stays)
                def _():
                    own(i).wait()

                @pl.when(jnp.logical_not(stays))
                def _():
                    copy(i).wait_send()

                @pl.when(jnp.logical_not(is_me(origin(i))))
                def _():
                    arrival(i).wait_recv()

        return start, wait

    base_start, base_wait = exchange(
        0,
        lambda i: base_ref.at[:, :, azimuths(i), :],
        lambda j: r_base.at[j],
        owner,
        holder,
        me,
    )
    groups = [(v, min(v + GROUP, variables)) for v in range(0, variables, GROUP)]

    def w_moves(g):
        first, stop = groups[g]
        return exchange(
            1 + g,
            lambda i: s_w.at[0, pl.ds(first, stop - first)],
            lambda j: plane_w.at[0, pl.ds(first, stop - first), azimuths(j), :],
            holder,
            owner,
            block,
        )

    later_start, later_wait = exchange(
        2 + 3 * variables,
        lambda i: s_w.at[1, pl.ds(0, RETURNED)],
        lambda j: plane_w.at[1, pl.ds(0, RETURNED), azimuths(j), :],
        holder,
        owner,
        block,
    )

    def march_moves(v):
        return exchange(
            3 + 3 * variables + v,
            lambda i: o_march.at[i, v],
            lambda j: b_one.at[:, v, azimuths(j), :],
            holder,
            owner,
            block,
        )

    settled = SWEEPS % 2

    def state_moves(v):
        return exchange(
            1 + variables + v,
            lambda i: x_one.at[
                settled, :, v, pl.ds(pl.multiple_of(8 + i * own_az, 8), own_az), :
            ],
            lambda j: r_state.at[j, v],
            owner,
            holder,
            me,
        )

    def out_moves(v):
        return exchange(
            1 + 2 * variables + v,
            lambda i: o_state.at[i, v],
            lambda j: g_state.at[:, v, azimuths(j), :],
            holder,
            owner,
            block,
        )

    forcing_start, forcing_wait = exchange(
        1 + 3 * variables,
        lambda i: o_forcing.at[i],
        lambda j: g_forcing.at[:, :, azimuths(j), :],
        holder,
        owner,
        block,
    )
    base_start()

    def halo_copies(e, v):
        slot = e % 2
        rows = pl.ds(pl.multiple_of(v * pair, 8), pair)
        return [
            pltpu.make_async_remote_copy(
                src_ref=x_ref.at[slot, source, rows, :],
                dst_ref=x_ref.at[slot, target, rows, :],
                send_sem=halo_send.at[side, e, v],
                recv_sem=halo_recv.at[side, e, v],
                device_id=device,
                device_id_type=MESH,
            )
            for side, source, target, device in (
                (0, own_az, 0, right_id),
                (1, 1, own_az + 1, left_id),
            )
        ]

    def edge_copies(e, v):
        return [
            pltpu.make_async_remote_copy(
                src_ref=edge_out.at[e, v, side],
                dst_ref=edge_in.at[e, v, side],
                send_sem=edge_send.at[side, e, v],
                recv_sem=edge_recv.at[side, e, v],
                device_id=target,
                device_id_type=MESH,
            )
            for side, target in ((0, beyond), (1, behind))
        ]

    def send_edges(slot, e, v):
        for ck in range(parts):
            edge_out[e, v, 0, pl.ds(ck, 1), :] = x_one[slot, ck, v, pl.ds(7 + span, 1), :]
            edge_out[e, v, 1, pl.ds(ck, 1), :] = x_one[slot, ck, v, pl.ds(8, 1), :]
        for copy in edge_copies(e, v):
            copy.start()

    for kk in range(per_dev):
        modes = lax.broadcasted_iota(jnp.int32, (nf, radii), 0) * per_dev + kk
        omega_ref[pl.ds(kk * nf, nf), :] = 0.5 * modes.astype(jnp.float32) / freqs
    load_state.wait()

    @pl.loop(0, variables)
    def _(v):
        send_edges(0, 0, v)

    load_forcing.wait()

    @pl.loop(0, variables)
    def _(v):
        for ck in range(parts):
            b_one[ck, v] = MARCH_WEIGHT * x_one[0, ck, v, pl.ds(8, span), :] + b_one[ck, v]

    for table in tables:
        table.wait()
    position = here * own_az + lax.broadcasted_iota(jnp.int32, (own_az, radii), 0)
    phases = (lobe_ref[0] * position) % (span * planes)
    shape = 1.0 + 0.5 * jnp.cos(2.0 * math.pi * phases.astype(jnp.float32) / (span * planes))
    base_wait()

    def coefficient(station, v):
        wanted = station_ref[station]
        return (BASE_SCALE * shape) * r_base[wanted // stored, wanted % stored, v]

    for g, (first, stop) in enumerate(groups):
        for v in range(first, stop):
            s_w[0, v] = coefficient(0, v)
        w_moves(g)[0]()
    for v in range(variables):
        w_ref[v] = coefficient(1, v)
        if v < RETURNED:
            s_w[1, v] = coefficient(1, v)
    later_start()

    def sweep_plane(e, v, w):
        src, dst = e % 2, (e + 1) % 2
        for copy in edge_copies(e, v):
            copy.wait()
        for ck in range(parts):
            x_one[src, ck, v, pl.ds(7, 1), :] = edge_in[e, v, 0, pl.ds(ck, 1), :]
            x_one[src, ck, v, pl.ds(8 + span, 1), :] = edge_in[e, v, 1, pl.ds(ck, 1), :]
        for kk in range(per_dev):
            rate = (me * per_dev + kk).astype(jnp.float32) * (0.5 / freqs)
            at = [c * per_dev + kk for c in range(2)]
            real, imag = [x_one[src, ck, v, pl.ds(8, span), :] for ck in at]
            mixing = (w * real - rate * imag, w * imag + rate * real)
            summed = [
                SIDE_WEIGHT
                * (x_one[src, ck, v, pl.ds(7, span), :] + x_one[src, ck, v, pl.ds(9, span), :])
                + b_one[ck, v]
                - mixed_in
                for ck, mixed_in in zip(at, mixing)
            ]
            q = times_right(jnp.concatenate(summed, axis=0), qt_ref[...])
            x_one[dst, at[0], v, pl.ds(8, span), :] = q[:span]
            x_one[dst, at[1], v, pl.ds(8, span), :] = q[span:]

    for g, (first, stop) in enumerate(groups):
        w_moves(g)[1]()

        @pl.loop(0, SWEEPS * (stop - first))
        def _(turn):
            e, v = turn // (stop - first), first + turn % (stop - first)
            sweep_plane(e, v, plane_w[0, v])

            @pl.when((e < SWEEPS - 1) | (v < RETURNED))
            def _():
                send_edges((e + 1) % 2, e + 1, v)

            @pl.when(e == SWEEPS - 1)
            def _():
                state_moves(v)[0]()

    def each_run(v, visit):
        for c in range(2):
            for kk in range(per_dev):
                start = pl.multiple_of(v * pair + (c * per_dev + kk) * nf, 8)
                visit(start, c * per_dev + kk)

    @pl.loop(0, variables)
    def _(v):
        state_moves(v)[1]()

        @pl.loop(0, own_az)
        def _(a):
            def unpack(start, ck):
                x_ref[0, a + 1, pl.ds(start, nf), :] = r_state[:, v, ck, a, :]

            each_run(v, unpack)

        for copy in halo_copies(0, v):
            copy.start()

    omega = omega_ref[...]

    def sweep_slabs(e, v):
        src, dst = e % 2, (e + 1) % 2
        rows = pl.ds(pl.multiple_of(v * pair, 8), pair)
        w = w_ref[v]
        summed = []
        for a in range(own_az):
            x = x_ref[src, a + 1, rows, :]
            beside = SIDE_WEIGHT * (x_ref[src, a, rows, :] + x_ref[src, a + 2, rows, :])
            real, imag = x[:freqs], x[freqs:]
            here_w = w[a : a + 1]
            mixing = [here_w * real - omega * imag, here_w * imag + omega * real]
            summed.append(beside + b_ref[a, rows, :] - jnp.concatenate(mixing, axis=0))
        q = times_right(jnp.concatenate(summed, axis=0), qt_ref[...])
        for a in range(own_az):
            x_ref[dst, a + 1, rows, :] = q[a * pair : (a + 1) * pair]

    def advect_slab(slot, a, final):
        x = x_ref[slot, a + 1]
        beside = 0.5 * (x_ref[slot, a + 2] - x_ref[slot, a])

        def lanes(y):
            return [y[v * pair : (v + 1) * pair] for v in range(variables)]

        both = jnp.concatenate(lanes(x) + lanes(beside), axis=1)
        in_time = times_stacked(inv_ref[...], both)
        u = [in_time[:, v * radii : (v + 1) * radii] for v in range(variables)]
        ua = [
            in_time[:, (variables + v) * radii : (variables + v + 1) * radii]
            for v in range(variables)
        ]
        radial = times_right(jnp.concatenate(u, axis=0), st_ref[...])
        ur = [radial[v * ntime : (v + 1) * ntime] for v in range(variables)]
        n = [u[1] * ur[v] + u[2] * ua[v] for v in range(variables)]
        n[0] = n[0] + u[0] * (ur[1] + ua[2])
        source = -ADVECT_SCALE * jnp.concatenate(n, axis=1)
        spectral = times_stacked(fwd_ref[...], source)
        for v in range(variables):
            forcing = spectral[:, v * radii : (v + 1) * radii]
            if final:
                for ck in range(parts):
                    o_forcing[:, ck, v, a, :] = forcing[ck * nf : (ck + 1) * nf]
            else:
                march = MARCH_WEIGHT * x[v * pair : (v + 1) * pair] + forcing
                b_ref[a, pl.ds(v * pair, pair), :] = march
                if v < RETURNED:
                    for ck in range(parts):
                        o_march[:, v, ck, a, :] = march[ck * nf : (ck + 1) * nf]

    def advect_all(e, final):
        slot = e % 2

        @pl.loop(1, own_az - 1)
        def _(a):
            advect_slab(slot, a, final)

        @pl.loop(0, variables)
        def _(v):
            for copy in halo_copies(e, v):
                copy.wait()

        @pl.loop(0, 2)
        def _(side):
            advect_slab(slot, side * (own_az - 1), final)

    advect_all(0, False)

    @pl.loop(0, SWEEPS * variables)
    def _(turn):
        e, v = turn // variables, turn % variables

        @pl.when(e > 0)
        def _():
            for copy in halo_copies(e, v):
                copy.wait()

        sweep_slabs(e, v)
        for copy in halo_copies(e + 1, v):
            copy.start()

        @pl.when(turn < nf)
        def _():
            for w in range(RETURNED):
                march_moves(w)[0](turn, turn + 1)

        @pl.when((e == SWEEPS - 1) & (v >= RETURNED))
        def _():
            @pl.loop(0, own_az)
            def _(a):
                def pack(start, ck):
                    o_state[:, v, ck, a, :] = x_ref[settled, a + 1, pl.ds(start, nf), :]

                each_run(v, pack)

            out_moves(v)[0]()

    advect_all(SWEEPS, True)
    forcing_start()
    later_wait()
    for v in range(RETURNED):
        march_moves(v)[1]()

    @pl.loop(0, SWEEPS * RETURNED)
    def _(turn):
        e, v = SWEEPS + turn // RETURNED, turn % RETURNED
        sweep_plane(e, v, plane_w[1, v])

        @pl.when(e < 2 * SWEEPS - 1)
        def _():
            send_edges((e + 1) % 2, e + 1, v)

    out_state = pltpu.make_async_copy(
        x_one.at[0, :, pl.ds(0, RETURNED), pl.ds(8, span), :],
        g_state.at[:, pl.ds(0, RETURNED), :, :],
        load_sem.at[0],
    )
    out_state.start()

    @pl.loop(RETURNED, variables)
    def _(v):
        out_moves(v)[1]()

    out_state.wait()

    forcing_wait()


GROUP = 1
RETURNED = 1


def per_device_tiled(state_in, forcing_in, base_flow, station_index, lobe_count):
    _, per_dev, variables, span_az, radii = state_in.shape
    nf = lax.axis_size("freq")
    planes = lax.axis_size("plane")
    freqs = per_dev * nf
    ntime = 3 * freqs // 2
    own_az = span_az // nf
    stored = base_flow.shape[0]
    slopes, inverse_p = radial_tables(radii)
    mode_ids = (np.arange(nf)[None, :] * per_dev + np.arange(per_dev)[:, None]).reshape(-1)
    inverse, forward = transform_tables(mode_ids, freqs, ntime)
    dims = (nf, planes, own_az, variables, per_dev, radii, stored)
    parts = 2 * per_dev
    edge_rows = -(-parts // 8) * 8
    anywhere = pl.BlockSpec(memory_space=pl.ANY)
    far = pl.BlockSpec(memory_space=pltpu.HBM)
    f32 = jnp.float32
    whole = (parts, variables, span_az, radii)
    slab = variables * 2 * freqs
    moves = 3 + 3 * variables + RETURNED
    rounds = 2 * SWEEPS
    outs = pl.pallas_call(
        functools.partial(relay, dims),
        out_shape=[jax.ShapeDtypeStruct(whole, f32)] * 2,
        in_specs=[pl.BlockSpec(memory_space=pltpu.SMEM)] + [far] * 8,
        out_specs=[anywhere, anywhere],
        scratch_shapes=[
            pltpu.VMEM((nf, variables, parts, own_az, radii), f32),
            pltpu.VMEM((nf, stored, variables, own_az, radii), f32),
            pltpu.VMEM((2, variables, own_az, radii), f32),
            pltpu.VMEM((2, variables, span_az, radii), f32),
            pltpu.VMEM((2, parts, variables, span_az + 16, radii), f32),
            pltpu.VMEM(whole, f32),
            pltpu.VMEM((rounds, variables, 2, edge_rows, radii), f32),
            pltpu.VMEM((rounds, variables, 2, edge_rows, radii), f32),
            pltpu.VMEM((2, own_az + 2, slab, radii), f32),
            pltpu.VMEM((own_az, slab, radii), f32),
            pltpu.VMEM((variables, own_az, radii), f32),
            pltpu.VMEM((nf, variables, parts, own_az, radii), f32),
            pltpu.VMEM((nf, RETURNED, parts, own_az, radii), f32),
            pltpu.VMEM((nf, parts, variables, own_az, radii), f32),
            pltpu.SemaphoreType.DMA((moves, nf)),
            pltpu.SemaphoreType.DMA((moves, nf)),
            pltpu.SemaphoreType.DMA((moves,)),
            pltpu.SemaphoreType.DMA((2, SWEEPS + 1, variables)),
            pltpu.SemaphoreType.DMA((2, SWEEPS + 1, variables)),
            pltpu.SemaphoreType.DMA((2, rounds, variables)),
            pltpu.SemaphoreType.DMA((2, rounds, variables)),
            pltpu.SemaphoreType.DMA((2,)),
            pltpu.VMEM((freqs, radii), f32),
            pltpu.VMEM((2 * radii, 2 * radii), jnp.bfloat16),
            pltpu.VMEM((2 * radii, 2 * radii), jnp.bfloat16),
            pltpu.VMEM((2 * ntime, 4 * freqs), jnp.bfloat16),
            pltpu.VMEM((4 * freqs, 2 * ntime), jnp.bfloat16),
            pltpu.SemaphoreType.DMA((5,)),
            pltpu.SMEM(station_index.shape, jnp.int32),
        ],
        compiler_params=pltpu.CompilerParams(
            collective_id=0, has_side_effects=True, vmem_limit_bytes=32 * 1024 * 1024
        ),
    )(
        lobe_count,
        *[
            pltpu.with_memory_space_constraint(x, pltpu.HBM)
            for x in (
                station_index,
                state_in.reshape(whole),
                base_flow,
                forcing_in.reshape(whole),
                right_table(inverse_p.T),
                right_table(slopes.T),
                stacked_table(inverse.transpose(2, 0, 1).reshape(ntime, 2 * freqs)),
                stacked_table(forward.reshape(2 * freqs, ntime)),
            )
        ],
    )
    return tuple(y.reshape(state_in.shape) for y in outs)


def per_device_any(*args):
    tiles = args[0].shape[3] % (8 * lax.axis_size("freq")) == 0
    return (per_device_tiled if tiles else per_device)(*args)


MESH = pl.DeviceIdType.MESH


def solution(mesh):
    return jax.shard_map(
        per_device_any,
        mesh=mesh,
        in_specs=(
            P(None, "freq", None, "plane", None),
            P(None, "freq", None, "plane", None),
            P("freq", None, "plane", None),
            P(),
            P(),
        ),
        out_specs=(P(None, "freq", None, "plane", None), P(None, "freq", None, "plane", None)),
        check_vma=False,
    )
```

```python
import functools
import math

import jax
import jax.numpy as jnp
import numpy as np
from jax import lax
from jax.experimental import pallas as pl
from jax.experimental.pallas import tpu as pltpu
from jax.sharding import PartitionSpec as P

SWEEPS = 4
STEPS = 2


SIDE_WEIGHT = 1.25
MARCH_WEIGHT = 4.0
DIAG_SHIFT = 4.0
ADVECT_SCALE = 0.5
BASE_SCALE = 0.5


def radial_tables(radius_count):
    indices = np.arange(radius_count)
    angles = math.pi * indices / (radius_count - 1)
    nodes = np.cos(angles)
    weights = np.where((indices == 0) | (indices == radius_count - 1), 2.0, 1.0)
    parity = 1.0 - 2.0 * ((indices[:, None] + indices[None, :]) % 2)
    offdiag = indices[:, None] != indices[None, :]
    spacing = np.where(offdiag, nodes[:, None] - nodes[None, :], 1.0)
    entries = np.where(offdiag, weights[:, None] / weights[None, :] * parity / spacing, 0.0)
    entries = entries - np.diag(entries.sum(axis=1))
    slopes = np.sin(angles)[:, None] * entries / (radius_count - 1)
    system = slopes.T @ slopes + DIAG_SHIFT * np.eye(radius_count)
    return slopes.astype(np.float32), np.linalg.inv(system).astype(np.float32)


def transform_tables(mode_ids, freqs, ntime):
    time_ids = np.arange(ntime)
    angles = 2.0 * math.pi * (mode_ids[:, None] * time_ids[None, :] % ntime) / ntime
    stacked = np.stack([np.cos(angles), -np.sin(angles)])
    return (
        (stacked / math.sqrt(freqs)).astype(np.float32),
        (stacked / math.sqrt(ntime)).astype(np.float32),
    )


def chevron(lobe_count, azimuths, start_az, total_az):
    position = start_az + jnp.arange(azimuths)
    phases = lobe_count[0] * position % total_az
    return 1.0 + 0.5 * jnp.cos(2.0 * math.pi * phases.astype(jnp.float32) / total_az)


def halves(x):
    high = x.astype(jnp.bfloat16)
    return high, (x - high.astype(jnp.float32)).astype(jnp.bfloat16)


def right_table(table):
    high, low = np_halves(table)
    return jnp.asarray(np.tile(np.concatenate([high, low], axis=1), (2, 1)))


def left_table(table):
    high, low = np_halves(table)
    return jnp.asarray(np.concatenate([high, high, low, low], axis=1))


def np_halves(table):
    high = table.astype(jnp.bfloat16)
    return high, (table - high.astype(np.float32)).astype(jnp.bfloat16)


def times_right(x, table):
    width = table.shape[1] // 2
    y = jnp.dot(jnp.concatenate(halves(x), axis=1), table, preferred_element_type=jnp.float32)
    return y[:, :width] + y[:, width:]


def times_left(table, x):
    high, low = halves(x)
    return jnp.dot(
        table,
        jnp.concatenate([high, low, high, low], axis=0),
        preferred_element_type=jnp.float32,
    )


def ring_of(f, p, nf, planes):
    at = f
    if nf % 4 == 0:
        high = nf // 4
        z, y, x = f // 4, (f // 2) % 2, f % 2
        column = 2 * y + (x + y) % 2
        at = column * high + z + (column % 2) * (high - 1 - 2 * z)
    return at * planes + p


def device_of(g, nf, planes):
    at = g // planes
    f = at
    if nf % 4 == 0:
        high = nf // 4
        column, z = at // high, at % high
        z = z + (column % 2) * (high - 1 - 2 * z)
        y = column // 2
        f = 4 * z + 2 * y + (column + y) % 2
    return f, g % planes


def march(
    dims,
    station_ref,
    shape_ref,
    rate_ref,
    state_ref,
    s_base,
    forcing_ref,
    far_omega,
    far_qt,
    far_st,
    far_inv,
    far_fwd,
    g_state,
    g_forcing,
    r_state,
    r_base,
    s_state,
    s_w,
    r_w,
    plane_w,
    x_one,
    b_one,
    edge_out,
    edge_in,
    x_ref,
    b_ref,
    f_ref,
    w_ref,
    o_state,
    o_forcing,
    send_sem,
    recv_sem,
    own_sem,
    halo_send,
    halo_recv,
    edge_send,
    edge_recv,
    load_sem,
    omega_ref,
    qt_ref,
    st_ref,
    inv_ref,
    fwd_ref,
    table_sem,
):
    nf, planes, own_az, variables, per_dev, radii, stored, rows, base_rows, w_rows = dims
    freqs = nf * per_dev
    span = nf * own_az
    runs = 2 * per_dev * variables
    ntime = inv_ref.shape[0]
    half = variables * freqs
    me = lax.axis_index("freq")
    plane = lax.axis_index("plane")
    ring = nf * planes
    here = ring_of(me, plane, nf, planes)
    part, block = here // nf, here % nf

    def named(device):
        return {"freq": device[0], "plane": device[1]}

    right_id = named(device_of((here + 1) % ring, nf, planes))
    left_id = named(device_of((here + ring - 1) % ring, nf, planes))
    barrier = pltpu.get_barrier_semaphore()

    @pl.loop(1, ring)
    def _(d):
        other = (me * planes + plane + d) % ring
        pl.semaphore_signal(
            barrier,
            inc=1,
            device_id={"freq": other // planes, "plane": other % planes},
            device_id_type=MESH,
        )

    beyond = {"freq": me, "plane": (plane + 1) % planes}
    behind = {"freq": me, "plane": (plane + planes - 1) % planes}
    load_state = pltpu.make_async_copy(state_ref, x_one.at[0, :, pl.ds(8, span), :], load_sem.at[0])
    load_forcing = pltpu.make_async_copy(forcing_ref, b_one, load_sem.at[1])
    load_state.start()
    load_forcing.start()
    tables = [
        pltpu.make_async_copy(far, near, table_sem.at[i])
        for i, (far, near) in enumerate(
            (
                (far_omega, omega_ref),
                (far_qt, qt_ref),
                (far_st, st_ref),
                (far_inv, inv_ref),
                (far_fwd, fwd_ref),
            )
        )
    ]
    for table in tables:
        table.start()
    pl.semaphore_wait(barrier, ring - 1)

    def owner(i):
        return device_of(plane * nf + i, nf, planes)

    def holder(i):
        return i, part

    def is_me(device):
        return (device[0] == me) & (device[1] == plane)

    def exchange(k, source, landing, target, origin, pick, mine, size, first):
        def rows_of(ref, i):
            return ref.at[pl.ds(pl.multiple_of(i * size, 8), size), :]

        def copy(i):
            return pltpu.make_async_remote_copy(
                src_ref=rows_of(source, pick(i)),
                dst_ref=rows_of(landing, mine),
                send_sem=send_sem.at[k, i],
                recv_sem=recv_sem.at[k, mine],
                device_id=named(target(i)),
                device_id_type=MESH,
            )

        def arrival(i):
            return pltpu.make_async_remote_copy(
                src_ref=rows_of(landing, i),
                dst_ref=rows_of(landing, i),
                send_sem=send_sem.at[k, i],
                recv_sem=recv_sem.at[k, i],
                device_id=named(origin(i)),
                device_id_type=MESH,
            )

        def own(i):
            return pltpu.make_async_copy(
                rows_of(source, pick(i)), rows_of(landing, mine), own_sem.at[k]
            )

        @pl.loop(0, nf)
        def _(d):
            i = (d + me) % nf
            stays = is_me(target(i))

            @pl.when(stays)
            def _():
                if first:
                    own(i).start()
                else:
                    own(i).wait()

            @pl.when(jnp.logical_not(stays))
            def _():
                if first:
                    copy(i).start()
                else:
                    copy(i).wait_send()

            if not first:

                @pl.when(jnp.logical_not(is_me(origin(i))))
                def _():
                    arrival(i).wait_recv()

    def same(i):
        return i

    base_args = (1, s_base, r_base, owner, holder, same, me, base_rows)
    state_args = (0, s_state, r_state, owner, holder, same, me, rows)
    w_args = (2, s_w, r_w, holder, owner, lambda i: 0, block, w_rows)
    out_state_args = (3, o_state, g_state, holder, owner, same, block, rows)
    out_forcing_args = (4, o_forcing, g_forcing, holder, owner, same, block, rows)
    exchange(*base_args, True)

    def halo_copies(e):
        slot = e % 2
        return (
            pltpu.make_async_remote_copy(
                src_ref=x_ref.at[slot, own_az],
                dst_ref=x_ref.at[slot, 0],
                send_sem=halo_send.at[0, e],
                recv_sem=halo_recv.at[0, e],
                device_id=right_id,
                device_id_type=MESH,
            ),
            pltpu.make_async_remote_copy(
                src_ref=x_ref.at[slot, 1],
                dst_ref=x_ref.at[slot, own_az + 1],
                send_sem=halo_send.at[1, e],
                recv_sem=halo_recv.at[1, e],
                device_id=left_id,
                device_id_type=MESH,
            ),
        )

    def place(a, c, v, kk):
        return ((c * variables + v) * per_dev + kk) * nf

    def packed_row(a, c, v, kk):
        return ((c * per_dev + kk) * variables + v) * own_az + a

    def each_run(visit):
        @pl.loop(0, own_az)
        def _(a):
            for c in range(2):
                for v in range(variables):
                    for kk in range(per_dev):
                        visit(a, place(a, c, v, kk), packed_row(a, c, v, kk))

    def in_row(a, c, v, kk):
        return ((c * per_dev + kk) * variables + v) * own_az + a

    def edge_copies(e):
        return [
            pltpu.make_async_remote_copy(
                src_ref=edge_out.at[e, side],
                dst_ref=edge_in.at[e, side],
                send_sem=edge_send.at[side, e],
                recv_sem=edge_recv.at[side, e],
                device_id=target,
                device_id_type=MESH,
            )
            for side, target in ((0, beyond), (1, behind))
        ]

    def send_edges(slot, e):
        for m in range(runs):
            edge_out[e, 0, pl.ds(m, 1), :] = x_one[slot, m, pl.ds(7 + span, 1), :]
            edge_out[e, 1, pl.ds(m, 1), :] = x_one[slot, m, pl.ds(8, 1), :]
        for copy in edge_copies(e):
            copy.start()

    for table in tables:
        table.wait()
    load_state.wait()
    send_edges(0, 0)
    load_forcing.wait()

    @pl.loop(0, runs)
    def _(m):
        b_one[m] = MARCH_WEIGHT * x_one[0, m, pl.ds(8, span), :] + b_one[m]

    exchange(*base_args, False)
    for station in range(STEPS):
        wanted = station_ref[station]

        @pl.loop(0, own_az)
        def _(a):
            for v in range(variables):
                scaled = (BASE_SCALE * shape_ref[a]) * r_base[
                    pl.ds(
                        (wanted // stored) * base_rows
                        + ((wanted % stored) * variables + v) * own_az
                        + a,
                        1,
                    ),
                    :,
                ]
                if station == 0:
                    s_w[pl.ds(v * own_az + a, 1), :] = scaled
                else:
                    w_ref[(station - 1) * own_az + a, pl.ds(v, 1), :] = scaled

        if station == 0:
            exchange(*w_args, True)
    exchange(*w_args, False)

    @pl.loop(0, nf)
    def _(j):
        for v in range(variables):
            plane_w[v, pl.ds(j * own_az, own_az), :] = r_w[pl.ds(j * w_rows + v * own_az, own_az), :]

    @pl.loop(0, SWEEPS)
    def _(e):
        src, dst = e % 2, (e + 1) % 2
        for copy in edge_copies(e):
            copy.wait()
        for m in range(runs):
            x_one[src, m, pl.ds(7, 1), :] = edge_in[e, 0, pl.ds(m, 1), :]
            x_one[src, m, pl.ds(8 + span, 1), :] = edge_in[e, 1, pl.ds(m, 1), :]
        for kk in range(per_dev):
            rate = rate_ref[kk]

            @pl.loop(0, variables)
            def _(v):
                w = plane_w[v]
                at = [(c * per_dev + kk) * variables + v for c in range(2)]
                real, imag = [x_one[src, m, pl.ds(8, span), :] for m in at]
                mixing = (w * real - rate * imag, w * imag + rate * real)
                summed = [
                    SIDE_WEIGHT
                    * (x_one[src, m, pl.ds(7, span), :] + x_one[src, m, pl.ds(9, span), :])
                    + b_one[m]
                    - mixed
                    for m, mixed in zip(at, mixing)
                ]
                q = times_right(jnp.concatenate(summed, axis=0), qt_ref[...])
                x_one[dst, at[0], pl.ds(8, span), :] = q[:span]
                x_one[dst, at[1], pl.ds(8, span), :] = q[span:]

        @pl.when(e < SWEEPS - 1)
        def _():
            send_edges(dst, e + 1)

    settled = SWEEPS % 2

    @pl.loop(0, nf)
    def _(j):
        for m in range(runs):
            s_state[pl.ds(j * rows + m * own_az, own_az), :] = x_one[
                settled, m, pl.ds(8 + j * own_az, own_az), :
            ]

    exchange(*state_args, True)
    exchange(*state_args, False)

    def unpack_state(a, start, row):
        x_ref[0, a + 1, pl.ds(start, nf), :] = r_state[pl.ds(row, nf, stride=rows), :]

    each_run(unpack_state)
    for copy in halo_copies(0):
        copy.start()
    omega = omega_ref[...][None]
    flat = (2 * half, radii)
    cube = (variables, freqs, radii)

    def sweep_slab(src, dst, a, station):
        x = x_ref[src, a + 1]
        beside = SIDE_WEIGHT * (x_ref[src, a] + x_ref[src, a + 2]) + b_ref[a]
        real, imag = x[:half].reshape(cube), x[half:].reshape(cube)
        w = w_ref[(station - 1) * own_az + a][:variables][:, None, :]
        mixing = jnp.concatenate([w * real - omega * imag, w * imag + omega * real], axis=0)
        summed = beside - mixing.reshape(flat)
        x_ref[dst, a + 1] = times_right(summed, qt_ref[...])

    def advect_slab(slot, a, final):
        x = x_ref[slot, a + 1]
        beside = 0.5 * (x_ref[slot, a + 2] - x_ref[slot, a])

        def lanes(y):
            return [
                jnp.concatenate(
                    [
                        y[v * freqs : (v + 1) * freqs],
                        y[half + v * freqs : half + (v + 1) * freqs],
                    ],
                    axis=0,
                )
                for v in range(variables)
            ]

        both = jnp.concatenate(lanes(x) + lanes(beside), axis=1)
        in_time = times_left(inv_ref[...], both)
        u = [in_time[:, v * radii : (v + 1) * radii] for v in range(variables)]
        ua = [
            in_time[:, (variables + v) * radii : (variables + v + 1) * radii]
            for v in range(variables)
        ]
        radial = times_right(jnp.concatenate(u, axis=0), st_ref[...])
        ur = [radial[v * ntime : (v + 1) * ntime] for v in range(variables)]
        n = [u[1] * ur[v] + u[2] * ua[v] for v in range(variables)]
        n[0] = n[0] + u[0] * (ur[1] + ua[2])
        source = -ADVECT_SCALE * jnp.concatenate(n, axis=1)
        spectral = times_left(fwd_ref[...], source)
        forcing = jnp.concatenate(
            [
                spectral[c * freqs : (c + 1) * freqs, v * radii : (v + 1) * radii]
                for c in range(2)
                for v in range(variables)
            ],
            axis=0,
        )
        if final:
            f_ref[a] = forcing
        else:
            b_ref[a] = MARCH_WEIGHT * x + forcing

    def advect_all(slot, e, final):
        @pl.loop(1, own_az - 1)
        def _(a):
            advect_slab(slot, a, final)

        for copy in halo_copies(e):
            copy.wait()
        advect_slab(slot, 0, final)
        if own_az > 1:
            advect_slab(slot, own_az - 1, final)

    advect_all(0, 0, False)
    for station in range(1, STEPS):

        @pl.loop(0, SWEEPS)
        def _(sweep):
            e = (station - 1) * SWEEPS + sweep
            src, dst = e % 2, (e + 1) % 2

            @pl.when(sweep > 0)
            def _():
                for copy in halo_copies(e):
                    copy.wait()

            sweep_slab(src, dst, 0, station)
            if own_az > 1:
                sweep_slab(src, dst, own_az - 1, station)
            for copy in halo_copies(e + 1):
                copy.start()

            @pl.loop(1, own_az - 1)
            def _(a):
                sweep_slab(src, dst, a, station)

        last = station * SWEEPS
        slot = last % 2
        final = station == STEPS - 1
        if final:

            def pack_state(a, start, row):
                o_state[pl.ds(row, nf, stride=rows), :] = x_ref[slot, a + 1, pl.ds(start, nf), :]

            each_run(pack_state)
            exchange(*out_state_args, True)

        advect_all(slot, last, final)

    def pack_forcing(a, start, row):
        o_forcing[pl.ds(row, nf, stride=rows), :] = f_ref[a, pl.ds(start, nf), :]

    each_run(pack_forcing)
    exchange(*out_forcing_args, True)
    exchange(*out_state_args, False)
    exchange(*out_forcing_args, False)


def per_device(state_in, forcing_in, base_flow, station_index, lobe_count):
    _, per_dev, variables, span_az, radii = state_in.shape
    nf = lax.axis_size("freq")
    planes = lax.axis_size("plane")
    freqs = per_dev * nf
    ntime = 3 * freqs // 2
    own_az = span_az // nf
    stored = base_flow.shape[0]
    slopes, inverse_p = radial_tables(radii)
    mode_ids = (np.arange(nf)[None, :] * per_dev + np.arange(per_dev)[:, None]).reshape(-1)
    inverse, forward = transform_tables(mode_ids, freqs, ntime)
    omegas = np.broadcast_to((0.5 * mode_ids / freqs).astype(np.float32)[:, None], (freqs, radii))
    plane = lax.axis_index("plane")
    here = ring_of(lax.axis_index("freq"), plane, nf, planes)
    shape_az = chevron(lobe_count, own_az, here * own_az, span_az * planes)

    def padded_rows(count):
        return -(-count // 8) * 8

    def chunks(x, size):
        x = x.reshape(-1, nf, own_az, radii).transpose(1, 0, 2, 3).reshape(nf, -1, radii)
        x = jnp.pad(x, ((0, 0), (0, size - x.shape[1]), (0, 0)))
        return x.reshape(nf * size, radii)

    count = 2 * per_dev * variables * own_az
    rows = padded_rows(count)
    base_rows = padded_rows(stored * variables * own_az)
    w_rows = padded_rows(variables * own_az)
    dims = (nf, planes, own_az, variables, per_dev, radii, stored, rows, base_rows, w_rows)
    half = variables * freqs
    exchanges = (STEPS - 1) * SWEEPS + 1
    runs = 2 * per_dev * variables
    edge_rows = padded_rows(runs)
    first_mode = lax.axis_index("freq") * per_dev
    rates = 0.5 * (first_mode + jnp.arange(per_dev)).astype(jnp.float32) / freqs
    smem = pl.BlockSpec(memory_space=pltpu.SMEM)
    anywhere = pl.BlockSpec(memory_space=pl.ANY)
    packed = (nf * rows, radii)
    f32 = jnp.float32
    outs = pl.pallas_call(
        functools.partial(march, dims),
        out_shape=[jax.ShapeDtypeStruct(packed, f32)] * 2,
        in_specs=[smem, smem, smem, anywhere, anywhere, anywhere] + [anywhere] * 5,
        out_specs=[anywhere, anywhere],
        scratch_shapes=[
            pltpu.VMEM(packed, f32),
            pltpu.VMEM((nf * base_rows, radii), f32),
            pltpu.VMEM(packed, f32),
            pltpu.VMEM((w_rows, radii), f32),
            pltpu.VMEM((nf * w_rows, radii), f32),
            pltpu.VMEM((variables, span_az, radii), f32),
            pltpu.VMEM((2, runs, span_az + 16, radii), f32),
            pltpu.VMEM((runs, span_az, radii), f32),
            pltpu.VMEM((SWEEPS, 2, edge_rows, radii), f32),
            pltpu.VMEM((SWEEPS, 2, edge_rows, radii), f32),
            pltpu.VMEM((2, own_az + 2, 2 * half, radii), f32),
            pltpu.VMEM((own_az, 2 * half, radii), f32),
            pltpu.VMEM((own_az, 2 * half, radii), f32),
            pltpu.VMEM(((STEPS - 1) * own_az, padded_rows(variables), radii), f32),
            pltpu.VMEM(packed, f32),
            pltpu.VMEM(packed, f32),
            pltpu.SemaphoreType.DMA((5, nf)),
            pltpu.SemaphoreType.DMA((5, nf)),
            pltpu.SemaphoreType.DMA((5,)),
            pltpu.SemaphoreType.DMA((2, exchanges)),
            pltpu.SemaphoreType.DMA((2, exchanges)),
            pltpu.SemaphoreType.DMA((2, SWEEPS)),
            pltpu.SemaphoreType.DMA((2, SWEEPS)),
            pltpu.SemaphoreType.DMA((2,)),
            pltpu.VMEM((freqs, radii), f32),
            pltpu.VMEM((2 * radii, 2 * radii), jnp.bfloat16),
            pltpu.VMEM((2 * radii, 2 * radii), jnp.bfloat16),
            pltpu.VMEM((ntime, 8 * freqs), jnp.bfloat16),
            pltpu.VMEM((2 * freqs, 4 * ntime), jnp.bfloat16),
            pltpu.SemaphoreType.DMA((5,)),
        ],
        compiler_params=pltpu.CompilerParams(
            collective_id=0, has_side_effects=True, vmem_limit_bytes=63_000 * 1024
        ),
    )(
        station_index,
        shape_az,
        rates,
        state_in.reshape(runs, span_az, radii),
        chunks(base_flow, base_rows),
        forcing_in.reshape(runs, span_az, radii),
        jnp.asarray(omegas),
        right_table(inverse_p.T),
        right_table(slopes.T),
        left_table(inverse.transpose(2, 0, 1).reshape(ntime, 2 * freqs)),
        left_table(forward.reshape(2 * freqs, ntime)),
    )

    return tuple(finish(y, nf, per_dev, variables, own_az, radii, rows, count) for y in outs)


def finish(y, nf, per_dev, variables, own_az, radii, rows, count):
    y = y.reshape(nf, rows, radii)[:, :count].reshape(nf, -1, own_az, radii)
    return y.transpose(1, 0, 2, 3).reshape(2, per_dev, variables, nf * own_az, radii)


def stacked_table(table):
    high, low = np_halves(table)
    return jnp.asarray(np.tile(np.concatenate([high, low], axis=0), (1, 2)))


def times_stacked(table, x):
    height = table.shape[0] // 2
    y = jnp.dot(table, jnp.concatenate(halves(x), axis=0), preferred_element_type=jnp.float32)
    return y[:height] + y[height:]


def relay(
    dims,
    lobe_ref,
    far_station,
    state_ref,
    base_ref,
    forcing_ref,
    far_qt,
    far_st,
    far_inv,
    far_fwd,
    g_state,
    g_forcing,
    r_state,
    found,
    offered,
    taken,
    s_w,
    plane_w,
    x_one,
    b_one,
    edge_out,
    edge_in,
    x_ref,
    b_ref,
    w_ref,
    o_state,
    o_march,
    o_forcing,
    send_sem,
    recv_sem,
    offer_send,
    offer_recv,
    w_send,
    w_recv,
    halo_send,
    halo_recv,
    edge_send,
    edge_recv,
    load_sem,
    omega_ref,
    qt_ref,
    st_ref,
    inv_ref,
    fwd_ref,
    table_sem,
    station_ref,
):
    nf, planes, own_az, variables, per_dev, radii, stored = dims
    freqs = nf * per_dev
    span = nf * own_az
    parts = 2 * per_dev
    ntime = inv_ref.shape[0] // 2
    pair = 2 * freqs
    me = lax.axis_index("freq")
    plane = lax.axis_index("plane")
    ring = nf * planes
    here = ring_of(me, plane, nf, planes)
    part, block = here // nf, here % nf
    fold = nf // 2
    side, seat = me // fold, me % fold
    share = span // fold
    blocks = share // own_az

    def mate(i):
        return side * fold + i, plane


    def named(device):
        return {"freq": device[0], "plane": device[1]}

    def is_me(device):
        return (device[0] == me) & (device[1] == plane)

    right_id = named(device_of((here + 1) % ring, nf, planes))
    left_id = named(device_of((here + ring - 1) % ring, nf, planes))
    barrier = pltpu.get_barrier_semaphore()

    def greet(device):
        pl.semaphore_signal(barrier, inc=1, device_id=device, device_id_type=MESH)

    @pl.loop(1, fold)
    def _(d):
        greet(named(mate((seat + d) % fold)))

    beyond = {"freq": me, "plane": (plane + 1) % planes}
    across = {"freq": (1 - side) * fold + seat, "plane": plane}
    greet(beyond)
    greet(across)
    load_state = pltpu.make_async_copy(
        state_ref, x_one.at[0, :, :, pl.ds(8, span), :], load_sem.at[0]
    )
    load_forcing = pltpu.make_async_copy(forcing_ref, b_one, load_sem.at[1])
    load_state.start()
    load_forcing.start()
    tables = [
        pltpu.make_async_copy(far, near, table_sem.at[i])
        for i, (far, near) in enumerate(
            (
                (far_station, station_ref),
                (far_qt, qt_ref),
                (far_st, st_ref),
                (far_inv, inv_ref),
                (far_fwd, fwd_ref),
            )
        )
    ]
    for table in tables:
        table.start()
    pl.semaphore_wait(barrier, fold + 1)

    def owner(i):
        return device_of(plane * nf + i, nf, planes)

    def holder(i):
        return i, part

    def azimuths(i):
        return pl.ds(pl.multiple_of(i * own_az, 8), own_az)

    def exchange(k, piece, landing, target, mine, count, landed, sent):
        def copy(i):
            return pltpu.make_async_remote_copy(
                src_ref=piece(i),
                dst_ref=landing(mine),
                send_sem=send_sem.at[k],
                recv_sem=recv_sem.at[k],
                device_id=named(target(i)),
                device_id_type=MESH,
            )

        def start(first=0, stop=count):
            @pl.loop(first, stop)
            def _(d):
                i = (d + me) % count
                stays = is_me(target(i))

                @pl.when(stays)
                def _():
                    pltpu.make_async_copy(piece(i), landing(mine), recv_sem.at[k]).start()

                @pl.when(jnp.logical_not(stays))
                def _():
                    copy(i).start()

        def all_of(ref):
            return pltpu.make_async_remote_copy(
                src_ref=ref,
                dst_ref=ref,
                send_sem=send_sem.at[k],
                recv_sem=recv_sem.at[k],
                device_id=beyond,
                device_id_type=MESH,
            )

        def wait():
            all_of(landed).wait_recv()

        def drain():
            if count < nf:
                all_of(sent(count - 1)).wait_send()
            else:

                @pl.when(part == plane)
                def _():
                    all_of(sent(count - 1)).wait_send()

                @pl.when(part != plane)
                def _():
                    all_of(sent(count)).wait_send()

        return start, wait, drain

    def chunk(i):
        return pl.ds(pl.multiple_of(i * share, 8), share)

    base_start, base_wait, base_drain = exchange(
        0,
        lambda i: base_ref.at[:, :, chunk(i), :],
        lambda j: found.at[j],
        mate,
        seat,
        fold,
        found,
        lambda n: found.at[pl.ds(0, n)],
    )

    def offers(station, v):
        return pltpu.make_async_remote_copy(
            src_ref=offered.at[station, v],
            dst_ref=taken.at[station, v],
            send_sem=offer_send.at[station, v],
            recv_sem=offer_recv.at[station, v],
            device_id=across,
            device_id_type=MESH,
        )

    def w_moves(station, v):
        return exchange(
            1 + station * variables + v,
            lambda i: s_w.at[station, v],
            lambda j: plane_w.at[station, v, chunk(j), :],
            mate,
            seat,
            fold,
            plane_w.at[station, v],
            lambda n: plane_w.at[station, v, pl.ds(0, n * share), :],
        )

    def coefficient_copies():
        for j in range(blocks):
            target = device_of(plane * nf + seat * blocks + j, nf, planes)
            source = s_w.at[1, :, pl.ds(j * own_az, own_az), :]
            remote = pltpu.make_async_remote_copy(
                src_ref=source,
                dst_ref=w_ref,
                send_sem=w_send.at[j],
                recv_sem=w_recv.at[0],
                device_id=named(target),
                device_id_type=MESH,
            )
            local = pltpu.make_async_copy(source, w_ref, w_recv.at[1])
            near = target[0] // fold == side
            yield remote, local, near & jnp.logical_not(is_me(target)), near & is_me(target)

    def coefficient_start():
        for remote, local, away, home in coefficient_copies():
            pl.when(away)(remote.start)
            pl.when(home)(local.start)

    def coefficient_wait():
        for remote, local, away, home in coefficient_copies():
            pl.when(away)(remote.wait_send)
            pl.when(home)(local.wait)
        source = (side * fold + block // blocks, part)
        arrived = pltpu.make_async_remote_copy(
            src_ref=w_ref,
            dst_ref=w_ref,
            send_sem=w_send.at[0],
            recv_sem=w_recv.at[0],
            device_id=named(source),
            device_id_type=MESH,
        )
        pl.when(jnp.logical_not(is_me(source)))(arrived.wait_recv)

    settled = SWEEPS % 2

    def state_moves(v):
        return exchange(
            1 + 2 * variables + v,
            lambda i: x_one.at[
                settled, :, v, pl.ds(pl.multiple_of(8 + i * own_az, 8), own_az), :
            ],
            lambda j: r_state.at[j, v],
            owner,
            me,
            nf,
            r_state.at[:, v],
            lambda n: r_state.at[pl.ds(0, n), v],
        )

    def march_moves(v):
        return exchange(
            1 + 4 * variables + v,
            lambda i: o_march.at[i, v],
            lambda j: b_one.at[:, v, azimuths(j), :],
            holder,
            block,
            nf,
            b_one.at[:, v],
            lambda n: o_march.at[pl.ds(0, n), v],
        )

    def out_moves(v):
        return exchange(
            1 + 3 * variables + v,
            lambda i: o_state.at[i, v],
            lambda j: g_state.at[:, v, azimuths(j), :],
            holder,
            block,
            nf,
            g_state.at[:, v],
            lambda n: o_state.at[pl.ds(0, n), v],
        )

    forcing_start, forcing_wait, forcing_drain = exchange(
        1 + 4 * variables + RETURNED,
        lambda i: o_forcing.at[i],
        lambda j: g_forcing.at[:, :, azimuths(j), :],
        holder,
        block,
        nf,
        g_forcing,
        lambda n: o_forcing.at[pl.ds(0, n)],
    )
    base_start()

    def halo_copies(e, v):
        slot = e % 2
        rows = pl.ds(pl.multiple_of(v * pair, 8), pair)
        return [
            pltpu.make_async_remote_copy(
                src_ref=x_ref.at[slot, source, rows, :],
                dst_ref=x_ref.at[slot, target, rows, :],
                send_sem=halo_send.at[side, slot, v],
                recv_sem=halo_recv.at[side, slot, v],
                device_id=device,
                device_id_type=MESH,
            )
            for side, source, target, device in (
                (0, own_az, 0, right_id),
                (1, 1, own_az + 1, left_id),
            )
        ]

    def edge_copy(e, v):
        turn = e % 2
        return pltpu.make_async_remote_copy(
            src_ref=edge_out.at[turn, v],
            dst_ref=edge_in.at[turn, v],
            send_sem=edge_send.at[turn, v],
            recv_sem=edge_recv.at[turn, v],
            device_id=beyond,
            device_id_type=MESH,
        )

    def send_edges(e, v):
        slot = e % 2
        for ck in range(parts):
            edge_out[slot, v, pl.ds(ck, 1), :] = x_one[slot, ck, v, pl.ds(7 + span, 1), :]
            edge_out[slot, v, pl.ds(parts + ck, 1), :] = x_one[slot, ck, v, pl.ds(8, 1), :]
        edge_copy(e, v).start()

    for kk in range(per_dev):
        modes = lax.broadcasted_iota(jnp.int32, (nf, radii), 0) * per_dev + kk
        omega_ref[pl.ds(kk * nf, nf), :] = 0.5 * modes.astype(jnp.float32) / freqs
    load_state.wait()

    @pl.loop(0, variables)
    def _(v):
        send_edges(0, v)

    load_forcing.wait()

    @pl.loop(0, variables)
    def _(v):
        for ck in range(parts):
            b_one[ck, v] = MARCH_WEIGHT * x_one[0, ck, v, pl.ds(8, span), :] + b_one[ck, v]

    for table in tables:
        table.wait()
    position = plane * span + seat * share + lax.broadcasted_iota(jnp.int32, (share, radii), 0)
    phases = (lobe_ref[0] * position) % (span * planes)
    shape = 1.0 + 0.5 * jnp.cos(2.0 * math.pi * phases.astype(jnp.float32) / (span * planes))
    base_wait()
    for station in range(STEPS):
        wanted = station_ref[station]
        for v in range(variables):
            offered[station, v] = (BASE_SCALE * shape) * found[
                (wanted // stored) % fold, wanted % stored, v
            ]
            offers(station, v).start()
    for station in range(STEPS):
        ours = jnp.full((share, radii), station_ref[station] // (stored * fold)) == side
        for v in range(variables):
            offers(station, v).wait()
            s_w[station, v] = jnp.where(ours, offered[station, v], taken[station, v])
            if station == 0 or v < RETURNED:
                w_moves(station, v)[0]()

    def sweep_plane(e, v, w):
        src, dst = e % 2, (e + 1) % 2
        edge_copy(e, v).wait()
        for ck in range(parts):
            x_one[src, ck, v, pl.ds(7, 1), :] = edge_in[src, v, pl.ds(ck, 1), :]
            x_one[src, ck, v, pl.ds(8 + span, 1), :] = edge_in[src, v, pl.ds(parts + ck, 1), :]
        for kk in range(per_dev):
            rate = (me * per_dev + kk).astype(jnp.float32) * (0.5 / freqs)
            at = [c * per_dev + kk for c in range(2)]
            real, imag = [x_one[src, ck, v, pl.ds(8, span), :] for ck in at]
            mixing = (w * real - rate * imag, w * imag + rate * real)
            summed = [
                SIDE_WEIGHT
                * (x_one[src, ck, v, pl.ds(7, span), :] + x_one[src, ck, v, pl.ds(9, span), :])
                + b_one[ck, v]
                - mixed_in
                for ck, mixed_in in zip(at, mixing)
            ]
            q = times_right(jnp.concatenate(summed, axis=0), qt_ref[...])
            x_one[dst, at[0], v, pl.ds(8, span), :] = q[:span]
            x_one[dst, at[1], v, pl.ds(8, span), :] = q[span:]

    @pl.loop(0, SWEEPS + LAG * (variables - 1))
    def _(turn):
        @pl.loop(0, variables)
        def _(v):
            e = turn - LAG * v

            @pl.when((e >= 0) & (e < SWEEPS))
            def _():
                @pl.when(e == 0)
                def _():
                    w_moves(0, v)[1]()

                sweep_plane(e, v, plane_w[0, v])

                @pl.when((e < SWEEPS - 1) | (v < RETURNED))
                def _():
                    send_edges(e + 1, v)

                @pl.when(e == SWEEPS - 1)
                def _():
                    state_moves(v)[0]()

    coefficient_start()

    def each_run(v, visit):
        for c in range(2):
            for kk in range(per_dev):
                start = pl.multiple_of(v * pair + (c * per_dev + kk) * nf, 8)
                visit(start, c * per_dev + kk)

    @pl.loop(0, variables)
    def _(v):
        state_moves(v)[1]()

        @pl.loop(0, own_az)
        def _(a):
            def unpack(start, ck):
                x_ref[0, a + 1, pl.ds(start, nf), :] = r_state[:, v, ck, a, :]

            each_run(v, unpack)

        for copy in halo_copies(0, v):
            copy.start()

    omega = omega_ref[...]

    def sweep_slabs(e, v):
        src, dst = e % 2, (e + 1) % 2
        rows = pl.ds(pl.multiple_of(v * pair, 8), pair)
        w = w_ref[v]
        summed = []
        for a in range(own_az):
            x = x_ref[src, a + 1, rows, :]
            beside = SIDE_WEIGHT * (x_ref[src, a, rows, :] + x_ref[src, a + 2, rows, :])
            real, imag = x[:freqs], x[freqs:]
            here_w = w[a : a + 1]
            mixing = [here_w * real - omega * imag, here_w * imag + omega * real]
            summed.append(beside + b_ref[a, rows, :] - jnp.concatenate(mixing, axis=0))
        q = times_right(jnp.concatenate(summed, axis=0), qt_ref[...])
        for a in range(own_az):
            x_ref[dst, a + 1, rows, :] = q[a * pair : (a + 1) * pair]

    def advect_slab(slot, a, final):
        x = x_ref[slot, a + 1]
        beside = 0.5 * (x_ref[slot, a + 2] - x_ref[slot, a])

        def lanes(y):
            return [y[v * pair : (v + 1) * pair] for v in range(variables)]

        both = jnp.concatenate(lanes(x) + lanes(beside), axis=1)
        in_time = times_stacked(inv_ref[...], both)
        u = [in_time[:, v * radii : (v + 1) * radii] for v in range(variables)]
        ua = [
            in_time[:, (variables + v) * radii : (variables + v + 1) * radii]
            for v in range(variables)
        ]
        radial = times_right(jnp.concatenate(u, axis=0), st_ref[...])
        ur = [radial[v * ntime : (v + 1) * ntime] for v in range(variables)]
        n = [u[1] * ur[v] + u[2] * ua[v] for v in range(variables)]
        n[0] = n[0] + u[0] * (ur[1] + ua[2])
        source = -ADVECT_SCALE * jnp.concatenate(n, axis=1)
        spectral = times_stacked(fwd_ref[...], source)
        for v in range(variables):
            forcing = spectral[:, v * radii : (v + 1) * radii]
            if final:
                for ck in range(parts):
                    o_forcing[:, ck, v, a, :] = forcing[ck * nf : (ck + 1) * nf]
            else:
                march = MARCH_WEIGHT * x[v * pair : (v + 1) * pair] + forcing
                b_ref[a, pl.ds(v * pair, pair), :] = march
                if v < RETURNED:
                    for ck in range(parts):
                        o_march[:, v, ck, a, :] = march[ck * nf : (ck + 1) * nf]

    def advect_all(e, final):
        slot = e % 2

        @pl.loop(1, own_az - 1)
        def _(a):
            advect_slab(slot, a, final)

        @pl.loop(0, variables)
        def _(v):
            for copy in halo_copies(e, v):
                copy.wait()

        @pl.loop(0, 2)
        def _(side):
            advect_slab(slot, side * (own_az - 1), final)

    advect_all(0, False)
    coefficient_wait()

    @pl.loop(0, SWEEPS * variables)
    def _(turn):
        e, v = turn // variables, turn % variables

        @pl.when(e > 0)
        def _():
            for copy in halo_copies(e, v):
                copy.wait()

        sweep_slabs(e, v)
        for copy in halo_copies(e + 1, v):
            copy.start()

        @pl.when(turn < nf)
        def _():
            for w in range(RETURNED):
                march_moves(w)[0](turn, turn + 1)

        @pl.when((e == SWEEPS - 1) & (v >= RETURNED))
        def _():
            @pl.loop(0, own_az)
            def _(a):
                def pack(start, ck):
                    o_state[:, v, ck, a, :] = x_ref[settled, a + 1, pl.ds(start, nf), :]

                each_run(v, pack)

            out_moves(v)[0]()

    advect_all(SWEEPS, True)
    forcing_start()
    for v in range(RETURNED):
        w_moves(1, v)[1]()
        march_moves(v)[1]()
        state_moves(v)[2]()

    @pl.loop(0, SWEEPS * RETURNED)
    def _(turn):
        e, v = SWEEPS + turn // RETURNED, turn % RETURNED
        sweep_plane(e, v, plane_w[1, v])

        @pl.when(e < 2 * SWEEPS - 1)
        def _():
            send_edges(e + 1, v)

    out_state = pltpu.make_async_copy(
        x_one.at[0, :, pl.ds(0, RETURNED), pl.ds(8, span), :],
        g_state.at[:, pl.ds(0, RETURNED), :, :],
        load_sem.at[0],
    )
    out_state.start()

    @pl.loop(RETURNED, variables)
    def _(v):
        out_moves(v)[1]()

    out_state.wait()
    forcing_wait()
    base_drain()
    for v in range(RETURNED):
        w_moves(1, v)[2]()
        march_moves(v)[2]()

    @pl.loop(0, variables)
    def _(v):
        w_moves(0, v)[2]()

    @pl.loop(RETURNED, variables)
    def _(v):
        state_moves(v)[2]()
        out_moves(v)[2]()

    forcing_drain()


LAG = 2
RETURNED = 1


def per_device_tiled(state_in, forcing_in, base_flow, station_index, lobe_count):
    _, per_dev, variables, span_az, radii = state_in.shape
    nf = lax.axis_size("freq")
    planes = lax.axis_size("plane")
    freqs = per_dev * nf
    ntime = 3 * freqs // 2
    own_az = span_az // nf
    stored = base_flow.shape[0]
    slopes, inverse_p = radial_tables(radii)
    mode_ids = (np.arange(nf)[None, :] * per_dev + np.arange(per_dev)[:, None]).reshape(-1)
    inverse, forward = transform_tables(mode_ids, freqs, ntime)
    dims = (nf, planes, own_az, variables, per_dev, radii, stored)
    parts = 2 * per_dev
    edge_rows = -(-2 * parts // 8) * 8
    anywhere = pl.BlockSpec(memory_space=pl.ANY)
    far = pl.BlockSpec(memory_space=pltpu.HBM)
    f32 = jnp.float32
    whole = (parts, variables, span_az, radii)
    slab = variables * 2 * freqs
    share = span_az // (nf // 2)
    moves = 2 + 4 * variables + RETURNED
    outs = pl.pallas_call(
        functools.partial(relay, dims),
        out_shape=[jax.ShapeDtypeStruct(whole, f32)] * 2,
        in_specs=[pl.BlockSpec(memory_space=pltpu.SMEM)] + [far] * 8,
        out_specs=[anywhere, anywhere],
        scratch_shapes=[
            pltpu.VMEM((nf, variables, parts, own_az, radii), f32),
            pltpu.VMEM((nf // 2, stored, variables, share, radii), f32),
            pltpu.VMEM((STEPS, variables, share, radii), f32),
            pltpu.VMEM((STEPS, variables, share, radii), f32),
            pltpu.VMEM((STEPS, variables, share, radii), f32),
            pltpu.VMEM((STEPS, variables, span_az, radii), f32),
            pltpu.VMEM((2, parts, variables, span_az + 16, radii), f32),
            pltpu.VMEM(whole, f32),
            pltpu.VMEM((2, variables, edge_rows, radii), f32),
            pltpu.VMEM((2, variables, edge_rows, radii), f32),
            pltpu.VMEM((2, own_az + 2, slab, radii), f32),
            pltpu.VMEM((own_az, slab, radii), f32),
            pltpu.VMEM((variables, own_az, radii), f32),
            pltpu.VMEM((nf, variables, parts, own_az, radii), f32),
            pltpu.VMEM((nf, RETURNED, parts, own_az, radii), f32),
            pltpu.VMEM((nf, parts, variables, own_az, radii), f32),
            pltpu.SemaphoreType.DMA((moves,)),
            pltpu.SemaphoreType.DMA((moves,)),
            pltpu.SemaphoreType.DMA((STEPS, variables)),
            pltpu.SemaphoreType.DMA((STEPS, variables)),
            pltpu.SemaphoreType.DMA((share // own_az,)),
            pltpu.SemaphoreType.DMA((2,)),
            pltpu.SemaphoreType.DMA((2, 2, variables)),
            pltpu.SemaphoreType.DMA((2, 2, variables)),
            pltpu.SemaphoreType.DMA((2, variables)),
            pltpu.SemaphoreType.DMA((2, variables)),
            pltpu.SemaphoreType.DMA((2,)),
            pltpu.VMEM((freqs, radii), f32),
            pltpu.VMEM((2 * radii, 2 * radii), jnp.bfloat16),
            pltpu.VMEM((2 * radii, 2 * radii), jnp.bfloat16),
            pltpu.VMEM((2 * ntime, 4 * freqs), jnp.bfloat16),
            pltpu.VMEM((4 * freqs, 2 * ntime), jnp.bfloat16),
            pltpu.SemaphoreType.DMA((5,)),
            pltpu.SMEM(station_index.shape, jnp.int32),
        ],
        compiler_params=pltpu.CompilerParams(
            collective_id=0, has_side_effects=True, vmem_limit_bytes=32 * 1024 * 1024
        ),
    )(
        lobe_count,
        *[
            pltpu.with_memory_space_constraint(x, pltpu.HBM)
            for x in (
                station_index,
                state_in.reshape(whole),
                base_flow,
                forcing_in.reshape(whole),
                right_table(inverse_p.T),
                right_table(slopes.T),
                stacked_table(inverse.transpose(2, 0, 1).reshape(ntime, 2 * freqs)),
                stacked_table(forward.reshape(2 * freqs, ntime)),
            )
        ],
    )
    return tuple(y.reshape(state_in.shape) for y in outs)


def per_device_any(*args):
    nf = lax.axis_size("freq")
    tiles = args[0].shape[3] % (8 * nf) == 0 and nf % 2 == 0 and lax.axis_size("plane") == 2
    return (per_device_tiled if tiles else per_device)(*args)


MESH = pl.DeviceIdType.MESH


def solution(mesh):
    return jax.shard_map(
        per_device_any,
        mesh=mesh,
        in_specs=(
            P(None, "freq", None, "plane", None),
            P(None, "freq", None, "plane", None),
            P("freq", None, "plane", None),
            P(),
            P(),
        ),
        out_specs=(P(None, "freq", None, "plane", None), P(None, "freq", None, "plane", None)),
        check_vma=False,
    )
```

```python
import functools
import math

import jax
import jax.numpy as jnp
import numpy as np
from jax import lax
from jax.experimental import pallas as pl
from jax.experimental.pallas import tpu as pltpu
from jax.sharding import PartitionSpec as P

SWEEPS = 4
STEPS = 2


SIDE_WEIGHT = 1.25
MARCH_WEIGHT = 4.0
DIAG_SHIFT = 4.0
ADVECT_SCALE = 0.5
BASE_SCALE = 0.5


def radial_tables(radius_count):
    indices = np.arange(radius_count)
    angles = math.pi * indices / (radius_count - 1)
    nodes = np.cos(angles)
    weights = np.where((indices == 0) | (indices == radius_count - 1), 2.0, 1.0)
    parity = 1.0 - 2.0 * ((indices[:, None] + indices[None, :]) % 2)
    offdiag = indices[:, None] != indices[None, :]
    spacing = np.where(offdiag, nodes[:, None] - nodes[None, :], 1.0)
    entries = np.where(offdiag, weights[:, None] / weights[None, :] * parity / spacing, 0.0)
    entries = entries - np.diag(entries.sum(axis=1))
    slopes = np.sin(angles)[:, None] * entries / (radius_count - 1)
    system = slopes.T @ slopes + DIAG_SHIFT * np.eye(radius_count)
    return slopes.astype(np.float32), np.linalg.inv(system).astype(np.float32)


def transform_tables(mode_ids, freqs, ntime):
    time_ids = np.arange(ntime)
    angles = 2.0 * math.pi * (mode_ids[:, None] * time_ids[None, :] % ntime) / ntime
    stacked = np.stack([np.cos(angles), -np.sin(angles)])
    return (
        (stacked / math.sqrt(freqs)).astype(np.float32),
        (stacked / math.sqrt(ntime)).astype(np.float32),
    )


def chevron(lobe_count, azimuths, start_az, total_az):
    position = start_az + jnp.arange(azimuths)
    phases = lobe_count[0] * position % total_az
    return 1.0 + 0.5 * jnp.cos(2.0 * math.pi * phases.astype(jnp.float32) / total_az)


def halves(x):
    high = x.astype(jnp.bfloat16)
    return high, (x - high.astype(jnp.float32)).astype(jnp.bfloat16)


def right_table(table):
    high, low = np_halves(table)
    return jnp.asarray(np.tile(np.concatenate([high, low], axis=1), (2, 1)))


def left_table(table):
    high, low = np_halves(table)
    return jnp.asarray(np.concatenate([high, high, low, low], axis=1))


def np_halves(table):
    high = table.astype(jnp.bfloat16)
    return high, (table - high.astype(np.float32)).astype(jnp.bfloat16)


def times_right(x, table):
    width = table.shape[1] // 2
    y = jnp.dot(jnp.concatenate(halves(x), axis=1), table, preferred_element_type=jnp.float32)
    return y[:, :width] + y[:, width:]


def times_left(table, x):
    high, low = halves(x)
    return jnp.dot(
        table,
        jnp.concatenate([high, low, high, low], axis=0),
        preferred_element_type=jnp.float32,
    )


def ring_of(f, p, nf, planes):
    at = f
    if nf % 4 == 0:
        high = nf // 4
        z, y, x = f // 4, (f // 2) % 2, f % 2
        column = 2 * y + (x + y) % 2
        at = column * high + z + (column % 2) * (high - 1 - 2 * z)
    return at * planes + p


def device_of(g, nf, planes):
    at = g // planes
    f = at
    if nf % 4 == 0:
        high = nf // 4
        column, z = at // high, at % high
        z = z + (column % 2) * (high - 1 - 2 * z)
        y = column // 2
        f = 4 * z + 2 * y + (column + y) % 2
    return f, g % planes


def march(
    dims,
    station_ref,
    shape_ref,
    rate_ref,
    state_ref,
    s_base,
    forcing_ref,
    far_omega,
    far_qt,
    far_st,
    far_inv,
    far_fwd,
    g_state,
    g_forcing,
    r_state,
    r_base,
    s_state,
    s_w,
    r_w,
    plane_w,
    x_one,
    b_one,
    edge_out,
    edge_in,
    x_ref,
    b_ref,
    f_ref,
    w_ref,
    o_state,
    o_forcing,
    send_sem,
    recv_sem,
    own_sem,
    halo_send,
    halo_recv,
    edge_send,
    edge_recv,
    load_sem,
    omega_ref,
    qt_ref,
    st_ref,
    inv_ref,
    fwd_ref,
    table_sem,
):
    nf, planes, own_az, variables, per_dev, radii, stored, rows, base_rows, w_rows = dims
    freqs = nf * per_dev
    span = nf * own_az
    runs = 2 * per_dev * variables
    ntime = inv_ref.shape[0]
    half = variables * freqs
    me = lax.axis_index("freq")
    plane = lax.axis_index("plane")
    ring = nf * planes
    here = ring_of(me, plane, nf, planes)
    part, block = here // nf, here % nf

    def named(device):
        return {"freq": device[0], "plane": device[1]}

    right_id = named(device_of((here + 1) % ring, nf, planes))
    left_id = named(device_of((here + ring - 1) % ring, nf, planes))
    barrier = pltpu.get_barrier_semaphore()

    @pl.loop(1, ring)
    def _(d):
        other = (me * planes + plane + d) % ring
        pl.semaphore_signal(
            barrier,
            inc=1,
            device_id={"freq": other // planes, "plane": other % planes},
            device_id_type=MESH,
        )

    beyond = {"freq": me, "plane": (plane + 1) % planes}
    behind = {"freq": me, "plane": (plane + planes - 1) % planes}
    load_state = pltpu.make_async_copy(state_ref, x_one.at[0, :, pl.ds(8, span), :], load_sem.at[0])
    load_forcing = pltpu.make_async_copy(forcing_ref, b_one, load_sem.at[1])
    load_state.start()
    load_forcing.start()
    tables = [
        pltpu.make_async_copy(far, near, table_sem.at[i])
        for i, (far, near) in enumerate(
            (
                (far_omega, omega_ref),
                (far_qt, qt_ref),
                (far_st, st_ref),
                (far_inv, inv_ref),
                (far_fwd, fwd_ref),
            )
        )
    ]
    for table in tables:
        table.start()
    pl.semaphore_wait(barrier, ring - 1)

    def owner(i):
        return device_of(plane * nf + i, nf, planes)

    def holder(i):
        return i, part

    def is_me(device):
        return (device[0] == me) & (device[1] == plane)

    def exchange(k, source, landing, target, origin, pick, mine, size, first):
        def rows_of(ref, i):
            return ref.at[pl.ds(pl.multiple_of(i * size, 8), size), :]

        def copy(i):
            return pltpu.make_async_remote_copy(
                src_ref=rows_of(source, pick(i)),
                dst_ref=rows_of(landing, mine),
                send_sem=send_sem.at[k, i],
                recv_sem=recv_sem.at[k, mine],
                device_id=named(target(i)),
                device_id_type=MESH,
            )

        def arrival(i):
            return pltpu.make_async_remote_copy(
                src_ref=rows_of(landing, i),
                dst_ref=rows_of(landing, i),
                send_sem=send_sem.at[k, i],
                recv_sem=recv_sem.at[k, i],
                device_id=named(origin(i)),
                device_id_type=MESH,
            )

        def own(i):
            return pltpu.make_async_copy(
                rows_of(source, pick(i)), rows_of(landing, mine), own_sem.at[k]
            )

        @pl.loop(0, nf)
        def _(d):
            i = (d + me) % nf
            stays = is_me(target(i))

            @pl.when(stays)
            def _():
                if first:
                    own(i).start()
                else:
                    own(i).wait()

            @pl.when(jnp.logical_not(stays))
            def _():
                if first:
                    copy(i).start()
                else:
                    copy(i).wait_send()

            if not first:

                @pl.when(jnp.logical_not(is_me(origin(i))))
                def _():
                    arrival(i).wait_recv()

    def same(i):
        return i

    base_args = (1, s_base, r_base, owner, holder, same, me, base_rows)
    state_args = (0, s_state, r_state, owner, holder, same, me, rows)
    w_args = (2, s_w, r_w, holder, owner, lambda i: 0, block, w_rows)
    out_state_args = (3, o_state, g_state, holder, owner, same, block, rows)
    out_forcing_args = (4, o_forcing, g_forcing, holder, owner, same, block, rows)
    exchange(*base_args, True)

    def halo_copies(e):
        slot = e % 2
        return (
            pltpu.make_async_remote_copy(
                src_ref=x_ref.at[slot, own_az],
                dst_ref=x_ref.at[slot, 0],
                send_sem=halo_send.at[0, e],
                recv_sem=halo_recv.at[0, e],
                device_id=right_id,
                device_id_type=MESH,
            ),
            pltpu.make_async_remote_copy(
                src_ref=x_ref.at[slot, 1],
                dst_ref=x_ref.at[slot, own_az + 1],
                send_sem=halo_send.at[1, e],
                recv_sem=halo_recv.at[1, e],
                device_id=left_id,
                device_id_type=MESH,
            ),
        )

    def place(a, c, v, kk):
        return ((c * variables + v) * per_dev + kk) * nf

    def packed_row(a, c, v, kk):
        return ((c * per_dev + kk) * variables + v) * own_az + a

    def each_run(visit):
        @pl.loop(0, own_az)
        def _(a):
            for c in range(2):
                for v in range(variables):
                    for kk in range(per_dev):
                        visit(a, place(a, c, v, kk), packed_row(a, c, v, kk))

    def in_row(a, c, v, kk):
        return ((c * per_dev + kk) * variables + v) * own_az + a

    def edge_copies(e):
        return [
            pltpu.make_async_remote_copy(
                src_ref=edge_out.at[e, side],
                dst_ref=edge_in.at[e, side],
                send_sem=edge_send.at[side, e],
                recv_sem=edge_recv.at[side, e],
                device_id=target,
                device_id_type=MESH,
            )
            for side, target in ((0, beyond), (1, behind))
        ]

    def send_edges(slot, e):
        for m in range(runs):
            edge_out[e, 0, pl.ds(m, 1), :] = x_one[slot, m, pl.ds(7 + span, 1), :]
            edge_out[e, 1, pl.ds(m, 1), :] = x_one[slot, m, pl.ds(8, 1), :]
        for copy in edge_copies(e):
            copy.start()

    for table in tables:
        table.wait()
    load_state.wait()
    send_edges(0, 0)
    load_forcing.wait()

    @pl.loop(0, runs)
    def _(m):
        b_one[m] = MARCH_WEIGHT * x_one[0, m, pl.ds(8, span), :] + b_one[m]

    exchange(*base_args, False)
    for station in range(STEPS):
        wanted = station_ref[station]

        @pl.loop(0, own_az)
        def _(a):
            for v in range(variables):
                scaled = (BASE_SCALE * shape_ref[a]) * r_base[
                    pl.ds(
                        (wanted // stored) * base_rows
                        + ((wanted % stored) * variables + v) * own_az
                        + a,
                        1,
                    ),
                    :,
                ]
                if station == 0:
                    s_w[pl.ds(v * own_az + a, 1), :] = scaled
                else:
                    w_ref[(station - 1) * own_az + a, pl.ds(v, 1), :] = scaled

        if station == 0:
            exchange(*w_args, True)
    exchange(*w_args, False)

    @pl.loop(0, nf)
    def _(j):
        for v in range(variables):
            plane_w[v, pl.ds(j * own_az, own_az), :] = r_w[pl.ds(j * w_rows + v * own_az, own_az), :]

    @pl.loop(0, SWEEPS)
    def _(e):
        src, dst = e % 2, (e + 1) % 2
        for copy in edge_copies(e):
            copy.wait()
        for m in range(runs):
            x_one[src, m, pl.ds(7, 1), :] = edge_in[e, 0, pl.ds(m, 1), :]
            x_one[src, m, pl.ds(8 + span, 1), :] = edge_in[e, 1, pl.ds(m, 1), :]
        for kk in range(per_dev):
            rate = rate_ref[kk]

            @pl.loop(0, variables)
            def _(v):
                w = plane_w[v]
                at = [(c * per_dev + kk) * variables + v for c in range(2)]
                real, imag = [x_one[src, m, pl.ds(8, span), :] for m in at]
                mixing = (w * real - rate * imag, w * imag + rate * real)
                summed = [
                    SIDE_WEIGHT
                    * (x_one[src, m, pl.ds(7, span), :] + x_one[src, m, pl.ds(9, span), :])
                    + b_one[m]
                    - mixed
                    for m, mixed in zip(at, mixing)
                ]
                q = times_right(jnp.concatenate(summed, axis=0), qt_ref[...])
                x_one[dst, at[0], pl.ds(8, span), :] = q[:span]
                x_one[dst, at[1], pl.ds(8, span), :] = q[span:]

        @pl.when(e < SWEEPS - 1)
        def _():
            send_edges(dst, e + 1)

    settled = SWEEPS % 2

    @pl.loop(0, nf)
    def _(j):
        for m in range(runs):
            s_state[pl.ds(j * rows + m * own_az, own_az), :] = x_one[
                settled, m, pl.ds(8 + j * own_az, own_az), :
            ]

    exchange(*state_args, True)
    exchange(*state_args, False)

    def unpack_state(a, start, row):
        x_ref[0, a + 1, pl.ds(start, nf), :] = r_state[pl.ds(row, nf, stride=rows), :]

    each_run(unpack_state)
    for copy in halo_copies(0):
        copy.start()
    omega = omega_ref[...][None]
    flat = (2 * half, radii)
    cube = (variables, freqs, radii)

    def sweep_slab(src, dst, a, station):
        x = x_ref[src, a + 1]
        beside = SIDE_WEIGHT * (x_ref[src, a] + x_ref[src, a + 2]) + b_ref[a]
        real, imag = x[:half].reshape(cube), x[half:].reshape(cube)
        w = w_ref[(station - 1) * own_az + a][:variables][:, None, :]
        mixing = jnp.concatenate([w * real - omega * imag, w * imag + omega * real], axis=0)
        summed = beside - mixing.reshape(flat)
        x_ref[dst, a + 1] = times_right(summed, qt_ref[...])

    def advect_slab(slot, a, final):
        x = x_ref[slot, a + 1]
        beside = 0.5 * (x_ref[slot, a + 2] - x_ref[slot, a])

        def lanes(y):
            return [
                jnp.concatenate(
                    [
                        y[v * freqs : (v + 1) * freqs],
                        y[half + v * freqs : half + (v + 1) * freqs],
                    ],
                    axis=0,
                )
                for v in range(variables)
            ]

        both = jnp.concatenate(lanes(x) + lanes(beside), axis=1)
        in_time = times_left(inv_ref[...], both)
        u = [in_time[:, v * radii : (v + 1) * radii] for v in range(variables)]
        ua = [
            in_time[:, (variables + v) * radii : (variables + v + 1) * radii]
            for v in range(variables)
        ]
        radial = times_right(jnp.concatenate(u, axis=0), st_ref[...])
        ur = [radial[v * ntime : (v + 1) * ntime] for v in range(variables)]
        n = [u[1] * ur[v] + u[2] * ua[v] for v in range(variables)]
        n[0] = n[0] + u[0] * (ur[1] + ua[2])
        source = -ADVECT_SCALE * jnp.concatenate(n, axis=1)
        spectral = times_left(fwd_ref[...], source)
        forcing = jnp.concatenate(
            [
                spectral[c * freqs : (c + 1) * freqs, v * radii : (v + 1) * radii]
                for c in range(2)
                for v in range(variables)
            ],
            axis=0,
        )
        if final:
            f_ref[a] = forcing
        else:
            b_ref[a] = MARCH_WEIGHT * x + forcing

    def advect_all(slot, e, final):
        @pl.loop(1, own_az - 1)
        def _(a):
            advect_slab(slot, a, final)

        for copy in halo_copies(e):
            copy.wait()
        advect_slab(slot, 0, final)
        if own_az > 1:
            advect_slab(slot, own_az - 1, final)

    advect_all(0, 0, False)
    for station in range(1, STEPS):

        @pl.loop(0, SWEEPS)
        def _(sweep):
            e = (station - 1) * SWEEPS + sweep
            src, dst = e % 2, (e + 1) % 2

            @pl.when(sweep > 0)
            def _():
                for copy in halo_copies(e):
                    copy.wait()

            sweep_slab(src, dst, 0, station)
            if own_az > 1:
                sweep_slab(src, dst, own_az - 1, station)
            for copy in halo_copies(e + 1):
                copy.start()

            @pl.loop(1, own_az - 1)
            def _(a):
                sweep_slab(src, dst, a, station)

        last = station * SWEEPS
        slot = last % 2
        final = station == STEPS - 1
        if final:

            def pack_state(a, start, row):
                o_state[pl.ds(row, nf, stride=rows), :] = x_ref[slot, a + 1, pl.ds(start, nf), :]

            each_run(pack_state)
            exchange(*out_state_args, True)

        advect_all(slot, last, final)

    def pack_forcing(a, start, row):
        o_forcing[pl.ds(row, nf, stride=rows), :] = f_ref[a, pl.ds(start, nf), :]

    each_run(pack_forcing)
    exchange(*out_forcing_args, True)
    exchange(*out_state_args, False)
    exchange(*out_forcing_args, False)


def per_device(state_in, forcing_in, base_flow, station_index, lobe_count):
    _, per_dev, variables, span_az, radii = state_in.shape
    nf = lax.axis_size("freq")
    planes = lax.axis_size("plane")
    freqs = per_dev * nf
    ntime = 3 * freqs // 2
    own_az = span_az // nf
    stored = base_flow.shape[0]
    slopes, inverse_p = radial_tables(radii)
    mode_ids = (np.arange(nf)[None, :] * per_dev + np.arange(per_dev)[:, None]).reshape(-1)
    inverse, forward = transform_tables(mode_ids, freqs, ntime)
    omegas = np.broadcast_to((0.5 * mode_ids / freqs).astype(np.float32)[:, None], (freqs, radii))
    plane = lax.axis_index("plane")
    here = ring_of(lax.axis_index("freq"), plane, nf, planes)
    shape_az = chevron(lobe_count, own_az, here * own_az, span_az * planes)

    def padded_rows(count):
        return -(-count // 8) * 8

    def chunks(x, size):
        x = x.reshape(-1, nf, own_az, radii).transpose(1, 0, 2, 3).reshape(nf, -1, radii)
        x = jnp.pad(x, ((0, 0), (0, size - x.shape[1]), (0, 0)))
        return x.reshape(nf * size, radii)

    count = 2 * per_dev * variables * own_az
    rows = padded_rows(count)
    base_rows = padded_rows(stored * variables * own_az)
    w_rows = padded_rows(variables * own_az)
    dims = (nf, planes, own_az, variables, per_dev, radii, stored, rows, base_rows, w_rows)
    half = variables * freqs
    exchanges = (STEPS - 1) * SWEEPS + 1
    runs = 2 * per_dev * variables
    edge_rows = padded_rows(runs)
    first_mode = lax.axis_index("freq") * per_dev
    rates = 0.5 * (first_mode + jnp.arange(per_dev)).astype(jnp.float32) / freqs
    smem = pl.BlockSpec(memory_space=pltpu.SMEM)
    anywhere = pl.BlockSpec(memory_space=pl.ANY)
    packed = (nf * rows, radii)
    f32 = jnp.float32
    outs = pl.pallas_call(
        functools.partial(march, dims),
        out_shape=[jax.ShapeDtypeStruct(packed, f32)] * 2,
        in_specs=[smem, smem, smem, anywhere, anywhere, anywhere] + [anywhere] * 5,
        out_specs=[anywhere, anywhere],
        scratch_shapes=[
            pltpu.VMEM(packed, f32),
            pltpu.VMEM((nf * base_rows, radii), f32),
            pltpu.VMEM(packed, f32),
            pltpu.VMEM((w_rows, radii), f32),
            pltpu.VMEM((nf * w_rows, radii), f32),
            pltpu.VMEM((variables, span_az, radii), f32),
            pltpu.VMEM((2, runs, span_az + 16, radii), f32),
            pltpu.VMEM((runs, span_az, radii), f32),
            pltpu.VMEM((SWEEPS, 2, edge_rows, radii), f32),
            pltpu.VMEM((SWEEPS, 2, edge_rows, radii), f32),
            pltpu.VMEM((2, own_az + 2, 2 * half, radii), f32),
            pltpu.VMEM((own_az, 2 * half, radii), f32),
            pltpu.VMEM((own_az, 2 * half, radii), f32),
            pltpu.VMEM(((STEPS - 1) * own_az, padded_rows(variables), radii), f32),
            pltpu.VMEM(packed, f32),
            pltpu.VMEM(packed, f32),
            pltpu.SemaphoreType.DMA((5, nf)),
            pltpu.SemaphoreType.DMA((5, nf)),
            pltpu.SemaphoreType.DMA((5,)),
            pltpu.SemaphoreType.DMA((2, exchanges)),
            pltpu.SemaphoreType.DMA((2, exchanges)),
            pltpu.SemaphoreType.DMA((2, SWEEPS)),
            pltpu.SemaphoreType.DMA((2, SWEEPS)),
            pltpu.SemaphoreType.DMA((2,)),
            pltpu.VMEM((freqs, radii), f32),
            pltpu.VMEM((2 * radii, 2 * radii), jnp.bfloat16),
            pltpu.VMEM((2 * radii, 2 * radii), jnp.bfloat16),
            pltpu.VMEM((ntime, 8 * freqs), jnp.bfloat16),
            pltpu.VMEM((2 * freqs, 4 * ntime), jnp.bfloat16),
            pltpu.SemaphoreType.DMA((5,)),
        ],
        compiler_params=pltpu.CompilerParams(
            collective_id=0, has_side_effects=True, vmem_limit_bytes=63_000 * 1024
        ),
    )(
        station_index,
        shape_az,
        rates,
        state_in.reshape(runs, span_az, radii),
        chunks(base_flow, base_rows),
        forcing_in.reshape(runs, span_az, radii),
        jnp.asarray(omegas),
        right_table(inverse_p.T),
        right_table(slopes.T),
        left_table(inverse.transpose(2, 0, 1).reshape(ntime, 2 * freqs)),
        left_table(forward.reshape(2 * freqs, ntime)),
    )

    return tuple(finish(y, nf, per_dev, variables, own_az, radii, rows, count) for y in outs)


def finish(y, nf, per_dev, variables, own_az, radii, rows, count):
    y = y.reshape(nf, rows, radii)[:, :count].reshape(nf, -1, own_az, radii)
    return y.transpose(1, 0, 2, 3).reshape(2, per_dev, variables, nf * own_az, radii)


def stacked_table(table):
    high, low = np_halves(table)
    return jnp.asarray(np.tile(np.concatenate([high, low], axis=0), (1, 2)))


def times_stacked(table, x):
    height = table.shape[0] // 2
    y = jnp.dot(table, jnp.concatenate(halves(x), axis=0), preferred_element_type=jnp.float32)
    return y[:height] + y[height:]


def relay(
    dims,
    lobe_ref,
    far_station,
    state_ref,
    base_ref,
    forcing_ref,
    far_qt,
    far_st,
    far_inv,
    far_fwd,
    g_both,
    r_state,
    found,
    offered,
    taken,
    s_w,
    plane_w,
    x_one,
    b_one,
    edge_out,
    edge_in,
    x_ref,
    b_ref,
    w_ref,
    o_state,
    o_march,
    o_forcing,
    send_sem,
    recv_sem,
    offer_send,
    offer_recv,
    w_send,
    w_recv,
    halo_send,
    halo_recv,
    edge_send,
    edge_recv,
    load_sem,
    omega_ref,
    qt_ref,
    st_ref,
    inv_ref,
    fwd_ref,
    table_sem,
    station_ref,
):
    nf, planes, own_az, variables, per_dev, radii, stored = dims
    g_state, g_forcing = g_both.at[0], g_both.at[1]
    freqs = nf * per_dev
    span = nf * own_az
    parts = 2 * per_dev
    ntime = inv_ref.shape[0] // 2
    pair = 2 * freqs
    me = lax.axis_index("freq")
    plane = lax.axis_index("plane")
    ring = nf * planes
    here = ring_of(me, plane, nf, planes)
    part, block = here // nf, here % nf
    fold = nf // 2
    side, seat = me // fold, me % fold
    share = span // fold
    blocks = share // own_az

    def mate(i):
        return side * fold + i, plane


    def named(device):
        return {"freq": device[0], "plane": device[1]}

    def is_me(device):
        return (device[0] == me) & (device[1] == plane)

    right_id = named(device_of((here + 1) % ring, nf, planes))
    left_id = named(device_of((here + ring - 1) % ring, nf, planes))
    barrier = pltpu.get_barrier_semaphore()

    def greet(device):
        pl.semaphore_signal(barrier, inc=1, device_id=device, device_id_type=MESH)

    @pl.loop(1, fold)
    def _(d):
        greet(named(mate((seat + d) % fold)))

    beyond = {"freq": me, "plane": (plane + 1) % planes}
    across = {"freq": (1 - side) * fold + seat, "plane": plane}
    greet(beyond)
    greet(across)
    load_state = pltpu.make_async_copy(
        state_ref, x_one.at[0, :, :, pl.ds(8, span), :], load_sem.at[0]
    )
    load_forcing = pltpu.make_async_copy(forcing_ref, b_one, load_sem.at[1])
    load_state.start()
    load_forcing.start()
    tables = [
        pltpu.make_async_copy(far, near, table_sem.at[i])
        for i, (far, near) in enumerate(
            (
                (far_station, station_ref),
                (far_qt, qt_ref),
                (far_st, st_ref),
                (far_inv, inv_ref),
                (far_fwd, fwd_ref),
            )
        )
    ]
    for table in tables:
        table.start()
    pl.semaphore_wait(barrier, fold + 1)

    def owner(i):
        return device_of(plane * nf + i, nf, planes)

    def holder(i):
        return i, part

    def azimuths(i):
        return pl.ds(pl.multiple_of(i * own_az, 8), own_az)

    def exchange(k, piece, landing, target, mine, count, landed, sent):
        def copy(i):
            return pltpu.make_async_remote_copy(
                src_ref=piece(i),
                dst_ref=landing(mine),
                send_sem=send_sem.at[k],
                recv_sem=recv_sem.at[k],
                device_id=named(target(i)),
                device_id_type=MESH,
            )

        def start(first=0, stop=count):
            @pl.loop(first, stop)
            def _(d):
                i = (d + me) % count
                stays = is_me(target(i))

                @pl.when(stays)
                def _():
                    pltpu.make_async_copy(piece(i), landing(mine), recv_sem.at[k]).start()

                @pl.when(jnp.logical_not(stays))
                def _():
                    copy(i).start()

        def all_of(ref):
            return pltpu.make_async_remote_copy(
                src_ref=ref,
                dst_ref=ref,
                send_sem=send_sem.at[k],
                recv_sem=recv_sem.at[k],
                device_id=beyond,
                device_id_type=MESH,
            )

        def wait():
            all_of(landed).wait_recv()

        def drain():
            if count < nf:
                all_of(sent(count - 1)).wait_send()
            else:

                @pl.when(part == plane)
                def _():
                    all_of(sent(count - 1)).wait_send()

                @pl.when(part != plane)
                def _():
                    all_of(sent(count)).wait_send()

        return start, wait, drain

    def chunk(i):
        return pl.ds(pl.multiple_of(i * share, 8), share)

    base_start, base_wait, base_drain = exchange(
        0,
        lambda i: base_ref.at[:, :, chunk(i), :],
        lambda j: found.at[j],
        mate,
        seat,
        fold,
        found,
        lambda n: found.at[pl.ds(0, n)],
    )

    def offers(station, v):
        return pltpu.make_async_remote_copy(
            src_ref=offered.at[station, v],
            dst_ref=taken.at[station, v],
            send_sem=offer_send.at[station, v],
            recv_sem=offer_recv.at[station, v],
            device_id=across,
            device_id_type=MESH,
        )

    def w_moves(station, v):
        return exchange(
            1 + station * variables + v,
            lambda i: s_w.at[station, v],
            lambda j: plane_w.at[station, v, chunk(j), :],
            mate,
            seat,
            fold,
            plane_w.at[station, v],
            lambda n: plane_w.at[station, v, pl.ds(0, n * share), :],
        )

    def coefficient_copies():
        for j in range(blocks):
            target = device_of(plane * nf + seat * blocks + j, nf, planes)
            source = s_w.at[1, :, pl.ds(j * own_az, own_az), :]
            remote = pltpu.make_async_remote_copy(
                src_ref=source,
                dst_ref=w_ref,
                send_sem=w_send.at[j],
                recv_sem=w_recv.at[0],
                device_id=named(target),
                device_id_type=MESH,
            )
            local = pltpu.make_async_copy(source, w_ref, w_recv.at[1])
            near = target[0] // fold == side
            yield remote, local, near & jnp.logical_not(is_me(target)), near & is_me(target)

    def coefficient_start():
        for remote, local, away, home in coefficient_copies():
            pl.when(away)(remote.start)
            pl.when(home)(local.start)

    def coefficient_wait():
        for remote, local, away, home in coefficient_copies():
            pl.when(away)(remote.wait_send)
            pl.when(home)(local.wait)
        source = (side * fold + block // blocks, part)
        arrived = pltpu.make_async_remote_copy(
            src_ref=w_ref,
            dst_ref=w_ref,
            send_sem=w_send.at[0],
            recv_sem=w_recv.at[0],
            device_id=named(source),
            device_id_type=MESH,
        )
        pl.when(jnp.logical_not(is_me(source)))(arrived.wait_recv)

    settled = SWEEPS % 2

    def state_moves(v):
        return exchange(
            1 + 2 * variables + v,
            lambda i: x_one.at[
                settled, :, v, pl.ds(pl.multiple_of(8 + i * own_az, 8), own_az), :
            ],
            lambda j: r_state.at[j, v],
            owner,
            me,
            nf,
            r_state.at[:, v],
            lambda n: r_state.at[pl.ds(0, n), v],
        )

    def march_moves(v):
        return exchange(
            1 + 4 * variables + v,
            lambda i: o_march.at[i, v],
            lambda j: b_one.at[:, v, azimuths(j), :],
            holder,
            block,
            nf,
            b_one.at[:, v],
            lambda n: o_march.at[pl.ds(0, n), v],
        )

    def out_moves(v):
        return exchange(
            1 + 3 * variables + v,
            lambda i: o_state.at[i, v],
            lambda j: g_state.at[:, v, azimuths(j), :],
            holder,
            block,
            nf,
            g_state.at[:, v],
            lambda n: o_state.at[pl.ds(0, n), v],
        )

    forcing_start, forcing_wait, forcing_drain = exchange(
        1 + 4 * variables + RETURNED,
        lambda i: o_forcing.at[i],
        lambda j: g_forcing.at[:, :, azimuths(j), :],
        holder,
        block,
        nf,
        g_forcing,
        lambda n: o_forcing.at[pl.ds(0, n)],
    )
    base_start()

    def halo_copies(e, v):
        slot = e % 2
        rows = pl.ds(pl.multiple_of(v * pair, 8), pair)
        return [
            pltpu.make_async_remote_copy(
                src_ref=x_ref.at[slot, source, rows, :],
                dst_ref=x_ref.at[slot, target, rows, :],
                send_sem=halo_send.at[side, slot, v],
                recv_sem=halo_recv.at[side, slot, v],
                device_id=device,
                device_id_type=MESH,
            )
            for side, source, target, device in (
                (0, own_az, 0, right_id),
                (1, 1, own_az + 1, left_id),
            )
        ]

    def edge_copy(e, v):
        turn = e % 2
        return pltpu.make_async_remote_copy(
            src_ref=edge_out.at[turn, v],
            dst_ref=edge_in.at[turn, v],
            send_sem=edge_send.at[turn, v],
            recv_sem=edge_recv.at[turn, v],
            device_id=beyond,
            device_id_type=MESH,
        )

    def send_edges(e, v):
        slot = e % 2
        for ck in range(parts):
            edge_out[slot, v, pl.ds(ck, 1), :] = x_one[slot, ck, v, pl.ds(7 + span, 1), :]
            edge_out[slot, v, pl.ds(parts + ck, 1), :] = x_one[slot, ck, v, pl.ds(8, 1), :]
        edge_copy(e, v).start()

    for kk in range(per_dev):
        modes = lax.broadcasted_iota(jnp.int32, (nf, radii), 0) * per_dev + kk
        omega_ref[pl.ds(kk * nf, nf), :] = 0.5 * modes.astype(jnp.float32) / freqs
    load_state.wait()

    @pl.loop(0, variables)
    def _(v):
        send_edges(0, v)

    load_forcing.wait()

    @pl.loop(0, variables)
    def _(v):
        for ck in range(parts):
            b_one[ck, v] = MARCH_WEIGHT * x_one[0, ck, v, pl.ds(8, span), :] + b_one[ck, v]

    for table in tables:
        table.wait()
    position = plane * span + seat * share + lax.broadcasted_iota(jnp.int32, (share, radii), 0)
    phases = (lobe_ref[0] * position) % (span * planes)
    shape = 1.0 + 0.5 * jnp.cos(2.0 * math.pi * phases.astype(jnp.float32) / (span * planes))
    base_wait()

    def offer(station):
        wanted = station_ref[station]
        for v in range(variables):
            offered[station, v] = (BASE_SCALE * shape) * found[
                (wanted // stored) % fold, wanted % stored, v
            ]
            offers(station, v).start()

    def settle(station, gathered):
        ours = jnp.full((share, radii), station_ref[station] // (stored * fold)) == side
        for v in range(variables):
            offers(station, v).wait()
            s_w[station, v] = jnp.where(ours, offered[station, v], taken[station, v])
            if v < gathered:
                w_moves(station, v)[0]()

    offer(0)
    settle(0, variables)
    for station in range(1, STEPS):
        offer(station)

    def sweep_plane(e, v, w):
        src, dst = e % 2, (e + 1) % 2
        edge_copy(e, v).wait()
        for ck in range(parts):
            x_one[src, ck, v, pl.ds(7, 1), :] = edge_in[src, v, pl.ds(ck, 1), :]
            x_one[src, ck, v, pl.ds(8 + span, 1), :] = edge_in[src, v, pl.ds(parts + ck, 1), :]
        for kk in range(per_dev):
            rate = (me * per_dev + kk).astype(jnp.float32) * (0.5 / freqs)
            at = [c * per_dev + kk for c in range(2)]
            real, imag = [x_one[src, ck, v, pl.ds(8, span), :] for ck in at]
            mixing = (w * real - rate * imag, w * imag + rate * real)
            summed = [
                SIDE_WEIGHT
                * (x_one[src, ck, v, pl.ds(7, span), :] + x_one[src, ck, v, pl.ds(9, span), :])
                + b_one[ck, v]
                - mixed_in
                for ck, mixed_in in zip(at, mixing)
            ]
            q = times_right(jnp.concatenate(summed, axis=0), qt_ref[...])
            x_one[dst, at[0], v, pl.ds(8, span), :] = q[:span]
            x_one[dst, at[1], v, pl.ds(8, span), :] = q[span:]

    @pl.loop(0, SWEEPS + LAG * (variables - 1))
    def _(turn):
        @pl.loop(0, variables)
        def _(v):
            e = turn - LAG * v

            @pl.when((e >= 0) & (e < SWEEPS))
            def _():
                @pl.when(e == 0)
                def _():
                    w_moves(0, v)[1]()

                sweep_plane(e, v, plane_w[0, v])

                @pl.when((e < SWEEPS - 1) | (v < RETURNED))
                def _():
                    send_edges(e + 1, v)

                @pl.when(e == SWEEPS - 1)
                def _():
                    state_moves(v)[0]()

    for station in range(1, STEPS):
        settle(station, RETURNED)
    coefficient_start()

    def each_run(v, visit):
        for c in range(2):
            for kk in range(per_dev):
                start = pl.multiple_of(v * pair + (c * per_dev + kk) * nf, 8)
                visit(start, c * per_dev + kk)

    @pl.loop(0, variables)
    def _(v):
        state_moves(v)[1]()

        @pl.loop(0, own_az)
        def _(a):
            def unpack(start, ck):
                x_ref[0, a + 1, pl.ds(start, nf), :] = r_state[:, v, ck, a, :]

            each_run(v, unpack)

        for copy in halo_copies(0, v):
            copy.start()

    omega = omega_ref[...]

    def sweep_slabs(e, v):
        src, dst = e % 2, (e + 1) % 2
        rows = pl.ds(pl.multiple_of(v * pair, 8), pair)
        w = w_ref[v]
        summed = []
        for a in range(own_az):
            x = x_ref[src, a + 1, rows, :]
            beside = SIDE_WEIGHT * (x_ref[src, a, rows, :] + x_ref[src, a + 2, rows, :])
            real, imag = x[:freqs], x[freqs:]
            here_w = w[a : a + 1]
            mixing = [here_w * real - omega * imag, here_w * imag + omega * real]
            summed.append(beside + b_ref[a, rows, :] - jnp.concatenate(mixing, axis=0))
        q = times_right(jnp.concatenate(summed, axis=0), qt_ref[...])
        for a in range(own_az):
            x_ref[dst, a + 1, rows, :] = q[a * pair : (a + 1) * pair]

    def advect_slab(slot, a, final):
        x = x_ref[slot, a + 1]
        beside = 0.5 * (x_ref[slot, a + 2] - x_ref[slot, a])

        def lanes(y):
            return [y[v * pair : (v + 1) * pair] for v in range(variables)]

        both = jnp.concatenate(lanes(x) + lanes(beside), axis=1)
        in_time = times_stacked(inv_ref[...], both)
        u = [in_time[:, v * radii : (v + 1) * radii] for v in range(variables)]
        ua = [
            in_time[:, (variables + v) * radii : (variables + v + 1) * radii]
            for v in range(variables)
        ]
        radial = times_right(jnp.concatenate(u, axis=0), st_ref[...])
        ur = [radial[v * ntime : (v + 1) * ntime] for v in range(variables)]
        n = [u[1] * ur[v] + u[2] * ua[v] for v in range(variables)]
        n[0] = n[0] + u[0] * (ur[1] + ua[2])
        source = -ADVECT_SCALE * jnp.concatenate(n, axis=1)
        spectral = times_stacked(fwd_ref[...], source)
        for v in range(variables):
            forcing = spectral[:, v * radii : (v + 1) * radii]
            if final:
                for ck in range(parts):
                    o_forcing[:, ck, v, a, :] = forcing[ck * nf : (ck + 1) * nf]
            else:
                march = MARCH_WEIGHT * x[v * pair : (v + 1) * pair] + forcing
                b_ref[a, pl.ds(v * pair, pair), :] = march
                if v < RETURNED:
                    for ck in range(parts):
                        o_march[:, v, ck, a, :] = march[ck * nf : (ck + 1) * nf]

    def advect_all(e, final):
        slot = e % 2

        @pl.loop(1, own_az - 1)
        def _(a):
            advect_slab(slot, a, final)

        @pl.loop(0, variables)
        def _(v):
            for copy in halo_copies(e, v):
                copy.wait()

        @pl.loop(0, 2)
        def _(side):
            advect_slab(slot, side * (own_az - 1), final)

    advect_all(0, False)
    coefficient_wait()

    @pl.loop(0, SWEEPS * variables)
    def _(turn):
        e, v = turn // variables, turn % variables

        @pl.when(e > 0)
        def _():
            for copy in halo_copies(e, v):
                copy.wait()

        sweep_slabs(e, v)
        for copy in halo_copies(e + 1, v):
            copy.start()

        @pl.when(turn < nf)
        def _():
            for w in range(RETURNED):
                march_moves(w)[0](turn, turn + 1)

        @pl.when((e == SWEEPS - 1) & (v >= RETURNED))
        def _():
            @pl.loop(0, own_az)
            def _(a):
                def pack(start, ck):
                    o_state[:, v, ck, a, :] = x_ref[settled, a + 1, pl.ds(start, nf), :]

                each_run(v, pack)

            out_moves(v)[0]()

    advect_all(SWEEPS, True)
    forcing_start()
    for v in range(RETURNED):
        w_moves(1, v)[1]()
        march_moves(v)[1]()
        state_moves(v)[2]()

    @pl.loop(0, SWEEPS * RETURNED)
    def _(turn):
        e, v = SWEEPS + turn // RETURNED, turn % RETURNED
        sweep_plane(e, v, plane_w[1, v])

        @pl.when(e < 2 * SWEEPS - 1)
        def _():
            send_edges(e + 1, v)

    out_state = pltpu.make_async_copy(
        x_one.at[0, :, pl.ds(0, RETURNED), pl.ds(8, span), :],
        g_state.at[:, pl.ds(0, RETURNED), :, :],
        load_sem.at[0],
    )
    out_state.start()

    @pl.loop(RETURNED, variables)
    def _(v):
        out_moves(v)[1]()

    out_state.wait()
    forcing_wait()
    base_drain()
    for v in range(RETURNED):
        w_moves(1, v)[2]()
        march_moves(v)[2]()

    @pl.loop(0, variables)
    def _(v):
        w_moves(0, v)[2]()

    @pl.loop(RETURNED, variables)
    def _(v):
        state_moves(v)[2]()
        out_moves(v)[2]()

    forcing_drain()


LAG = 2
RETURNED = 1


def per_device_tiled(state_in, forcing_in, base_flow, station_index, lobe_count):
    _, per_dev, variables, span_az, radii = state_in.shape
    nf = lax.axis_size("freq")
    planes = lax.axis_size("plane")
    freqs = per_dev * nf
    ntime = 3 * freqs // 2
    own_az = span_az // nf
    stored = base_flow.shape[0]
    slopes, inverse_p = radial_tables(radii)
    mode_ids = (np.arange(nf)[None, :] * per_dev + np.arange(per_dev)[:, None]).reshape(-1)
    inverse, forward = transform_tables(mode_ids, freqs, ntime)
    dims = (nf, planes, own_az, variables, per_dev, radii, stored)
    parts = 2 * per_dev
    edge_rows = -(-2 * parts // 8) * 8
    anywhere = pl.BlockSpec(memory_space=pl.ANY)
    far = pl.BlockSpec(memory_space=pltpu.HBM)
    f32 = jnp.float32
    whole = (parts, variables, span_az, radii)
    slab = variables * 2 * freqs
    share = span_az // (nf // 2)
    moves = 2 + 4 * variables + RETURNED
    outs = pl.pallas_call(
        functools.partial(relay, dims),
        out_shape=jax.ShapeDtypeStruct((2, *whole), f32),
        in_specs=[pl.BlockSpec(memory_space=pltpu.SMEM)] + [far] * 8,
        out_specs=anywhere,
        scratch_shapes=[
            pltpu.VMEM((nf, variables, parts, own_az, radii), f32),
            pltpu.VMEM((nf // 2, stored, variables, share, radii), f32),
            pltpu.VMEM((STEPS, variables, share, radii), f32),
            pltpu.VMEM((STEPS, variables, share, radii), f32),
            pltpu.VMEM((STEPS, variables, share, radii), f32),
            pltpu.VMEM((STEPS, variables, span_az, radii), f32),
            pltpu.VMEM((2, parts, variables, span_az + 16, radii), f32),
            pltpu.VMEM(whole, f32),
            pltpu.VMEM((2, variables, edge_rows, radii), f32),
            pltpu.VMEM((2, variables, edge_rows, radii), f32),
            pltpu.VMEM((2, own_az + 2, slab, radii), f32),
            pltpu.VMEM((own_az, slab, radii), f32),
            pltpu.VMEM((variables, own_az, radii), f32),
            pltpu.VMEM((nf, variables, parts, own_az, radii), f32),
            pltpu.VMEM((nf, RETURNED, parts, own_az, radii), f32),
            pltpu.VMEM((nf, parts, variables, own_az, radii), f32),
            pltpu.SemaphoreType.DMA((moves,)),
            pltpu.SemaphoreType.DMA((moves,)),
            pltpu.SemaphoreType.DMA((STEPS, variables)),
            pltpu.SemaphoreType.DMA((STEPS, variables)),
            pltpu.SemaphoreType.DMA((share // own_az,)),
            pltpu.SemaphoreType.DMA((2,)),
            pltpu.SemaphoreType.DMA((2, 2, variables)),
            pltpu.SemaphoreType.DMA((2, 2, variables)),
            pltpu.SemaphoreType.DMA((2, variables)),
            pltpu.SemaphoreType.DMA((2, variables)),
            pltpu.SemaphoreType.DMA((2,)),
            pltpu.VMEM((freqs, radii), f32),
            pltpu.VMEM((2 * radii, 2 * radii), jnp.bfloat16),
            pltpu.VMEM((2 * radii, 2 * radii), jnp.bfloat16),
            pltpu.VMEM((2 * ntime, 4 * freqs), jnp.bfloat16),
            pltpu.VMEM((4 * freqs, 2 * ntime), jnp.bfloat16),
            pltpu.SemaphoreType.DMA((5,)),
            pltpu.SMEM(station_index.shape, jnp.int32),
        ],
        compiler_params=pltpu.CompilerParams(
            collective_id=0, has_side_effects=True, vmem_limit_bytes=32 * 1024 * 1024
        ),
    )(
        lobe_count,
        *[
            pltpu.with_memory_space_constraint(x, pltpu.HBM)
            for x in (
                station_index,
                state_in.reshape(whole),
                base_flow,
                forcing_in.reshape(whole),
                right_table(inverse_p.T),
                right_table(slopes.T),
                stacked_table(inverse.transpose(2, 0, 1).reshape(ntime, 2 * freqs)),
                stacked_table(forward.reshape(2 * freqs, ntime)),
            )
        ],
    )
    return tuple(outs[n].reshape(state_in.shape) for n in range(2))


def per_device_any(*args):
    nf = lax.axis_size("freq")
    tiles = args[0].shape[3] % (8 * nf) == 0 and nf % 2 == 0 and lax.axis_size("plane") == 2
    return (per_device_tiled if tiles else per_device)(*args)


MESH = pl.DeviceIdType.MESH


def solution(mesh):
    return jax.shard_map(
        per_device_any,
        mesh=mesh,
        in_specs=(
            P(None, "freq", None, "plane", None),
            P(None, "freq", None, "plane", None),
            P("freq", None, "plane", None),
            P(),
            P(),
        ),
        out_specs=(P(None, "freq", None, "plane", None), P(None, "freq", None, "plane", None)),
        check_vma=False,
    )
```

```python
import functools
import math

import jax
import jax.numpy as jnp
import numpy as np
from jax import lax
from jax.experimental import pallas as pl
from jax.experimental.pallas import tpu as pltpu
from jax.sharding import PartitionSpec as P

SWEEPS = 4
STEPS = 2


SIDE_WEIGHT = 1.25
MARCH_WEIGHT = 4.0
DIAG_SHIFT = 4.0
ADVECT_SCALE = 0.5
BASE_SCALE = 0.5


def radial_tables(radius_count):
    indices = np.arange(radius_count)
    angles = math.pi * indices / (radius_count - 1)
    nodes = np.cos(angles)
    weights = np.where((indices == 0) | (indices == radius_count - 1), 2.0, 1.0)
    parity = 1.0 - 2.0 * ((indices[:, None] + indices[None, :]) % 2)
    offdiag = indices[:, None] != indices[None, :]
    spacing = np.where(offdiag, nodes[:, None] - nodes[None, :], 1.0)
    entries = np.where(offdiag, weights[:, None] / weights[None, :] * parity / spacing, 0.0)
    entries = entries - np.diag(entries.sum(axis=1))
    slopes = np.sin(angles)[:, None] * entries / (radius_count - 1)
    system = slopes.T @ slopes + DIAG_SHIFT * np.eye(radius_count)
    return slopes.astype(np.float32), np.linalg.inv(system).astype(np.float32)


def transform_tables(mode_ids, freqs, ntime):
    time_ids = np.arange(ntime)
    angles = 2.0 * math.pi * (mode_ids[:, None] * time_ids[None, :] % ntime) / ntime
    stacked = np.stack([np.cos(angles), -np.sin(angles)])
    return (
        (stacked / math.sqrt(freqs)).astype(np.float32),
        (stacked / math.sqrt(ntime)).astype(np.float32),
    )


def chevron(lobe_count, azimuths, start_az, total_az):
    position = start_az + jnp.arange(azimuths)
    phases = lobe_count[0] * position % total_az
    return 1.0 + 0.5 * jnp.cos(2.0 * math.pi * phases.astype(jnp.float32) / total_az)


def halves(x):
    high = x.astype(jnp.bfloat16)
    return high, (x - high.astype(jnp.float32)).astype(jnp.bfloat16)


def right_table(table):
    high, low = np_halves(table)
    return jnp.asarray(np.tile(np.concatenate([high, low], axis=1), (2, 1)))


def left_table(table):
    high, low = np_halves(table)
    return jnp.asarray(np.concatenate([high, high, low, low], axis=1))


def np_halves(table):
    high = table.astype(jnp.bfloat16)
    return high, (table - high.astype(np.float32)).astype(jnp.bfloat16)


def times_right(x, table):
    width = table.shape[1] // 2
    y = jnp.dot(jnp.concatenate(halves(x), axis=1), table, preferred_element_type=jnp.float32)
    return y[:, :width] + y[:, width:]


def times_left(table, x):
    high, low = halves(x)
    return jnp.dot(
        table,
        jnp.concatenate([high, low, high, low], axis=0),
        preferred_element_type=jnp.float32,
    )


def ring_of(f, p, nf, planes):
    at = f
    if nf % 4 == 0:
        high = nf // 4
        z, y, x = f // 4, (f // 2) % 2, f % 2
        column = 2 * y + (x + y) % 2
        at = column * high + z + (column % 2) * (high - 1 - 2 * z)
    return at * planes + p


def device_of(g, nf, planes):
    at = g // planes
    f = at
    if nf % 4 == 0:
        high = nf // 4
        column, z = at // high, at % high
        z = z + (column % 2) * (high - 1 - 2 * z)
        y = column // 2
        f = 4 * z + 2 * y + (column + y) % 2
    return f, g % planes


def march(
    dims,
    station_ref,
    shape_ref,
    rate_ref,
    state_ref,
    s_base,
    forcing_ref,
    far_omega,
    far_qt,
    far_st,
    far_inv,
    far_fwd,
    g_state,
    g_forcing,
    r_state,
    r_base,
    s_state,
    s_w,
    r_w,
    plane_w,
    x_one,
    b_one,
    edge_out,
    edge_in,
    x_ref,
    b_ref,
    f_ref,
    w_ref,
    o_state,
    o_forcing,
    send_sem,
    recv_sem,
    own_sem,
    halo_send,
    halo_recv,
    edge_send,
    edge_recv,
    load_sem,
    omega_ref,
    qt_ref,
    st_ref,
    inv_ref,
    fwd_ref,
    table_sem,
):
    nf, planes, own_az, variables, per_dev, radii, stored, rows, base_rows, w_rows = dims
    freqs = nf * per_dev
    span = nf * own_az
    runs = 2 * per_dev * variables
    ntime = inv_ref.shape[0]
    half = variables * freqs
    me = lax.axis_index("freq")
    plane = lax.axis_index("plane")
    ring = nf * planes
    here = ring_of(me, plane, nf, planes)
    part, block = here // nf, here % nf

    def named(device):
        return {"freq": device[0], "plane": device[1]}

    right_id = named(device_of((here + 1) % ring, nf, planes))
    left_id = named(device_of((here + ring - 1) % ring, nf, planes))
    barrier = pltpu.get_barrier_semaphore()

    @pl.loop(1, ring)
    def _(d):
        other = (me * planes + plane + d) % ring
        pl.semaphore_signal(
            barrier,
            inc=1,
            device_id={"freq": other // planes, "plane": other % planes},
            device_id_type=MESH,
        )

    beyond = {"freq": me, "plane": (plane + 1) % planes}
    behind = {"freq": me, "plane": (plane + planes - 1) % planes}
    load_state = pltpu.make_async_copy(state_ref, x_one.at[0, :, pl.ds(8, span), :], load_sem.at[0])
    load_forcing = pltpu.make_async_copy(forcing_ref, b_one, load_sem.at[1])
    load_state.start()
    load_forcing.start()
    tables = [
        pltpu.make_async_copy(far, near, table_sem.at[i])
        for i, (far, near) in enumerate(
            (
                (far_omega, omega_ref),
                (far_qt, qt_ref),
                (far_st, st_ref),
                (far_inv, inv_ref),
                (far_fwd, fwd_ref),
            )
        )
    ]
    for table in tables:
        table.start()
    pl.semaphore_wait(barrier, ring - 1)

    def owner(i):
        return device_of(plane * nf + i, nf, planes)

    def holder(i):
        return i, part

    def is_me(device):
        return (device[0] == me) & (device[1] == plane)

    def exchange(k, source, landing, target, origin, pick, mine, size, first):
        def rows_of(ref, i):
            return ref.at[pl.ds(pl.multiple_of(i * size, 8), size), :]

        def copy(i):
            return pltpu.make_async_remote_copy(
                src_ref=rows_of(source, pick(i)),
                dst_ref=rows_of(landing, mine),
                send_sem=send_sem.at[k, i],
                recv_sem=recv_sem.at[k, mine],
                device_id=named(target(i)),
                device_id_type=MESH,
            )

        def arrival(i):
            return pltpu.make_async_remote_copy(
                src_ref=rows_of(landing, i),
                dst_ref=rows_of(landing, i),
                send_sem=send_sem.at[k, i],
                recv_sem=recv_sem.at[k, i],
                device_id=named(origin(i)),
                device_id_type=MESH,
            )

        def own(i):
            return pltpu.make_async_copy(
                rows_of(source, pick(i)), rows_of(landing, mine), own_sem.at[k]
            )

        @pl.loop(0, nf)
        def _(d):
            i = (d + me) % nf
            stays = is_me(target(i))

            @pl.when(stays)
            def _():
                if first:
                    own(i).start()
                else:
                    own(i).wait()

            @pl.when(jnp.logical_not(stays))
            def _():
                if first:
                    copy(i).start()
                else:
                    copy(i).wait_send()

            if not first:

                @pl.when(jnp.logical_not(is_me(origin(i))))
                def _():
                    arrival(i).wait_recv()

    def same(i):
        return i

    base_args = (1, s_base, r_base, owner, holder, same, me, base_rows)
    state_args = (0, s_state, r_state, owner, holder, same, me, rows)
    w_args = (2, s_w, r_w, holder, owner, lambda i: 0, block, w_rows)
    out_state_args = (3, o_state, g_state, holder, owner, same, block, rows)
    out_forcing_args = (4, o_forcing, g_forcing, holder, owner, same, block, rows)
    exchange(*base_args, True)

    def halo_copies(e):
        slot = e % 2
        return (
            pltpu.make_async_remote_copy(
                src_ref=x_ref.at[slot, own_az],
                dst_ref=x_ref.at[slot, 0],
                send_sem=halo_send.at[0, e],
                recv_sem=halo_recv.at[0, e],
                device_id=right_id,
                device_id_type=MESH,
            ),
            pltpu.make_async_remote_copy(
                src_ref=x_ref.at[slot, 1],
                dst_ref=x_ref.at[slot, own_az + 1],
                send_sem=halo_send.at[1, e],
                recv_sem=halo_recv.at[1, e],
                device_id=left_id,
                device_id_type=MESH,
            ),
        )

    def place(a, c, v, kk):
        return ((c * variables + v) * per_dev + kk) * nf

    def packed_row(a, c, v, kk):
        return ((c * per_dev + kk) * variables + v) * own_az + a

    def each_run(visit):
        @pl.loop(0, own_az)
        def _(a):
            for c in range(2):
                for v in range(variables):
                    for kk in range(per_dev):
                        visit(a, place(a, c, v, kk), packed_row(a, c, v, kk))

    def in_row(a, c, v, kk):
        return ((c * per_dev + kk) * variables + v) * own_az + a

    def edge_copies(e):
        return [
            pltpu.make_async_remote_copy(
                src_ref=edge_out.at[e, side],
                dst_ref=edge_in.at[e, side],
                send_sem=edge_send.at[side, e],
                recv_sem=edge_recv.at[side, e],
                device_id=target,
                device_id_type=MESH,
            )
            for side, target in ((0, beyond), (1, behind))
        ]

    def send_edges(slot, e):
        for m in range(runs):
            edge_out[e, 0, pl.ds(m, 1), :] = x_one[slot, m, pl.ds(7 + span, 1), :]
            edge_out[e, 1, pl.ds(m, 1), :] = x_one[slot, m, pl.ds(8, 1), :]
        for copy in edge_copies(e):
            copy.start()

    for table in tables:
        table.wait()
    load_state.wait()
    send_edges(0, 0)
    load_forcing.wait()

    @pl.loop(0, runs)
    def _(m):
        b_one[m] = MARCH_WEIGHT * x_one[0, m, pl.ds(8, span), :] + b_one[m]

    exchange(*base_args, False)
    for station in range(STEPS):
        wanted = station_ref[station]

        @pl.loop(0, own_az)
        def _(a):
            for v in range(variables):
                scaled = (BASE_SCALE * shape_ref[a]) * r_base[
                    pl.ds(
                        (wanted // stored) * base_rows
                        + ((wanted % stored) * variables + v) * own_az
                        + a,
                        1,
                    ),
                    :,
                ]
                if station == 0:
                    s_w[pl.ds(v * own_az + a, 1), :] = scaled
                else:
                    w_ref[(station - 1) * own_az + a, pl.ds(v, 1), :] = scaled

        if station == 0:
            exchange(*w_args, True)
    exchange(*w_args, False)

    @pl.loop(0, nf)
    def _(j):
        for v in range(variables):
            plane_w[v, pl.ds(j * own_az, own_az), :] = r_w[pl.ds(j * w_rows + v * own_az, own_az), :]

    @pl.loop(0, SWEEPS)
    def _(e):
        src, dst = e % 2, (e + 1) % 2
        for copy in edge_copies(e):
            copy.wait()
        for m in range(runs):
            x_one[src, m, pl.ds(7, 1), :] = edge_in[e, 0, pl.ds(m, 1), :]
            x_one[src, m, pl.ds(8 + span, 1), :] = edge_in[e, 1, pl.ds(m, 1), :]
        for kk in range(per_dev):
            rate = rate_ref[kk]

            @pl.loop(0, variables)
            def _(v):
                w = plane_w[v]
                at = [(c * per_dev + kk) * variables + v for c in range(2)]
                real, imag = [x_one[src, m, pl.ds(8, span), :] for m in at]
                mixing = (w * real - rate * imag, w * imag + rate * real)
                summed = [
                    SIDE_WEIGHT
                    * (x_one[src, m, pl.ds(7, span), :] + x_one[src, m, pl.ds(9, span), :])
                    + b_one[m]
                    - mixed
                    for m, mixed in zip(at, mixing)
                ]
                q = times_right(jnp.concatenate(summed, axis=0), qt_ref[...])
                x_one[dst, at[0], pl.ds(8, span), :] = q[:span]
                x_one[dst, at[1], pl.ds(8, span), :] = q[span:]

        @pl.when(e < SWEEPS - 1)
        def _():
            send_edges(dst, e + 1)

    settled = SWEEPS % 2

    @pl.loop(0, nf)
    def _(j):
        for m in range(runs):
            s_state[pl.ds(j * rows + m * own_az, own_az), :] = x_one[
                settled, m, pl.ds(8 + j * own_az, own_az), :
            ]

    exchange(*state_args, True)
    exchange(*state_args, False)

    def unpack_state(a, start, row):
        x_ref[0, a + 1, pl.ds(start, nf), :] = r_state[pl.ds(row, nf, stride=rows), :]

    each_run(unpack_state)
    for copy in halo_copies(0):
        copy.start()
    omega = omega_ref[...][None]
    flat = (2 * half, radii)
    cube = (variables, freqs, radii)

    def sweep_slab(src, dst, a, station):
        x = x_ref[src, a + 1]
        beside = SIDE_WEIGHT * (x_ref[src, a] + x_ref[src, a + 2]) + b_ref[a]
        real, imag = x[:half].reshape(cube), x[half:].reshape(cube)
        w = w_ref[(station - 1) * own_az + a][:variables][:, None, :]
        mixing = jnp.concatenate([w * real - omega * imag, w * imag + omega * real], axis=0)
        summed = beside - mixing.reshape(flat)
        x_ref[dst, a + 1] = times_right(summed, qt_ref[...])

    def advect_slab(slot, a, final):
        x = x_ref[slot, a + 1]
        beside = 0.5 * (x_ref[slot, a + 2] - x_ref[slot, a])

        def lanes(y):
            return [
                jnp.concatenate(
                    [
                        y[v * freqs : (v + 1) * freqs],
                        y[half + v * freqs : half + (v + 1) * freqs],
                    ],
                    axis=0,
                )
                for v in range(variables)
            ]

        both = jnp.concatenate(lanes(x) + lanes(beside), axis=1)
        in_time = times_left(inv_ref[...], both)
        u = [in_time[:, v * radii : (v + 1) * radii] for v in range(variables)]
        ua = [
            in_time[:, (variables + v) * radii : (variables + v + 1) * radii]
            for v in range(variables)
        ]
        radial = times_right(jnp.concatenate(u, axis=0), st_ref[...])
        ur = [radial[v * ntime : (v + 1) * ntime] for v in range(variables)]
        n = [u[1] * ur[v] + u[2] * ua[v] for v in range(variables)]
        n[0] = n[0] + u[0] * (ur[1] + ua[2])
        source = -ADVECT_SCALE * jnp.concatenate(n, axis=1)
        spectral = times_left(fwd_ref[...], source)
        forcing = jnp.concatenate(
            [
                spectral[c * freqs : (c + 1) * freqs, v * radii : (v + 1) * radii]
                for c in range(2)
                for v in range(variables)
            ],
            axis=0,
        )
        if final:
            f_ref[a] = forcing
        else:
            b_ref[a] = MARCH_WEIGHT * x + forcing

    def advect_all(slot, e, final):
        @pl.loop(1, own_az - 1)
        def _(a):
            advect_slab(slot, a, final)

        for copy in halo_copies(e):
            copy.wait()
        advect_slab(slot, 0, final)
        if own_az > 1:
            advect_slab(slot, own_az - 1, final)

    advect_all(0, 0, False)
    for station in range(1, STEPS):

        @pl.loop(0, SWEEPS)
        def _(sweep):
            e = (station - 1) * SWEEPS + sweep
            src, dst = e % 2, (e + 1) % 2

            @pl.when(sweep > 0)
            def _():
                for copy in halo_copies(e):
                    copy.wait()

            sweep_slab(src, dst, 0, station)
            if own_az > 1:
                sweep_slab(src, dst, own_az - 1, station)
            for copy in halo_copies(e + 1):
                copy.start()

            @pl.loop(1, own_az - 1)
            def _(a):
                sweep_slab(src, dst, a, station)

        last = station * SWEEPS
        slot = last % 2
        final = station == STEPS - 1
        if final:

            def pack_state(a, start, row):
                o_state[pl.ds(row, nf, stride=rows), :] = x_ref[slot, a + 1, pl.ds(start, nf), :]

            each_run(pack_state)
            exchange(*out_state_args, True)

        advect_all(slot, last, final)

    def pack_forcing(a, start, row):
        o_forcing[pl.ds(row, nf, stride=rows), :] = f_ref[a, pl.ds(start, nf), :]

    each_run(pack_forcing)
    exchange(*out_forcing_args, True)
    exchange(*out_state_args, False)
    exchange(*out_forcing_args, False)


def per_device(state_in, forcing_in, base_flow, station_index, lobe_count):
    _, per_dev, variables, span_az, radii = state_in.shape
    nf = lax.axis_size("freq")
    planes = lax.axis_size("plane")
    freqs = per_dev * nf
    ntime = 3 * freqs // 2
    own_az = span_az // nf
    stored = base_flow.shape[0]
    slopes, inverse_p = radial_tables(radii)
    mode_ids = (np.arange(nf)[None, :] * per_dev + np.arange(per_dev)[:, None]).reshape(-1)
    inverse, forward = transform_tables(mode_ids, freqs, ntime)
    omegas = np.broadcast_to((0.5 * mode_ids / freqs).astype(np.float32)[:, None], (freqs, radii))
    plane = lax.axis_index("plane")
    here = ring_of(lax.axis_index("freq"), plane, nf, planes)
    shape_az = chevron(lobe_count, own_az, here * own_az, span_az * planes)

    def padded_rows(count):
        return -(-count // 8) * 8

    def chunks(x, size):
        x = x.reshape(-1, nf, own_az, radii).transpose(1, 0, 2, 3).reshape(nf, -1, radii)
        x = jnp.pad(x, ((0, 0), (0, size - x.shape[1]), (0, 0)))
        return x.reshape(nf * size, radii)

    count = 2 * per_dev * variables * own_az
    rows = padded_rows(count)
    base_rows = padded_rows(stored * variables * own_az)
    w_rows = padded_rows(variables * own_az)
    dims = (nf, planes, own_az, variables, per_dev, radii, stored, rows, base_rows, w_rows)
    half = variables * freqs
    exchanges = (STEPS - 1) * SWEEPS + 1
    runs = 2 * per_dev * variables
    edge_rows = padded_rows(runs)
    first_mode = lax.axis_index("freq") * per_dev
    rates = 0.5 * (first_mode + jnp.arange(per_dev)).astype(jnp.float32) / freqs
    smem = pl.BlockSpec(memory_space=pltpu.SMEM)
    anywhere = pl.BlockSpec(memory_space=pl.ANY)
    packed = (nf * rows, radii)
    f32 = jnp.float32
    outs = pl.pallas_call(
        functools.partial(march, dims),
        out_shape=[jax.ShapeDtypeStruct(packed, f32)] * 2,
        in_specs=[smem, smem, smem, anywhere, anywhere, anywhere] + [anywhere] * 5,
        out_specs=[anywhere, anywhere],
        scratch_shapes=[
            pltpu.VMEM(packed, f32),
            pltpu.VMEM((nf * base_rows, radii), f32),
            pltpu.VMEM(packed, f32),
            pltpu.VMEM((w_rows, radii), f32),
            pltpu.VMEM((nf * w_rows, radii), f32),
            pltpu.VMEM((variables, span_az, radii), f32),
            pltpu.VMEM((2, runs, span_az + 16, radii), f32),
            pltpu.VMEM((runs, span_az, radii), f32),
            pltpu.VMEM((SWEEPS, 2, edge_rows, radii), f32),
            pltpu.VMEM((SWEEPS, 2, edge_rows, radii), f32),
            pltpu.VMEM((2, own_az + 2, 2 * half, radii), f32),
            pltpu.VMEM((own_az, 2 * half, radii), f32),
            pltpu.VMEM((own_az, 2 * half, radii), f32),
            pltpu.VMEM(((STEPS - 1) * own_az, padded_rows(variables), radii), f32),
            pltpu.VMEM(packed, f32),
            pltpu.VMEM(packed, f32),
            pltpu.SemaphoreType.DMA((5, nf)),
            pltpu.SemaphoreType.DMA((5, nf)),
            pltpu.SemaphoreType.DMA((5,)),
            pltpu.SemaphoreType.DMA((2, exchanges)),
            pltpu.SemaphoreType.DMA((2, exchanges)),
            pltpu.SemaphoreType.DMA((2, SWEEPS)),
            pltpu.SemaphoreType.DMA((2, SWEEPS)),
            pltpu.SemaphoreType.DMA((2,)),
            pltpu.VMEM((freqs, radii), f32),
            pltpu.VMEM((2 * radii, 2 * radii), jnp.bfloat16),
            pltpu.VMEM((2 * radii, 2 * radii), jnp.bfloat16),
            pltpu.VMEM((ntime, 8 * freqs), jnp.bfloat16),
            pltpu.VMEM((2 * freqs, 4 * ntime), jnp.bfloat16),
            pltpu.SemaphoreType.DMA((5,)),
        ],
        compiler_params=pltpu.CompilerParams(
            collective_id=0, has_side_effects=True, vmem_limit_bytes=63_000 * 1024
        ),
    )(
        station_index,
        shape_az,
        rates,
        state_in.reshape(runs, span_az, radii),
        chunks(base_flow, base_rows),
        forcing_in.reshape(runs, span_az, radii),
        jnp.asarray(omegas),
        right_table(inverse_p.T),
        right_table(slopes.T),
        left_table(inverse.transpose(2, 0, 1).reshape(ntime, 2 * freqs)),
        left_table(forward.reshape(2 * freqs, ntime)),
    )

    return tuple(finish(y, nf, per_dev, variables, own_az, radii, rows, count) for y in outs)


def finish(y, nf, per_dev, variables, own_az, radii, rows, count):
    y = y.reshape(nf, rows, radii)[:, :count].reshape(nf, -1, own_az, radii)
    return y.transpose(1, 0, 2, 3).reshape(2, per_dev, variables, nf * own_az, radii)


def stacked_table(table):
    high, low = np_halves(table)
    return jnp.asarray(np.tile(np.concatenate([high, low], axis=0), (1, 2)))


def times_stacked(table, x):
    height = table.shape[0] // 2
    y = jnp.dot(table, jnp.concatenate(halves(x), axis=0), preferred_element_type=jnp.float32)
    return y[:height] + y[height:]


def relay(
    dims,
    lobe_ref,
    far_station,
    state_ref,
    base_ref,
    forcing_ref,
    far_qt,
    far_st,
    far_inv,
    far_fwd,
    g_both,
    r_state,
    found_first,
    found_rest,
    offered,
    taken,
    s_w,
    plane_w,
    x_one,
    b_one,
    edge_out,
    edge_in,
    x_ref,
    b_ref,
    w_ref,
    o_state,
    o_march,
    o_forcing,
    send_sem,
    recv_sem,
    offer_send,
    offer_recv,
    w_send,
    w_recv,
    halo_send,
    halo_recv,
    edge_send,
    edge_recv,
    load_sem,
    omega_ref,
    qt_ref,
    st_ref,
    inv_ref,
    fwd_ref,
    table_sem,
    station_ref,
):
    nf, planes, own_az, variables, per_dev, radii, stored = dims
    g_state, g_forcing = g_both.at[0], g_both.at[1]
    freqs = nf * per_dev
    span = nf * own_az
    parts = 2 * per_dev
    ntime = inv_ref.shape[0] // 2
    pair = 2 * freqs
    me = lax.axis_index("freq")
    plane = lax.axis_index("plane")
    ring = nf * planes
    here = ring_of(me, plane, nf, planes)
    part, block = here // nf, here % nf
    fold = nf // 2
    side, seat = me // fold, me % fold
    share = span // fold
    blocks = share // own_az

    def mate(i):
        return side * fold + i, plane


    def named(device):
        return {"freq": device[0], "plane": device[1]}

    def is_me(device):
        return (device[0] == me) & (device[1] == plane)

    right_id = named(device_of((here + 1) % ring, nf, planes))
    left_id = named(device_of((here + ring - 1) % ring, nf, planes))
    barrier = pltpu.get_barrier_semaphore()

    def greet(device):
        pl.semaphore_signal(barrier, inc=1, device_id=device, device_id_type=MESH)

    @pl.loop(1, fold)
    def _(d):
        greet(named(mate((seat + d) % fold)))

    beyond = {"freq": me, "plane": (plane + 1) % planes}
    across = {"freq": (1 - side) * fold + seat, "plane": plane}
    greet(beyond)
    greet(across)
    load_state = pltpu.make_async_copy(
        state_ref, x_one.at[0, :, :, pl.ds(8, span), :], load_sem.at[0]
    )
    load_forcing = pltpu.make_async_copy(forcing_ref, b_one, load_sem.at[1])
    load_state.start()
    load_forcing.start()
    tables = [
        pltpu.make_async_copy(far, near, table_sem.at[i])
        for i, (far, near) in enumerate(
            (
                (far_station, station_ref),
                (far_qt, qt_ref),
                (far_st, st_ref),
                (far_inv, inv_ref),
                (far_fwd, fwd_ref),
            )
        )
    ]
    for table in tables:
        table.start()
    pl.semaphore_wait(barrier, fold + 1)

    def owner(i):
        return device_of(plane * nf + i, nf, planes)

    def holder(i):
        return i, part

    def azimuths(i):
        return pl.ds(pl.multiple_of(i * own_az, 8), own_az)

    def exchange(k, piece, landing, target, mine, count, landed, sent):
        def copy(i):
            return pltpu.make_async_remote_copy(
                src_ref=piece(i),
                dst_ref=landing(mine),
                send_sem=send_sem.at[k],
                recv_sem=recv_sem.at[k],
                device_id=named(target(i)),
                device_id_type=MESH,
            )

        def start(first=0, stop=count):
            @pl.loop(first, stop)
            def _(d):
                i = (d + me) % count
                stays = is_me(target(i))

                @pl.when(stays)
                def _():
                    pltpu.make_async_copy(piece(i), landing(mine), recv_sem.at[k]).start()

                @pl.when(jnp.logical_not(stays))
                def _():
                    copy(i).start()

        def all_of(ref):
            return pltpu.make_async_remote_copy(
                src_ref=ref,
                dst_ref=ref,
                send_sem=send_sem.at[k],
                recv_sem=recv_sem.at[k],
                device_id=beyond,
                device_id_type=MESH,
            )

        def wait():
            all_of(landed).wait_recv()

        def drain():
            if count < nf:
                all_of(sent(count - 1)).wait_send()
            else:

                @pl.when(part == plane)
                def _():
                    all_of(sent(count - 1)).wait_send()

                @pl.when(part != plane)
                def _():
                    all_of(sent(count)).wait_send()

        return start, wait, drain

    def chunk(i):
        return pl.ds(pl.multiple_of(i * share, 8), share)

    def base_moves(n):
        some = (pl.ds(0, FIRST), pl.ds(FIRST, variables - FIRST))[n]
        found = (found_first, found_rest)[n]
        return exchange(
            n * (2 + 4 * variables + RETURNED),
            lambda i: base_ref.at[:, some, chunk(i), :],
            lambda j: found.at[j],
            mate,
            seat,
            fold,
            found,
            lambda count: found.at[pl.ds(0, count)],
        )

    def offers(station, v):
        return pltpu.make_async_remote_copy(
            src_ref=offered.at[station, v],
            dst_ref=taken.at[station, v],
            send_sem=offer_send.at[station, v],
            recv_sem=offer_recv.at[station, v],
            device_id=across,
            device_id_type=MESH,
        )

    def w_moves(station, v):
        return exchange(
            1 + station * variables + v,
            lambda i: s_w.at[station, v],
            lambda j: plane_w.at[station, v, chunk(j), :],
            mate,
            seat,
            fold,
            plane_w.at[station, v],
            lambda n: plane_w.at[station, v, pl.ds(0, n * share), :],
        )

    def coefficient_copies():
        for j in range(blocks):
            target = device_of(plane * nf + seat * blocks + j, nf, planes)
            source = s_w.at[1, :, pl.ds(j * own_az, own_az), :]
            remote = pltpu.make_async_remote_copy(
                src_ref=source,
                dst_ref=w_ref,
                send_sem=w_send.at[j],
                recv_sem=w_recv.at[0],
                device_id=named(target),
                device_id_type=MESH,
            )
            local = pltpu.make_async_copy(source, w_ref, w_recv.at[1])
            near = target[0] // fold == side
            yield remote, local, near & jnp.logical_not(is_me(target)), near & is_me(target)

    def coefficient_start():
        for remote, local, away, home in coefficient_copies():
            pl.when(away)(remote.start)
            pl.when(home)(local.start)

    def coefficient_wait():
        for remote, local, away, home in coefficient_copies():
            pl.when(away)(remote.wait_send)
            pl.when(home)(local.wait)
        source = (side * fold + block // blocks, part)
        arrived = pltpu.make_async_remote_copy(
            src_ref=w_ref,
            dst_ref=w_ref,
            send_sem=w_send.at[0],
            recv_sem=w_recv.at[0],
            device_id=named(source),
            device_id_type=MESH,
        )
        pl.when(jnp.logical_not(is_me(source)))(arrived.wait_recv)

    settled = SWEEPS % 2

    def state_moves(v):
        return exchange(
            1 + 2 * variables + v,
            lambda i: x_one.at[
                settled, :, v, pl.ds(pl.multiple_of(8 + i * own_az, 8), own_az), :
            ],
            lambda j: r_state.at[j, v],
            owner,
            me,
            nf,
            r_state.at[:, v],
            lambda n: r_state.at[pl.ds(0, n), v],
        )

    def march_moves(v):
        return exchange(
            1 + 4 * variables + v,
            lambda i: o_march.at[i, v],
            lambda j: b_one.at[:, v, azimuths(j), :],
            holder,
            block,
            nf,
            b_one.at[:, v],
            lambda n: o_march.at[pl.ds(0, n), v],
        )

    def out_moves(v):
        return exchange(
            1 + 3 * variables + v,
            lambda i: o_state.at[i, v],
            lambda j: g_state.at[:, v, azimuths(j), :],
            holder,
            block,
            nf,
            g_state.at[:, v],
            lambda n: o_state.at[pl.ds(0, n), v],
        )

    forcing_start, forcing_wait, forcing_drain = exchange(
        1 + 4 * variables + RETURNED,
        lambda i: o_forcing.at[i],
        lambda j: g_forcing.at[:, :, azimuths(j), :],
        holder,
        block,
        nf,
        g_forcing,
        lambda n: o_forcing.at[pl.ds(0, n)],
    )
    for n in range(2):
        base_moves(n)[0]()

    def halo_copies(e, v):
        slot = e % 2
        rows = pl.ds(pl.multiple_of(v * pair, 8), pair)
        return [
            pltpu.make_async_remote_copy(
                src_ref=x_ref.at[slot, source, rows, :],
                dst_ref=x_ref.at[slot, target, rows, :],
                send_sem=halo_send.at[side, slot, v],
                recv_sem=halo_recv.at[side, slot, v],
                device_id=device,
                device_id_type=MESH,
            )
            for side, source, target, device in (
                (0, own_az, 0, right_id),
                (1, 1, own_az + 1, left_id),
            )
        ]

    def edge_copy(e, v):
        turn = e % 2
        return pltpu.make_async_remote_copy(
            src_ref=edge_out.at[turn, v],
            dst_ref=edge_in.at[turn, v],
            send_sem=edge_send.at[turn, v],
            recv_sem=edge_recv.at[turn, v],
            device_id=beyond,
            device_id_type=MESH,
        )

    def send_edges(e, v):
        slot = e % 2
        for ck in range(parts):
            edge_out[slot, v, pl.ds(ck, 1), :] = x_one[slot, ck, v, pl.ds(7 + span, 1), :]
            edge_out[slot, v, pl.ds(parts + ck, 1), :] = x_one[slot, ck, v, pl.ds(8, 1), :]
        edge_copy(e, v).start()

    for kk in range(per_dev):
        modes = lax.broadcasted_iota(jnp.int32, (nf, radii), 0) * per_dev + kk
        omega_ref[pl.ds(kk * nf, nf), :] = 0.5 * modes.astype(jnp.float32) / freqs
    load_state.wait()

    @pl.loop(0, variables)
    def _(v):
        send_edges(0, v)

    load_forcing.wait()

    @pl.loop(0, variables)
    def _(v):
        for ck in range(parts):
            b_one[ck, v] = MARCH_WEIGHT * x_one[0, ck, v, pl.ds(8, span), :] + b_one[ck, v]

    for table in tables:
        table.wait()
    position = plane * span + seat * share + lax.broadcasted_iota(jnp.int32, (share, radii), 0)
    phases = (lobe_ref[0] * position) % (span * planes)
    shape = 1.0 + 0.5 * jnp.cos(2.0 * math.pi * phases.astype(jnp.float32) / (span * planes))
    def offer(station, first, stop):
        wanted = station_ref[station]
        for v in range(first, stop):
            found, at = (found_first, v) if v < FIRST else (found_rest, v - FIRST)
            offered[station, v] = (BASE_SCALE * shape) * found[
                (wanted // stored) % fold, wanted % stored, at
            ]
            offers(station, v).start()

    def settle(station, gathered):
        ours = jnp.full((share, radii), station_ref[station] // (stored * fold)) == side
        for v in range(variables):
            offers(station, v).wait()
            s_w[station, v] = jnp.where(ours, offered[station, v], taken[station, v])
            if v < gathered:
                w_moves(station, v)[0]()

    base_moves(0)[1]()
    offer(0, 0, FIRST)
    base_moves(1)[1]()
    offer(0, FIRST, variables)
    settle(0, variables)
    for station in range(1, STEPS):
        offer(station, 0, variables)

    def sweep_rows(src, v, w, first, size):
        here = pl.ds(first, size)
        above, below = pl.ds(first - 1, size), pl.ds(first + 1, size)
        summed = []
        for kk in range(per_dev):
            rate = (me * per_dev + kk).astype(jnp.float32) * (0.5 / freqs)
            at = [c * per_dev + kk for c in range(2)]
            real, imag = [x_one[src, ck, v, here, :] for ck in at]
            mixing = (w * real - rate * imag, w * imag + rate * real)
            summed.append(
                [
                    SIDE_WEIGHT * (x_one[src, ck, v, above, :] + x_one[src, ck, v, below, :])
                    + b_one[ck, v, pl.ds(first - 8, size), :]
                    - mixed
                    for ck, mixed in zip(at, mixing)
                ]
            )
        return summed

    def sweep_plane(e, v, station, last):
        src, dst = e % 2, (e + 1) % 2
        edge_copy(e, v).wait()
        for ck in range(parts):
            x_one[src, ck, v, pl.ds(7, 1), :] = edge_in[src, v, pl.ds(ck, 1), :]
            x_one[src, ck, v, pl.ds(8 + span, 1), :] = edge_in[src, v, pl.ds(parts + ck, 1), :]

        @pl.when(jnp.logical_not(last))
        def _():
            tiles = []
            for first in (span, 8):
                w = plane_w[station, v, pl.ds(first - 8, 8), :]
                for pair_of in sweep_rows(src, v, w, first, 8):
                    tiles += pair_of
            q = times_right(jnp.concatenate(tiles, axis=0), qt_ref[...])
            for kk in range(per_dev):
                for c in range(2):
                    ck, n = c * per_dev + kk, 8 * (2 * kk + c)
                    edge_out[dst, v, pl.ds(ck, 1), :] = q[n + 7 : n + 8]
                    n += 8 * parts
                    edge_out[dst, v, pl.ds(parts + ck, 1), :] = q[n : n + 1]
            edge_copy(e + 1, v).start()

        for kk, summed in enumerate(sweep_rows(src, v, plane_w[station, v], 8, span)):
            q = times_right(jnp.concatenate(summed, axis=0), qt_ref[...])
            x_one[dst, kk, v, pl.ds(8, span), :] = q[:span]
            x_one[dst, per_dev + kk, v, pl.ds(8, span), :] = q[span:]

    @pl.loop(0, SWEEPS + LAG * (variables - 1))
    def _(turn):
        @pl.loop(0, variables)
        def _(v):
            e = turn - LAG * v

            @pl.when((e >= 0) & (e < SWEEPS))
            def _():
                @pl.when(e == 0)
                def _():
                    w_moves(0, v)[1]()

                sweep_plane(e, v, 0, (e == SWEEPS - 1) & (v >= RETURNED))

                @pl.when(e == SWEEPS - 1)
                def _():
                    state_moves(v)[0]()

    for station in range(1, STEPS):
        settle(station, RETURNED)
    coefficient_start()

    def each_run(v, visit):
        for c in range(2):
            for kk in range(per_dev):
                start = pl.multiple_of(v * pair + (c * per_dev + kk) * nf, 8)
                visit(start, c * per_dev + kk)

    @pl.loop(0, variables)
    def _(v):
        state_moves(v)[1]()

        @pl.loop(0, own_az)
        def _(a):
            def unpack(start, ck):
                x_ref[0, a + 1, pl.ds(start, nf), :] = r_state[:, v, ck, a, :]

            each_run(v, unpack)

        for copy in halo_copies(0, v):
            copy.start()

    omega = omega_ref[...]

    def sweep_slabs(e, v):
        src, dst = e % 2, (e + 1) % 2
        rows = pl.ds(pl.multiple_of(v * pair, 8), pair)
        w = w_ref[v]
        summed = []
        for a in range(own_az):
            x = x_ref[src, a + 1, rows, :]
            beside = SIDE_WEIGHT * (x_ref[src, a, rows, :] + x_ref[src, a + 2, rows, :])
            real, imag = x[:freqs], x[freqs:]
            here_w = w[a : a + 1]
            mixing = [here_w * real - omega * imag, here_w * imag + omega * real]
            summed.append(beside + b_ref[a, rows, :] - jnp.concatenate(mixing, axis=0))
        q = times_right(jnp.concatenate(summed, axis=0), qt_ref[...])
        for a in range(own_az):
            x_ref[dst, a + 1, rows, :] = q[a * pair : (a + 1) * pair]

    def advect_slab(slot, a, final):
        x = x_ref[slot, a + 1]
        beside = 0.5 * (x_ref[slot, a + 2] - x_ref[slot, a])

        def lanes(y):
            return [y[v * pair : (v + 1) * pair] for v in range(variables)]

        both = jnp.concatenate(lanes(x) + lanes(beside), axis=1)
        in_time = times_stacked(inv_ref[...], both)
        u = [in_time[:, v * radii : (v + 1) * radii] for v in range(variables)]
        ua = [
            in_time[:, (variables + v) * radii : (variables + v + 1) * radii]
            for v in range(variables)
        ]
        radial = times_right(jnp.concatenate(u, axis=0), st_ref[...])
        ur = [radial[v * ntime : (v + 1) * ntime] for v in range(variables)]
        n = [u[1] * ur[v] + u[2] * ua[v] for v in range(variables)]
        n[0] = n[0] + u[0] * (ur[1] + ua[2])
        source = -ADVECT_SCALE * jnp.concatenate(n, axis=1)
        spectral = times_stacked(fwd_ref[...], source)
        for v in range(variables):
            forcing = spectral[:, v * radii : (v + 1) * radii]
            if final:
                for ck in range(parts):
                    o_forcing[:, ck, v, a, :] = forcing[ck * nf : (ck + 1) * nf]
            else:
                march = MARCH_WEIGHT * x[v * pair : (v + 1) * pair] + forcing
                b_ref[a, pl.ds(v * pair, pair), :] = march
                if v < RETURNED:
                    for ck in range(parts):
                        o_march[:, v, ck, a, :] = march[ck * nf : (ck + 1) * nf]

    def advect_all(e, final):
        slot = e % 2

        @pl.loop(1, own_az - 1)
        def _(a):
            advect_slab(slot, a, final)

        @pl.loop(0, variables)
        def _(v):
            for copy in halo_copies(e, v):
                copy.wait()

        @pl.loop(0, 2)
        def _(side):
            advect_slab(slot, side * (own_az - 1), final)

    advect_all(0, False)
    coefficient_wait()

    @pl.loop(0, SWEEPS * variables)
    def _(turn):
        e, v = turn // variables, turn % variables

        @pl.when(e > 0)
        def _():
            for copy in halo_copies(e, v):
                copy.wait()

        sweep_slabs(e, v)
        for copy in halo_copies(e + 1, v):
            copy.start()

        @pl.when(turn < nf)
        def _():
            for w in range(RETURNED):
                march_moves(w)[0](turn, turn + 1)

        @pl.when((e == SWEEPS - 1) & (v >= RETURNED))
        def _():
            @pl.loop(0, own_az)
            def _(a):
                def pack(start, ck):
                    o_state[:, v, ck, a, :] = x_ref[settled, a + 1, pl.ds(start, nf), :]

                each_run(v, pack)

            out_moves(v)[0]()

    advect_all(SWEEPS, True)
    forcing_start()
    for v in range(RETURNED):
        w_moves(1, v)[1]()
        march_moves(v)[1]()
        state_moves(v)[2]()

    @pl.loop(0, SWEEPS * RETURNED)
    def _(turn):
        e, v = SWEEPS + turn // RETURNED, turn % RETURNED
        sweep_plane(e, v, 1, e == 2 * SWEEPS - 1)

    out_state = pltpu.make_async_copy(
        x_one.at[0, :, pl.ds(0, RETURNED), pl.ds(8, span), :],
        g_state.at[:, pl.ds(0, RETURNED), :, :],
        load_sem.at[0],
    )
    out_state.start()

    @pl.loop(RETURNED, variables)
    def _(v):
        out_moves(v)[1]()

    out_state.wait()
    forcing_wait()
    for n in range(2):
        base_moves(n)[2]()
    for v in range(RETURNED):
        w_moves(1, v)[2]()
        march_moves(v)[2]()

    @pl.loop(0, variables)
    def _(v):
        w_moves(0, v)[2]()

    @pl.loop(RETURNED, variables)
    def _(v):
        state_moves(v)[2]()
        out_moves(v)[2]()

    forcing_drain()


LAG = 2
FIRST = 1
RETURNED = 1


def per_device_tiled(state_in, forcing_in, base_flow, station_index, lobe_count):
    _, per_dev, variables, span_az, radii = state_in.shape
    nf = lax.axis_size("freq")
    planes = lax.axis_size("plane")
    freqs = per_dev * nf
    ntime = 3 * freqs // 2
    own_az = span_az // nf
    stored = base_flow.shape[0]
    slopes, inverse_p = radial_tables(radii)
    mode_ids = (np.arange(nf)[None, :] * per_dev + np.arange(per_dev)[:, None]).reshape(-1)
    inverse, forward = transform_tables(mode_ids, freqs, ntime)
    dims = (nf, planes, own_az, variables, per_dev, radii, stored)
    parts = 2 * per_dev
    edge_rows = -(-2 * parts // 8) * 8
    anywhere = pl.BlockSpec(memory_space=pl.ANY)
    far = pl.BlockSpec(memory_space=pltpu.HBM)
    f32 = jnp.float32
    whole = (parts, variables, span_az, radii)
    slab = variables * 2 * freqs
    share = span_az // (nf // 2)
    moves = 3 + 4 * variables + RETURNED
    outs = pl.pallas_call(
        functools.partial(relay, dims),
        out_shape=jax.ShapeDtypeStruct((2, *whole), f32),
        in_specs=[pl.BlockSpec(memory_space=pltpu.SMEM)] + [far] * 8,
        out_specs=anywhere,
        scratch_shapes=[
            pltpu.VMEM((nf, variables, parts, own_az, radii), f32),
            pltpu.VMEM((nf // 2, stored, FIRST, share, radii), f32),
            pltpu.VMEM((nf // 2, stored, variables - FIRST, share, radii), f32),
            pltpu.VMEM((STEPS, variables, share, radii), f32),
            pltpu.VMEM((STEPS, variables, share, radii), f32),
            pltpu.VMEM((STEPS, variables, share, radii), f32),
            pltpu.VMEM((STEPS, variables, span_az, radii), f32),
            pltpu.VMEM((2, parts, variables, span_az + 16, radii), f32),
            pltpu.VMEM(whole, f32),
            pltpu.VMEM((2, variables, edge_rows, radii), f32),
            pltpu.VMEM((2, variables, edge_rows, radii), f32),
            pltpu.VMEM((2, own_az + 2, slab, radii), f32),
            pltpu.VMEM((own_az, slab, radii), f32),
            pltpu.VMEM((variables, own_az, radii), f32),
            pltpu.VMEM((nf, variables, parts, own_az, radii), f32),
            pltpu.VMEM((nf, RETURNED, parts, own_az, radii), f32),
            pltpu.VMEM((nf, parts, variables, own_az, radii), f32),
            pltpu.SemaphoreType.DMA((moves,)),
            pltpu.SemaphoreType.DMA((moves,)),
            pltpu.SemaphoreType.DMA((STEPS, variables)),
            pltpu.SemaphoreType.DMA((STEPS, variables)),
            pltpu.SemaphoreType.DMA((share // own_az,)),
            pltpu.SemaphoreType.DMA((2,)),
            pltpu.SemaphoreType.DMA((2, 2, variables)),
            pltpu.SemaphoreType.DMA((2, 2, variables)),
            pltpu.SemaphoreType.DMA((2, variables)),
            pltpu.SemaphoreType.DMA((2, variables)),
            pltpu.SemaphoreType.DMA((2,)),
            pltpu.VMEM((freqs, radii), f32),
            pltpu.VMEM((2 * radii, 2 * radii), jnp.bfloat16),
            pltpu.VMEM((2 * radii, 2 * radii), jnp.bfloat16),
            pltpu.VMEM((2 * ntime, 4 * freqs), jnp.bfloat16),
            pltpu.VMEM((4 * freqs, 2 * ntime), jnp.bfloat16),
            pltpu.SemaphoreType.DMA((5,)),
            pltpu.SMEM(station_index.shape, jnp.int32),
        ],
        compiler_params=pltpu.CompilerParams(
            collective_id=0, has_side_effects=True, vmem_limit_bytes=32 * 1024 * 1024
        ),
    )(
        lobe_count,
        *[
            pltpu.with_memory_space_constraint(x, pltpu.HBM)
            for x in (
                station_index,
                state_in.reshape(whole),
                base_flow,
                forcing_in.reshape(whole),
                right_table(inverse_p.T),
                right_table(slopes.T),
                stacked_table(inverse.transpose(2, 0, 1).reshape(ntime, 2 * freqs)),
                stacked_table(forward.reshape(2 * freqs, ntime)),
            )
        ],
    )
    return tuple(outs[n].reshape(state_in.shape) for n in range(2))


def per_device_any(*args):
    nf = lax.axis_size("freq")
    tiles = args[0].shape[3] % (8 * nf) == 0 and nf % 2 == 0 and lax.axis_size("plane") == 2
    return (per_device_tiled if tiles else per_device)(*args)


MESH = pl.DeviceIdType.MESH


def solution(mesh):
    return jax.shard_map(
        per_device_any,
        mesh=mesh,
        in_specs=(
            P(None, "freq", None, "plane", None),
            P(None, "freq", None, "plane", None),
            P("freq", None, "plane", None),
            P(),
            P(),
        ),
        out_specs=(P(None, "freq", None, "plane", None), P(None, "freq", None, "plane", None)),
        check_vma=False,
    )
```

```python
import functools
import math

import jax
import jax.numpy as jnp
import numpy as np
from jax import lax
from jax.experimental import pallas as pl
from jax.experimental.pallas import tpu as pltpu
from jax.sharding import PartitionSpec as P

SWEEPS = 4
STEPS = 2


SIDE_WEIGHT = 1.25
MARCH_WEIGHT = 4.0
DIAG_SHIFT = 4.0
ADVECT_SCALE = 0.5
BASE_SCALE = 0.5


def radial_tables(radius_count):
    indices = np.arange(radius_count)
    angles = math.pi * indices / (radius_count - 1)
    nodes = np.cos(angles)
    weights = np.where((indices == 0) | (indices == radius_count - 1), 2.0, 1.0)
    parity = 1.0 - 2.0 * ((indices[:, None] + indices[None, :]) % 2)
    offdiag = indices[:, None] != indices[None, :]
    spacing = np.where(offdiag, nodes[:, None] - nodes[None, :], 1.0)
    entries = np.where(offdiag, weights[:, None] / weights[None, :] * parity / spacing, 0.0)
    entries = entries - np.diag(entries.sum(axis=1))
    slopes = np.sin(angles)[:, None] * entries / (radius_count - 1)
    system = slopes.T @ slopes + DIAG_SHIFT * np.eye(radius_count)
    return slopes.astype(np.float32), np.linalg.inv(system).astype(np.float32)


def transform_tables(mode_ids, freqs, ntime):
    time_ids = np.arange(ntime)
    angles = 2.0 * math.pi * (mode_ids[:, None] * time_ids[None, :] % ntime) / ntime
    stacked = np.stack([np.cos(angles), -np.sin(angles)])
    return (
        (stacked / math.sqrt(freqs)).astype(np.float32),
        (stacked / math.sqrt(ntime)).astype(np.float32),
    )


def chevron(lobe_count, azimuths, start_az, total_az):
    position = start_az + jnp.arange(azimuths)
    phases = lobe_count[0] * position % total_az
    return 1.0 + 0.5 * jnp.cos(2.0 * math.pi * phases.astype(jnp.float32) / total_az)


def halves(x):
    high = x.astype(jnp.bfloat16)
    return high, (x - high.astype(jnp.float32)).astype(jnp.bfloat16)


def right_table(table):
    high, low = np_halves(table)
    return jnp.asarray(np.tile(np.concatenate([high, low], axis=1), (2, 1)))


def left_table(table):
    high, low = np_halves(table)
    return jnp.asarray(np.concatenate([high, high, low, low], axis=1))


def np_halves(table):
    high = table.astype(jnp.bfloat16)
    return high, (table - high.astype(np.float32)).astype(jnp.bfloat16)


def times_right(x, table):
    width = table.shape[1] // 2
    y = jnp.dot(jnp.concatenate(halves(x), axis=1), table, preferred_element_type=jnp.float32)
    return y[:, :width] + y[:, width:]


def times_left(table, x):
    high, low = halves(x)
    return jnp.dot(
        table,
        jnp.concatenate([high, low, high, low], axis=0),
        preferred_element_type=jnp.float32,
    )


def ring_of(f, p, nf, planes):
    at = f
    if nf % 4 == 0:
        high = nf // 4
        z, y, x = f // 4, (f // 2) % 2, f % 2
        column = 2 * y + (x + y) % 2
        at = column * high + z + (column % 2) * (high - 1 - 2 * z)
    return at * planes + p


def device_of(g, nf, planes):
    at = g // planes
    f = at
    if nf % 4 == 0:
        high = nf // 4
        column, z = at // high, at % high
        z = z + (column % 2) * (high - 1 - 2 * z)
        y = column // 2
        f = 4 * z + 2 * y + (column + y) % 2
    return f, g % planes


def march(
    dims,
    station_ref,
    shape_ref,
    rate_ref,
    state_ref,
    s_base,
    forcing_ref,
    far_omega,
    far_qt,
    far_st,
    far_inv,
    far_fwd,
    g_state,
    g_forcing,
    r_state,
    r_base,
    s_state,
    s_w,
    r_w,
    plane_w,
    x_one,
    b_one,
    edge_out,
    edge_in,
    x_ref,
    b_ref,
    f_ref,
    w_ref,
    o_state,
    o_forcing,
    send_sem,
    recv_sem,
    own_sem,
    halo_send,
    halo_recv,
    edge_send,
    edge_recv,
    load_sem,
    omega_ref,
    qt_ref,
    st_ref,
    inv_ref,
    fwd_ref,
    table_sem,
):
    nf, planes, own_az, variables, per_dev, radii, stored, rows, base_rows, w_rows = dims
    freqs = nf * per_dev
    span = nf * own_az
    runs = 2 * per_dev * variables
    ntime = inv_ref.shape[0]
    half = variables * freqs
    me = lax.axis_index("freq")
    plane = lax.axis_index("plane")
    ring = nf * planes
    here = ring_of(me, plane, nf, planes)
    part, block = here // nf, here % nf

    def named(device):
        return {"freq": device[0], "plane": device[1]}

    right_id = named(device_of((here + 1) % ring, nf, planes))
    left_id = named(device_of((here + ring - 1) % ring, nf, planes))
    barrier = pltpu.get_barrier_semaphore()

    @pl.loop(1, ring)
    def _(d):
        other = (me * planes + plane + d) % ring
        pl.semaphore_signal(
            barrier,
            inc=1,
            device_id={"freq": other // planes, "plane": other % planes},
            device_id_type=MESH,
        )

    beyond = {"freq": me, "plane": (plane + 1) % planes}
    behind = {"freq": me, "plane": (plane + planes - 1) % planes}
    load_state = pltpu.make_async_copy(state_ref, x_one.at[0, :, pl.ds(8, span), :], load_sem.at[0])
    load_forcing = pltpu.make_async_copy(forcing_ref, b_one, load_sem.at[1])
    load_state.start()
    load_forcing.start()
    tables = [
        pltpu.make_async_copy(far, near, table_sem.at[i])
        for i, (far, near) in enumerate(
            (
                (far_omega, omega_ref),
                (far_qt, qt_ref),
                (far_st, st_ref),
                (far_inv, inv_ref),
                (far_fwd, fwd_ref),
            )
        )
    ]
    for table in tables:
        table.start()
    pl.semaphore_wait(barrier, ring - 1)

    def owner(i):
        return device_of(plane * nf + i, nf, planes)

    def holder(i):
        return i, part

    def is_me(device):
        return (device[0] == me) & (device[1] == plane)

    def exchange(k, source, landing, target, origin, pick, mine, size, first):
        def rows_of(ref, i):
            return ref.at[pl.ds(pl.multiple_of(i * size, 8), size), :]

        def copy(i):
            return pltpu.make_async_remote_copy(
                src_ref=rows_of(source, pick(i)),
                dst_ref=rows_of(landing, mine),
                send_sem=send_sem.at[k, i],
                recv_sem=recv_sem.at[k, mine],
                device_id=named(target(i)),
                device_id_type=MESH,
            )

        def arrival(i):
            return pltpu.make_async_remote_copy(
                src_ref=rows_of(landing, i),
                dst_ref=rows_of(landing, i),
                send_sem=send_sem.at[k, i],
                recv_sem=recv_sem.at[k, i],
                device_id=named(origin(i)),
                device_id_type=MESH,
            )

        def own(i):
            return pltpu.make_async_copy(
                rows_of(source, pick(i)), rows_of(landing, mine), own_sem.at[k]
            )

        @pl.loop(0, nf)
        def _(d):
            i = (d + me) % nf
            stays = is_me(target(i))

            @pl.when(stays)
            def _():
                if first:
                    own(i).start()
                else:
                    own(i).wait()

            @pl.when(jnp.logical_not(stays))
            def _():
                if first:
                    copy(i).start()
                else:
                    copy(i).wait_send()

            if not first:

                @pl.when(jnp.logical_not(is_me(origin(i))))
                def _():
                    arrival(i).wait_recv()

    def same(i):
        return i

    base_args = (1, s_base, r_base, owner, holder, same, me, base_rows)
    state_args = (0, s_state, r_state, owner, holder, same, me, rows)
    w_args = (2, s_w, r_w, holder, owner, lambda i: 0, block, w_rows)
    out_state_args = (3, o_state, g_state, holder, owner, same, block, rows)
    out_forcing_args = (4, o_forcing, g_forcing, holder, owner, same, block, rows)
    exchange(*base_args, True)

    def halo_copies(e):
        slot = e % 2
        return (
            pltpu.make_async_remote_copy(
                src_ref=x_ref.at[slot, own_az],
                dst_ref=x_ref.at[slot, 0],
                send_sem=halo_send.at[0, e],
                recv_sem=halo_recv.at[0, e],
                device_id=right_id,
                device_id_type=MESH,
            ),
            pltpu.make_async_remote_copy(
                src_ref=x_ref.at[slot, 1],
                dst_ref=x_ref.at[slot, own_az + 1],
                send_sem=halo_send.at[1, e],
                recv_sem=halo_recv.at[1, e],
                device_id=left_id,
                device_id_type=MESH,
            ),
        )

    def place(a, c, v, kk):
        return ((c * variables + v) * per_dev + kk) * nf

    def packed_row(a, c, v, kk):
        return ((c * per_dev + kk) * variables + v) * own_az + a

    def each_run(visit):
        @pl.loop(0, own_az)
        def _(a):
            for c in range(2):
                for v in range(variables):
                    for kk in range(per_dev):
                        visit(a, place(a, c, v, kk), packed_row(a, c, v, kk))

    def in_row(a, c, v, kk):
        return ((c * per_dev + kk) * variables + v) * own_az + a

    def edge_copies(e):
        return [
            pltpu.make_async_remote_copy(
                src_ref=edge_out.at[e, side],
                dst_ref=edge_in.at[e, side],
                send_sem=edge_send.at[side, e],
                recv_sem=edge_recv.at[side, e],
                device_id=target,
                device_id_type=MESH,
            )
            for side, target in ((0, beyond), (1, behind))
        ]

    def send_edges(slot, e):
        for m in range(runs):
            edge_out[e, 0, pl.ds(m, 1), :] = x_one[slot, m, pl.ds(7 + span, 1), :]
            edge_out[e, 1, pl.ds(m, 1), :] = x_one[slot, m, pl.ds(8, 1), :]
        for copy in edge_copies(e):
            copy.start()

    for table in tables:
        table.wait()
    load_state.wait()
    send_edges(0, 0)
    load_forcing.wait()

    @pl.loop(0, runs)
    def _(m):
        b_one[m] = MARCH_WEIGHT * x_one[0, m, pl.ds(8, span), :] + b_one[m]

    exchange(*base_args, False)
    for station in range(STEPS):
        wanted = station_ref[station]

        @pl.loop(0, own_az)
        def _(a):
            for v in range(variables):
                scaled = (BASE_SCALE * shape_ref[a]) * r_base[
                    pl.ds(
                        (wanted // stored) * base_rows
                        + ((wanted % stored) * variables + v) * own_az
                        + a,
                        1,
                    ),
                    :,
                ]
                if station == 0:
                    s_w[pl.ds(v * own_az + a, 1), :] = scaled
                else:
                    w_ref[(station - 1) * own_az + a, pl.ds(v, 1), :] = scaled

        if station == 0:
            exchange(*w_args, True)
    exchange(*w_args, False)

    @pl.loop(0, nf)
    def _(j):
        for v in range(variables):
            plane_w[v, pl.ds(j * own_az, own_az), :] = r_w[pl.ds(j * w_rows + v * own_az, own_az), :]

    @pl.loop(0, SWEEPS)
    def _(e):
        src, dst = e % 2, (e + 1) % 2
        for copy in edge_copies(e):
            copy.wait()
        for m in range(runs):
            x_one[src, m, pl.ds(7, 1), :] = edge_in[e, 0, pl.ds(m, 1), :]
            x_one[src, m, pl.ds(8 + span, 1), :] = edge_in[e, 1, pl.ds(m, 1), :]
        for kk in range(per_dev):
            rate = rate_ref[kk]

            @pl.loop(0, variables)
            def _(v):
                w = plane_w[v]
                at = [(c * per_dev + kk) * variables + v for c in range(2)]
                real, imag = [x_one[src, m, pl.ds(8, span), :] for m in at]
                mixing = (w * real - rate * imag, w * imag + rate * real)
                summed = [
                    SIDE_WEIGHT
                    * (x_one[src, m, pl.ds(7, span), :] + x_one[src, m, pl.ds(9, span), :])
                    + b_one[m]
                    - mixed
                    for m, mixed in zip(at, mixing)
                ]
                q = times_right(jnp.concatenate(summed, axis=0), qt_ref[...])
                x_one[dst, at[0], pl.ds(8, span), :] = q[:span]
                x_one[dst, at[1], pl.ds(8, span), :] = q[span:]

        @pl.when(e < SWEEPS - 1)
        def _():
            send_edges(dst, e + 1)

    settled = SWEEPS % 2

    @pl.loop(0, nf)
    def _(j):
        for m in range(runs):
            s_state[pl.ds(j * rows + m * own_az, own_az), :] = x_one[
                settled, m, pl.ds(8 + j * own_az, own_az), :
            ]

    exchange(*state_args, True)
    exchange(*state_args, False)

    def unpack_state(a, start, row):
        x_ref[0, a + 1, pl.ds(start, nf), :] = r_state[pl.ds(row, nf, stride=rows), :]

    each_run(unpack_state)
    for copy in halo_copies(0):
        copy.start()
    omega = omega_ref[...][None]
    flat = (2 * half, radii)
    cube = (variables, freqs, radii)

    def sweep_slab(src, dst, a, station):
        x = x_ref[src, a + 1]
        beside = SIDE_WEIGHT * (x_ref[src, a] + x_ref[src, a + 2]) + b_ref[a]
        real, imag = x[:half].reshape(cube), x[half:].reshape(cube)
        w = w_ref[(station - 1) * own_az + a][:variables][:, None, :]
        mixing = jnp.concatenate([w * real - omega * imag, w * imag + omega * real], axis=0)
        summed = beside - mixing.reshape(flat)
        x_ref[dst, a + 1] = times_right(summed, qt_ref[...])

    def advect_slab(slot, a, final):
        x = x_ref[slot, a + 1]
        beside = 0.5 * (x_ref[slot, a + 2] - x_ref[slot, a])

        def lanes(y):
            return [
                jnp.concatenate(
                    [
                        y[v * freqs : (v + 1) * freqs],
                        y[half + v * freqs : half + (v + 1) * freqs],
                    ],
                    axis=0,
                )
                for v in range(variables)
            ]

        both = jnp.concatenate(lanes(x) + lanes(beside), axis=1)
        in_time = times_left(inv_ref[...], both)
        u = [in_time[:, v * radii : (v + 1) * radii] for v in range(variables)]
        ua = [
            in_time[:, (variables + v) * radii : (variables + v + 1) * radii]
            for v in range(variables)
        ]
        radial = times_right(jnp.concatenate(u, axis=0), st_ref[...])
        ur = [radial[v * ntime : (v + 1) * ntime] for v in range(variables)]
        n = [u[1] * ur[v] + u[2] * ua[v] for v in range(variables)]
        n[0] = n[0] + u[0] * (ur[1] + ua[2])
        source = -ADVECT_SCALE * jnp.concatenate(n, axis=1)
        spectral = times_left(fwd_ref[...], source)
        forcing = jnp.concatenate(
            [
                spectral[c * freqs : (c + 1) * freqs, v * radii : (v + 1) * radii]
                for c in range(2)
                for v in range(variables)
            ],
            axis=0,
        )
        if final:
            f_ref[a] = forcing
        else:
            b_ref[a] = MARCH_WEIGHT * x + forcing

    def advect_all(slot, e, final):
        @pl.loop(1, own_az - 1)
        def _(a):
            advect_slab(slot, a, final)

        for copy in halo_copies(e):
            copy.wait()
        advect_slab(slot, 0, final)
        if own_az > 1:
            advect_slab(slot, own_az - 1, final)

    advect_all(0, 0, False)
    for station in range(1, STEPS):

        @pl.loop(0, SWEEPS)
        def _(sweep):
            e = (station - 1) * SWEEPS + sweep
            src, dst = e % 2, (e + 1) % 2

            @pl.when(sweep > 0)
            def _():
                for copy in halo_copies(e):
                    copy.wait()

            sweep_slab(src, dst, 0, station)
            if own_az > 1:
                sweep_slab(src, dst, own_az - 1, station)
            for copy in halo_copies(e + 1):
                copy.start()

            @pl.loop(1, own_az - 1)
            def _(a):
                sweep_slab(src, dst, a, station)

        last = station * SWEEPS
        slot = last % 2
        final = station == STEPS - 1
        if final:

            def pack_state(a, start, row):
                o_state[pl.ds(row, nf, stride=rows), :] = x_ref[slot, a + 1, pl.ds(start, nf), :]

            each_run(pack_state)
            exchange(*out_state_args, True)

        advect_all(slot, last, final)

    def pack_forcing(a, start, row):
        o_forcing[pl.ds(row, nf, stride=rows), :] = f_ref[a, pl.ds(start, nf), :]

    each_run(pack_forcing)
    exchange(*out_forcing_args, True)
    exchange(*out_state_args, False)
    exchange(*out_forcing_args, False)


def per_device(state_in, forcing_in, base_flow, station_index, lobe_count):
    _, per_dev, variables, span_az, radii = state_in.shape
    nf = lax.axis_size("freq")
    planes = lax.axis_size("plane")
    freqs = per_dev * nf
    ntime = 3 * freqs // 2
    own_az = span_az // nf
    stored = base_flow.shape[0]
    slopes, inverse_p = radial_tables(radii)
    mode_ids = (np.arange(nf)[None, :] * per_dev + np.arange(per_dev)[:, None]).reshape(-1)
    inverse, forward = transform_tables(mode_ids, freqs, ntime)
    omegas = np.broadcast_to((0.5 * mode_ids / freqs).astype(np.float32)[:, None], (freqs, radii))
    plane = lax.axis_index("plane")
    here = ring_of(lax.axis_index("freq"), plane, nf, planes)
    shape_az = chevron(lobe_count, own_az, here * own_az, span_az * planes)

    def padded_rows(count):
        return -(-count // 8) * 8

    def chunks(x, size):
        x = x.reshape(-1, nf, own_az, radii).transpose(1, 0, 2, 3).reshape(nf, -1, radii)
        x = jnp.pad(x, ((0, 0), (0, size - x.shape[1]), (0, 0)))
        return x.reshape(nf * size, radii)

    count = 2 * per_dev * variables * own_az
    rows = padded_rows(count)
    base_rows = padded_rows(stored * variables * own_az)
    w_rows = padded_rows(variables * own_az)
    dims = (nf, planes, own_az, variables, per_dev, radii, stored, rows, base_rows, w_rows)
    half = variables * freqs
    exchanges = (STEPS - 1) * SWEEPS + 1
    runs = 2 * per_dev * variables
    edge_rows = padded_rows(runs)
    first_mode = lax.axis_index("freq") * per_dev
    rates = 0.5 * (first_mode + jnp.arange(per_dev)).astype(jnp.float32) / freqs
    smem = pl.BlockSpec(memory_space=pltpu.SMEM)
    anywhere = pl.BlockSpec(memory_space=pl.ANY)
    packed = (nf * rows, radii)
    f32 = jnp.float32
    outs = pl.pallas_call(
        functools.partial(march, dims),
        out_shape=[jax.ShapeDtypeStruct(packed, f32)] * 2,
        in_specs=[smem, smem, smem, anywhere, anywhere, anywhere] + [anywhere] * 5,
        out_specs=[anywhere, anywhere],
        scratch_shapes=[
            pltpu.VMEM(packed, f32),
            pltpu.VMEM((nf * base_rows, radii), f32),
            pltpu.VMEM(packed, f32),
            pltpu.VMEM((w_rows, radii), f32),
            pltpu.VMEM((nf * w_rows, radii), f32),
            pltpu.VMEM((variables, span_az, radii), f32),
            pltpu.VMEM((2, runs, span_az + 16, radii), f32),
            pltpu.VMEM((runs, span_az, radii), f32),
            pltpu.VMEM((SWEEPS, 2, edge_rows, radii), f32),
            pltpu.VMEM((SWEEPS, 2, edge_rows, radii), f32),
            pltpu.VMEM((2, own_az + 2, 2 * half, radii), f32),
            pltpu.VMEM((own_az, 2 * half, radii), f32),
            pltpu.VMEM((own_az, 2 * half, radii), f32),
            pltpu.VMEM(((STEPS - 1) * own_az, padded_rows(variables), radii), f32),
            pltpu.VMEM(packed, f32),
            pltpu.VMEM(packed, f32),
            pltpu.SemaphoreType.DMA((5, nf)),
            pltpu.SemaphoreType.DMA((5, nf)),
            pltpu.SemaphoreType.DMA((5,)),
            pltpu.SemaphoreType.DMA((2, exchanges)),
            pltpu.SemaphoreType.DMA((2, exchanges)),
            pltpu.SemaphoreType.DMA((2, SWEEPS)),
            pltpu.SemaphoreType.DMA((2, SWEEPS)),
            pltpu.SemaphoreType.DMA((2,)),
            pltpu.VMEM((freqs, radii), f32),
            pltpu.VMEM((2 * radii, 2 * radii), jnp.bfloat16),
            pltpu.VMEM((2 * radii, 2 * radii), jnp.bfloat16),
            pltpu.VMEM((ntime, 8 * freqs), jnp.bfloat16),
            pltpu.VMEM((2 * freqs, 4 * ntime), jnp.bfloat16),
            pltpu.SemaphoreType.DMA((5,)),
        ],
        compiler_params=pltpu.CompilerParams(
            collective_id=0, has_side_effects=True, vmem_limit_bytes=63_000 * 1024
        ),
    )(
        station_index,
        shape_az,
        rates,
        state_in.reshape(runs, span_az, radii),
        chunks(base_flow, base_rows),
        forcing_in.reshape(runs, span_az, radii),
        jnp.asarray(omegas),
        right_table(inverse_p.T),
        right_table(slopes.T),
        left_table(inverse.transpose(2, 0, 1).reshape(ntime, 2 * freqs)),
        left_table(forward.reshape(2 * freqs, ntime)),
    )

    return tuple(finish(y, nf, per_dev, variables, own_az, radii, rows, count) for y in outs)


def finish(y, nf, per_dev, variables, own_az, radii, rows, count):
    y = y.reshape(nf, rows, radii)[:, :count].reshape(nf, -1, own_az, radii)
    return y.transpose(1, 0, 2, 3).reshape(2, per_dev, variables, nf * own_az, radii)


def stacked_table(table):
    high, low = np_halves(table)
    return jnp.asarray(np.tile(np.concatenate([high, low], axis=0), (1, 2)))


def times_stacked(table, x):
    height = table.shape[0] // 2
    y = jnp.dot(table, jnp.concatenate(halves(x), axis=0), preferred_element_type=jnp.float32)
    return y[:height] + y[height:]


def relay(
    dims,
    lobe_ref,
    far_station,
    state_ref,
    base_ref,
    forcing_ref,
    far_qt,
    far_st,
    far_inv,
    far_fwd,
    g_both,
    r_state,
    found_first,
    found_rest,
    offered,
    taken,
    s_w,
    plane_w,
    x_one,
    b_one,
    edge_out,
    edge_in,
    x_ref,
    b_ref,
    w_ref,
    o_state,
    o_march,
    o_forcing,
    send_sem,
    recv_sem,
    offer_send,
    offer_recv,
    w_send,
    w_recv,
    halo_send,
    halo_recv,
    edge_send,
    edge_recv,
    load_sem,
    omega_ref,
    qt_ref,
    st_ref,
    inv_ref,
    fwd_ref,
    table_sem,
    station_ref,
):
    nf, planes, own_az, variables, per_dev, radii, stored = dims
    g_state, g_forcing = g_both.at[0], g_both.at[1]
    freqs = nf * per_dev
    span = nf * own_az
    parts = 2 * per_dev
    ntime = inv_ref.shape[0] // 2
    pair = 2 * freqs
    me = lax.axis_index("freq")
    plane = lax.axis_index("plane")
    ring = nf * planes
    here = ring_of(me, plane, nf, planes)
    part, block = here // nf, here % nf
    fold = nf // 2
    side, seat = me // fold, me % fold
    share = span // fold
    blocks = share // own_az

    def mate(i):
        return side * fold + i, plane


    def named(device):
        return {"freq": device[0], "plane": device[1]}

    def is_me(device):
        return (device[0] == me) & (device[1] == plane)

    right_id = named(device_of((here + 1) % ring, nf, planes))
    left_id = named(device_of((here + ring - 1) % ring, nf, planes))
    barrier = pltpu.get_barrier_semaphore()

    def greet(device):
        pl.semaphore_signal(barrier, inc=1, device_id=device, device_id_type=MESH)

    @pl.loop(1, fold)
    def _(d):
        greet(named(mate((seat + d) % fold)))

    beyond = {"freq": me, "plane": (plane + 1) % planes}
    across = {"freq": (1 - side) * fold + seat, "plane": plane}
    greet(beyond)
    greet(across)
    load_state = pltpu.make_async_copy(
        state_ref, x_one.at[0, :, :, pl.ds(8, span), :], load_sem.at[0]
    )
    load_forcing = pltpu.make_async_copy(forcing_ref, b_one, load_sem.at[1])
    load_state.start()
    load_forcing.start()
    tables = [
        pltpu.make_async_copy(far, near, table_sem.at[i])
        for i, (far, near) in enumerate(
            (
                (far_station, station_ref),
                (far_qt, qt_ref),
                (far_st, st_ref),
                (far_inv, inv_ref),
                (far_fwd, fwd_ref),
            )
        )
    ]
    for table in tables:
        table.start()
    pl.semaphore_wait(barrier, fold + 1)

    def owner(i):
        return device_of(plane * nf + i, nf, planes)

    def holder(i):
        return i, part

    def azimuths(i):
        return pl.ds(pl.multiple_of(i * own_az, 8), own_az)

    def exchange(k, piece, landing, target, mine, count, landed, sent):
        def copy(i):
            return pltpu.make_async_remote_copy(
                src_ref=piece(i),
                dst_ref=landing(mine),
                send_sem=send_sem.at[k],
                recv_sem=recv_sem.at[k],
                device_id=named(target(i)),
                device_id_type=MESH,
            )

        def start(first=0, stop=count):
            @pl.loop(first, stop)
            def _(d):
                i = (d + me) % count
                stays = is_me(target(i))

                @pl.when(stays)
                def _():
                    pltpu.make_async_copy(piece(i), landing(mine), recv_sem.at[k]).start()

                @pl.when(jnp.logical_not(stays))
                def _():
                    copy(i).start()

        def all_of(ref):
            return pltpu.make_async_remote_copy(
                src_ref=ref,
                dst_ref=ref,
                send_sem=send_sem.at[k],
                recv_sem=recv_sem.at[k],
                device_id=beyond,
                device_id_type=MESH,
            )

        def wait():
            all_of(landed).wait_recv()

        def drain():
            if count < nf:
                all_of(sent(count - 1)).wait_send()
            else:

                @pl.when(part == plane)
                def _():
                    all_of(sent(count - 1)).wait_send()

                @pl.when(part != plane)
                def _():
                    all_of(sent(count)).wait_send()

        return start, wait, drain

    def chunk(i):
        return pl.ds(pl.multiple_of(i * share, 8), share)

    def base_moves(n):
        some = (pl.ds(0, FIRST), pl.ds(FIRST, variables - FIRST))[n]
        found = (found_first, found_rest)[n]
        return exchange(
            n * (2 + 4 * variables + RETURNED),
            lambda i: base_ref.at[:, some, chunk(i), :],
            lambda j: found.at[j],
            mate,
            seat,
            fold,
            found,
            lambda count: found.at[pl.ds(0, count)],
        )

    def offers(station, v):
        return pltpu.make_async_remote_copy(
            src_ref=offered.at[station, v],
            dst_ref=taken.at[station, v],
            send_sem=offer_send.at[station, v],
            recv_sem=offer_recv.at[station, v],
            device_id=across,
            device_id_type=MESH,
        )

    def w_moves(station, v):
        return exchange(
            1 + station * variables + v,
            lambda i: s_w.at[station, v],
            lambda j: plane_w.at[station, v, chunk(j), :],
            mate,
            seat,
            fold,
            plane_w.at[station, v],
            lambda n: plane_w.at[station, v, pl.ds(0, n * share), :],
        )

    def coefficient_copies():
        for j in range(blocks):
            target = device_of(plane * nf + seat * blocks + j, nf, planes)
            source = s_w.at[1, :, pl.ds(j * own_az, own_az), :]
            remote = pltpu.make_async_remote_copy(
                src_ref=source,
                dst_ref=w_ref,
                send_sem=w_send.at[j],
                recv_sem=w_recv.at[0],
                device_id=named(target),
                device_id_type=MESH,
            )
            local = pltpu.make_async_copy(source, w_ref, w_recv.at[1])
            near = target[0] // fold == side
            yield remote, local, near & jnp.logical_not(is_me(target)), near & is_me(target)

    def coefficient_start():
        for remote, local, away, home in coefficient_copies():
            pl.when(away)(remote.start)
            pl.when(home)(local.start)

    def coefficient_wait():
        for remote, local, away, home in coefficient_copies():
            pl.when(away)(remote.wait_send)
            pl.when(home)(local.wait)
        source = (side * fold + block // blocks, part)
        arrived = pltpu.make_async_remote_copy(
            src_ref=w_ref,
            dst_ref=w_ref,
            send_sem=w_send.at[0],
            recv_sem=w_recv.at[0],
            device_id=named(source),
            device_id_type=MESH,
        )
        pl.when(jnp.logical_not(is_me(source)))(arrived.wait_recv)

    settled = SWEEPS % 2

    def state_moves(v):
        return exchange(
            1 + 2 * variables + v,
            lambda i: x_one.at[
                settled, :, v, pl.ds(pl.multiple_of(8 + i * own_az, 8), own_az), :
            ],
            lambda j: r_state.at[j, v],
            owner,
            me,
            nf,
            r_state.at[:, v],
            lambda n: r_state.at[pl.ds(0, n), v],
        )

    def march_moves(v):
        return exchange(
            1 + 4 * variables + v,
            lambda i: o_march.at[i, v],
            lambda j: b_one.at[:, v, azimuths(j), :],
            holder,
            block,
            nf,
            b_one.at[:, v],
            lambda n: o_march.at[pl.ds(0, n), v],
        )

    def out_moves(v):
        return exchange(
            1 + 3 * variables + v,
            lambda i: o_state.at[i, v],
            lambda j: g_state.at[:, v, azimuths(j), :],
            holder,
            block,
            nf,
            g_state.at[:, v],
            lambda n: o_state.at[pl.ds(0, n), v],
        )

    forcing_start, forcing_wait, forcing_drain = exchange(
        1 + 4 * variables + RETURNED,
        lambda i: o_forcing.at[i],
        lambda j: g_forcing.at[:, :, azimuths(j), :],
        holder,
        block,
        nf,
        g_forcing,
        lambda n: o_forcing.at[pl.ds(0, n)],
    )
    for n in range(2):
        base_moves(n)[0]()

    def halo_copies(e, v):
        slot = e % 2
        rows = pl.ds(pl.multiple_of(v * pair, 8), pair)
        return [
            pltpu.make_async_remote_copy(
                src_ref=x_ref.at[slot, source, rows, :],
                dst_ref=x_ref.at[slot, target, rows, :],
                send_sem=halo_send.at[side, slot, v],
                recv_sem=halo_recv.at[side, slot, v],
                device_id=device,
                device_id_type=MESH,
            )
            for side, source, target, device in (
                (0, own_az, 0, right_id),
                (1, 1, own_az + 1, left_id),
            )
        ]

    def edge_copy(e, v):
        turn = e % 2
        return pltpu.make_async_remote_copy(
            src_ref=edge_out.at[turn, v],
            dst_ref=edge_in.at[turn, v],
            send_sem=edge_send.at[turn, v],
            recv_sem=edge_recv.at[turn, v],
            device_id=beyond,
            device_id_type=MESH,
        )

    def send_edges(e, v):
        slot = e % 2
        for ck in range(parts):
            edge_out[slot, v, pl.ds(ck, 1), :] = x_one[slot, ck, v, pl.ds(7 + span, 1), :]
            edge_out[slot, v, pl.ds(parts + ck, 1), :] = x_one[slot, ck, v, pl.ds(8, 1), :]
        edge_copy(e, v).start()

    for kk in range(per_dev):
        modes = lax.broadcasted_iota(jnp.int32, (nf, radii), 0) * per_dev + kk
        omega_ref[pl.ds(kk * nf, nf), :] = 0.5 * modes.astype(jnp.float32) / freqs
    load_state.wait()

    @pl.loop(0, variables)
    def _(v):
        send_edges(0, v)

    load_forcing.wait()

    @pl.loop(0, variables)
    def _(v):
        for ck in range(parts):
            b_one[ck, v] = MARCH_WEIGHT * x_one[0, ck, v, pl.ds(8, span), :] + b_one[ck, v]

    for table in tables:
        table.wait()
    position = plane * span + seat * share + lax.broadcasted_iota(jnp.int32, (share, radii), 0)
    phases = (lobe_ref[0] * position) % (span * planes)
    shape = 1.0 + 0.5 * jnp.cos(2.0 * math.pi * phases.astype(jnp.float32) / (span * planes))
    def offer(station, first, stop):
        wanted = station_ref[station]
        for v in range(first, stop):
            found, at = (found_first, v) if v < FIRST else (found_rest, v - FIRST)
            offered[station, v] = (BASE_SCALE * shape) * found[
                (wanted // stored) % fold, wanted % stored, at
            ]
            offers(station, v).start()

    def settle(station, gathered):
        ours = jnp.full((share, radii), station_ref[station] // (stored * fold)) == side
        for v in range(variables):
            offers(station, v).wait()
            s_w[station, v] = jnp.where(ours, offered[station, v], taken[station, v])
            if v < gathered:
                w_moves(station, v)[0]()

    base_moves(0)[1]()
    offer(0, 0, FIRST)
    base_moves(1)[1]()
    offer(0, FIRST, variables)
    settle(0, variables)
    for station in range(1, STEPS):
        offer(station, 0, variables)

    def sweep_rows(src, v, w, first, size):
        here = pl.ds(first, size)
        above, below = pl.ds(first - 1, size), pl.ds(first + 1, size)
        summed = []
        for kk in range(per_dev):
            rate = (me * per_dev + kk).astype(jnp.float32) * (0.5 / freqs)
            at = [c * per_dev + kk for c in range(2)]
            real, imag = [x_one[src, ck, v, here, :] for ck in at]
            mixing = (w * real - rate * imag, w * imag + rate * real)
            summed.append(
                [
                    SIDE_WEIGHT * (x_one[src, ck, v, above, :] + x_one[src, ck, v, below, :])
                    + b_one[ck, v, pl.ds(first - 8, size), :]
                    - mixed
                    for ck, mixed in zip(at, mixing)
                ]
            )
        return summed

    def sweep_plane(e, v, station, last):
        src, dst = e % 2, (e + 1) % 2
        edge_copy(e, v).wait()
        for ck in range(parts):
            x_one[src, ck, v, pl.ds(7, 1), :] = edge_in[src, v, pl.ds(ck, 1), :]
            x_one[src, ck, v, pl.ds(8 + span, 1), :] = edge_in[src, v, pl.ds(parts + ck, 1), :]

        @pl.when(jnp.logical_not(last))
        def _():
            tiles = []
            for first in (span, 8):
                w = plane_w[station, v, pl.ds(first - 8, 8), :]
                for pair_of in sweep_rows(src, v, w, first, 8):
                    tiles += pair_of
            q = times_right(jnp.concatenate(tiles, axis=0), qt_ref[...])
            for kk in range(per_dev):
                for c in range(2):
                    ck, n = c * per_dev + kk, 8 * (2 * kk + c)
                    edge_out[dst, v, pl.ds(ck, 1), :] = q[n + 7 : n + 8]
                    n += 8 * parts
                    edge_out[dst, v, pl.ds(parts + ck, 1), :] = q[n : n + 1]
            edge_copy(e + 1, v).start()

        for kk, summed in enumerate(sweep_rows(src, v, plane_w[station, v], 8, span)):
            q = times_right(jnp.concatenate(summed, axis=0), qt_ref[...])
            x_one[dst, kk, v, pl.ds(8, span), :] = q[:span]
            x_one[dst, per_dev + kk, v, pl.ds(8, span), :] = q[span:]

    @pl.loop(0, SWEEPS + LAG * (variables - 1))
    def _(turn):
        @pl.loop(0, variables)
        def _(v):
            e = turn - LAG * v

            @pl.when((e >= 0) & (e < SWEEPS))
            def _():
                @pl.when(e == 0)
                def _():
                    w_moves(0, v)[1]()

                sweep_plane(e, v, 0, (e == SWEEPS - 1) & (v >= RETURNED))

                @pl.when(e == SWEEPS - 1)
                def _():
                    state_moves(v)[0]()

    for station in range(1, STEPS):
        settle(station, RETURNED)
    coefficient_start()

    def each_run(v, visit):
        for c in range(2):
            for kk in range(per_dev):
                start = pl.multiple_of(v * pair + (c * per_dev + kk) * nf, 8)
                visit(start, c * per_dev + kk)

    @pl.loop(0, variables)
    def _(v):
        state_moves(v)[1]()

        @pl.loop(0, own_az)
        def _(a):
            def unpack(start, ck):
                x_ref[0, a + 1, pl.ds(start, nf), :] = r_state[:, v, ck, a, :]

            each_run(v, unpack)

        for copy in halo_copies(0, v):
            copy.start()

    omega = omega_ref[...]

    def sweep_slabs(e, v):
        src, dst = e % 2, (e + 1) % 2
        rows = pl.ds(pl.multiple_of(v * pair, 8), pair)
        w = w_ref[v]
        summed = []
        for a in range(own_az):
            x = x_ref[src, a + 1, rows, :]
            beside = SIDE_WEIGHT * (x_ref[src, a, rows, :] + x_ref[src, a + 2, rows, :])
            real, imag = x[:freqs], x[freqs:]
            here_w = w[a : a + 1]
            mixing = [here_w * real - omega * imag, here_w * imag + omega * real]
            summed.append(beside + b_ref[a, rows, :] - jnp.concatenate(mixing, axis=0))
        q = times_right(jnp.concatenate(summed, axis=0), qt_ref[...])
        for a in range(own_az):
            x_ref[dst, a + 1, rows, :] = q[a * pair : (a + 1) * pair]

    def advect_slab(slot, a, final):
        x = x_ref[slot, a + 1]
        beside = 0.5 * (x_ref[slot, a + 2] - x_ref[slot, a])

        def lanes(y):
            return [y[v * pair : (v + 1) * pair] for v in range(variables)]

        both = jnp.concatenate(lanes(x) + lanes(beside), axis=1)
        in_time = times_stacked(inv_ref[...], both)
        u = [in_time[:, v * radii : (v + 1) * radii] for v in range(variables)]
        ua = [
            in_time[:, (variables + v) * radii : (variables + v + 1) * radii]
            for v in range(variables)
        ]
        radial = times_right(jnp.concatenate(u, axis=0), st_ref[...])
        ur = [radial[v * ntime : (v + 1) * ntime] for v in range(variables)]
        n = [u[1] * ur[v] + u[2] * ua[v] for v in range(variables)]
        n[0] = n[0] + u[0] * (ur[1] + ua[2])
        source = -ADVECT_SCALE * jnp.concatenate(n, axis=1)
        spectral = times_stacked(fwd_ref[...], source)
        for v in range(variables):
            forcing = spectral[:, v * radii : (v + 1) * radii]
            if final:
                for ck in range(parts):
                    o_forcing[:, ck, v, a, :] = forcing[ck * nf : (ck + 1) * nf]
            else:
                march = MARCH_WEIGHT * x[v * pair : (v + 1) * pair] + forcing
                b_ref[a, pl.ds(v * pair, pair), :] = march
                if v < RETURNED:
                    for ck in range(parts):
                        o_march[:, v, ck, a, :] = march[ck * nf : (ck + 1) * nf]

    def advect_all(e, final):
        slot = e % 2

        @pl.loop(1, own_az - 1)
        def _(a):
            advect_slab(slot, a, final)

        @pl.loop(0, variables)
        def _(v):
            for copy in halo_copies(e, v):
                copy.wait()

        @pl.loop(0, 2)
        def _(side):
            advect_slab(slot, side * (own_az - 1), final)

    advect_all(0, False)
    coefficient_wait()

    @pl.loop(0, SWEEPS * variables)
    def _(turn):
        e, v = turn // variables, (turn + RETURNED) % variables

        @pl.when(e > 0)
        def _():
            for copy in halo_copies(e, v):
                copy.wait()

        sweep_slabs(e, v)
        for copy in halo_copies(e + 1, v):
            copy.start()

        @pl.when(turn < nf)
        def _():
            for w in range(RETURNED):
                march_moves(w)[0](turn, turn + 1)

        @pl.when((e == SWEEPS - 1) & (v >= RETURNED))
        def _():
            @pl.loop(0, own_az)
            def _(a):
                def pack(start, ck):
                    o_state[:, v, ck, a, :] = x_ref[settled, a + 1, pl.ds(start, nf), :]

                each_run(v, pack)

            out_moves(v)[0]()

    advect_all(SWEEPS, True)
    forcing_start()
    for v in range(RETURNED):
        w_moves(1, v)[1]()
        march_moves(v)[1]()
        state_moves(v)[2]()

    @pl.loop(0, SWEEPS * RETURNED)
    def _(turn):
        e, v = SWEEPS + turn // RETURNED, turn % RETURNED
        sweep_plane(e, v, 1, e == 2 * SWEEPS - 1)

    out_state = pltpu.make_async_copy(
        x_one.at[0, :, pl.ds(0, RETURNED), pl.ds(8, span), :],
        g_state.at[:, pl.ds(0, RETURNED), :, :],
        load_sem.at[0],
    )
    out_state.start()

    @pl.loop(RETURNED, variables)
    def _(v):
        out_moves(v)[1]()

    out_state.wait()
    forcing_wait()
    for n in range(2):
        base_moves(n)[2]()
    for v in range(RETURNED):
        w_moves(1, v)[2]()
        march_moves(v)[2]()

    @pl.loop(0, variables)
    def _(v):
        w_moves(0, v)[2]()

    @pl.loop(RETURNED, variables)
    def _(v):
        state_moves(v)[2]()
        out_moves(v)[2]()

    forcing_drain()


LAG = 2
FIRST = 1
RETURNED = 1


def per_device_tiled(state_in, forcing_in, base_flow, station_index, lobe_count):
    _, per_dev, variables, span_az, radii = state_in.shape
    nf = lax.axis_size("freq")
    planes = lax.axis_size("plane")
    freqs = per_dev * nf
    ntime = 3 * freqs // 2
    own_az = span_az // nf
    stored = base_flow.shape[0]
    slopes, inverse_p = radial_tables(radii)
    mode_ids = (np.arange(nf)[None, :] * per_dev + np.arange(per_dev)[:, None]).reshape(-1)
    inverse, forward = transform_tables(mode_ids, freqs, ntime)
    dims = (nf, planes, own_az, variables, per_dev, radii, stored)
    parts = 2 * per_dev
    edge_rows = -(-2 * parts // 8) * 8
    anywhere = pl.BlockSpec(memory_space=pl.ANY)
    far = pl.BlockSpec(memory_space=pltpu.HBM)
    f32 = jnp.float32
    whole = (parts, variables, span_az, radii)
    slab = variables * 2 * freqs
    share = span_az // (nf // 2)
    moves = 3 + 4 * variables + RETURNED
    outs = pl.pallas_call(
        functools.partial(relay, dims),
        out_shape=jax.ShapeDtypeStruct((2, *whole), f32),
        in_specs=[pl.BlockSpec(memory_space=pltpu.SMEM)] + [far] * 8,
        out_specs=anywhere,
        scratch_shapes=[
            pltpu.VMEM((nf, variables, parts, own_az, radii), f32),
            pltpu.VMEM((nf // 2, stored, FIRST, share, radii), f32),
            pltpu.VMEM((nf // 2, stored, variables - FIRST, share, radii), f32),
            pltpu.VMEM((STEPS, variables, share, radii), f32),
            pltpu.VMEM((STEPS, variables, share, radii), f32),
            pltpu.VMEM((STEPS, variables, share, radii), f32),
            pltpu.VMEM((STEPS, variables, span_az, radii), f32),
            pltpu.VMEM((2, parts, variables, span_az + 16, radii), f32),
            pltpu.VMEM(whole, f32),
            pltpu.VMEM((2, variables, edge_rows, radii), f32),
            pltpu.VMEM((2, variables, edge_rows, radii), f32),
            pltpu.VMEM((2, own_az + 2, slab, radii), f32),
            pltpu.VMEM((own_az, slab, radii), f32),
            pltpu.VMEM((variables, own_az, radii), f32),
            pltpu.VMEM((nf, variables, parts, own_az, radii), f32),
            pltpu.VMEM((nf, RETURNED, parts, own_az, radii), f32),
            pltpu.VMEM((nf, parts, variables, own_az, radii), f32),
            pltpu.SemaphoreType.DMA((moves,)),
            pltpu.SemaphoreType.DMA((moves,)),
            pltpu.SemaphoreType.DMA((STEPS, variables)),
            pltpu.SemaphoreType.DMA((STEPS, variables)),
            pltpu.SemaphoreType.DMA((share // own_az,)),
            pltpu.SemaphoreType.DMA((2,)),
            pltpu.SemaphoreType.DMA((2, 2, variables)),
            pltpu.SemaphoreType.DMA((2, 2, variables)),
            pltpu.SemaphoreType.DMA((2, variables)),
            pltpu.SemaphoreType.DMA((2, variables)),
            pltpu.SemaphoreType.DMA((2,)),
            pltpu.VMEM((freqs, radii), f32),
            pltpu.VMEM((2 * radii, 2 * radii), jnp.bfloat16),
            pltpu.VMEM((2 * radii, 2 * radii), jnp.bfloat16),
            pltpu.VMEM((2 * ntime, 4 * freqs), jnp.bfloat16),
            pltpu.VMEM((4 * freqs, 2 * ntime), jnp.bfloat16),
            pltpu.SemaphoreType.DMA((5,)),
            pltpu.SMEM(station_index.shape, jnp.int32),
        ],
        compiler_params=pltpu.CompilerParams(
            collective_id=0, has_side_effects=True, vmem_limit_bytes=32 * 1024 * 1024
        ),
    )(
        lobe_count,
        *[
            pltpu.with_memory_space_constraint(x, pltpu.HBM)
            for x in (
                station_index,
                state_in.reshape(whole),
                base_flow,
                forcing_in.reshape(whole),
                right_table(inverse_p.T),
                right_table(slopes.T),
                stacked_table(inverse.transpose(2, 0, 1).reshape(ntime, 2 * freqs)),
                stacked_table(forward.reshape(2 * freqs, ntime)),
            )
        ],
    )
    return tuple(outs[n].reshape(state_in.shape) for n in range(2))


def per_device_any(*args):
    nf = lax.axis_size("freq")
    tiles = args[0].shape[3] % (8 * nf) == 0 and nf % 2 == 0 and lax.axis_size("plane") == 2
    return (per_device_tiled if tiles else per_device)(*args)


MESH = pl.DeviceIdType.MESH


def solution(mesh):
    return jax.shard_map(
        per_device_any,
        mesh=mesh,
        in_specs=(
            P(None, "freq", None, "plane", None),
            P(None, "freq", None, "plane", None),
            P("freq", None, "plane", None),
            P(),
            P(),
        ),
        out_specs=(P(None, "freq", None, "plane", None), P(None, "freq", None, "plane", None)),
        check_vma=False,
    )
```
